128 devices in a mesh: lat: 16 (over x, y), lon: 4 (over z_lo, core), mem: 2 (over z_hi).
Axes of the slice: x: 4, y: 4, z: 4 (z_hi: 2, z_lo: 2; z = z_hi * 2 + z_lo), core: 2. Of those that a mesh axis runs over, the one named last changes fastest.
Arguments:
- velo: float32 [2, 4, 512, 2048], P(None, None, 'lat', 'lon'), may hold values from -6 to 6
- temp: float32 [4, 512, 2048], P(None, 'lat', 'lon'), may hold values from -6 to 6
- land: int32 [512, 2048], P('lat', 'lon'), may hold values 0 or 1
- target: bfloat16 [2, 4, 128, 512], P(None, None, 'lat', 'lon'), may hold values from -3 to 3
- w_first: bfloat16 [4, 9, 64, 3], P('mem'), may hold values from -1.25 to 1.25
- w_middle: bfloat16 [4, 9, 64, 64], P('mem'), may hold values from -0.25 to 0.25
- w_last: bfloat16 [4, 9, 2, 64], P('mem'), may hold values from -0.25 to 0.25
Outputs:
- velo_next: float32 [2, 4, 512, 2048], P(None, None, 'lat', 'lon')
- temp_next: float32 [4, 512, 2048], P(None, 'lat', 'lon')
- grad_first: float32 [4, 9, 64, 3], P('mem')
- grad_middle: float32 [4, 9, 64, 64], P('mem')
- grad_last: float32 [4, 9, 2, 64], P('mem')
The draws below stay inside these ranges and needn't reach their ends.
All inputs are finite; a program needn't handle non-finite values. No bound on the sum of `land` on one device may be relied on, other than what follows from the above.
Results may differ from the reference program's by a relative error of at most 0.0003.
Values may be sent and summed in bfloat16 or wider, within the bound.
A program may use at most 128 MiB of HBM per device.

```python
import math
import jax
import jax.numpy as jnp
from jax import lax

LEV = 4
COARSE = 4
HID = 64
MEMBERS = 4
NY = 512
NX = 2048
NYC = 128
NXC = 512


def touch_ends(drawn, stream_key, least, largest):
    index_at = [jax.random.randint(jax.random.fold_in(stream_key, axis), (), 0, length) for axis, length in enumerate(drawn.shape)]
    longest = drawn.shape.index(max(drawn.shape))
    beside = index_at[:longest] + [(index_at[longest] + 1) % drawn.shape[longest]] + index_at[longest + 1:]
    return drawn.at[tuple(index_at)].set(least).at[tuple(beside)].set(largest)


def block_levels(own_key, extent, split, low, largest):
    level, own = 1.0, jax.random.fold_in(own_key, 6)
    for dim, shards_of in split:
        heights = jnp.exp(jax.random.uniform(jax.random.fold_in(own, dim), (shards_of,), jnp.float32, low / len(split), largest / len(split)))
        level = level * jnp.repeat(heights, extent[dim] // shards_of).reshape([-1 if axis == dim else 1 for axis in range(len(extent))])
    return level


def gaussian(stream_key, dims, scale, reach, split=(), held_as=jnp.bfloat16):
    drawn = jax.random.normal(stream_key, dims, jnp.float32) * scale
    if len(split) > 0:
        drawn = block_levels(stream_key, dims, split, -0.22, 0.18) * drawn
    return jnp.clip(drawn, min=-reach, max=reach).astype(held_as)


def setup_inputs(seed: int = 0) -> dict:
    seeds = jax.random.split(jax.random.key(seed), 8)
    return {
        "velo": gaussian(seeds[0], (2, LEV, NY, NX), 1.0, 6.0, ((2, 16), (3, 4)), jnp.float32),
        "temp": gaussian(seeds[1], (LEV, NY, NX), 1.0, 6.0, ((1, 16), (2, 4)), jnp.float32),
        "land": touch_ends((jax.random.randint(seeds[2], (NY, NX), 0, 5) < 4).astype(jnp.int32), jax.random.fold_in(seeds[2], 1), 0, 1),
        "target": gaussian(seeds[3], (2, LEV, NYC, NXC), 0.5, 3.0, ((2, 16), (3, 4))),
        "w_first": gaussian(seeds[4], (MEMBERS, 9, HID, 3), 27 ** -0.5, 1.25, ((0, 2),)),
        "w_middle": gaussian(seeds[5], (MEMBERS, 9, HID, HID), (9 * HID) ** -0.5, 0.25, ((0, 2),)),
        "w_last": gaussian(seeds[6], (MEMBERS, 9, 2, HID), (9 * HID) ** -0.5, 0.25, ((0, 2),)),
    }


def pad_coarse(x):
    x = jnp.pad(x, ((0, 0), (1, 1), (0, 0)))
    return jnp.concatenate([x[..., -1:], x, x[..., :1]], axis=-1)

def conv_sum(padded, weights, sign):
    height = padded.shape[-2] - 2
    width = padded.shape[-1] - 2
    total = None
    for a in (-1, 0, 1):
        for b in (-1, 0, 1):
            k = (a + 1) * 3 + (b + 1)
            piece = padded[:, 1 + sign * a:1 + sign * a + height, 1 + sign * b:1 + sign * b + width]
            if sign > 0:
                term = jnp.einsum('oc,cyx->oyx', weights[k].astype(jnp.float32), piece.astype(jnp.float32))
            else:
                term = jnp.einsum('oc,oyx->cyx', weights[k].astype(jnp.float32), piece.astype(jnp.float32))
            total = term if total is None else total + term
    return total

def weight_grad(cotangent, padded):
    height = cotangent.shape[-2]
    width = cotangent.shape[-1]
    result = []
    for a in (-1, 0, 1):
        for b in (-1, 0, 1):
            piece = padded[:, 1 + a:1 + a + height, 1 + b:1 + b + width]
            result.append(jnp.einsum('oyx,cyx->oc', cotangent.astype(jnp.float32), piece.astype(jnp.float32)))
    return jnp.stack(result, 0)

def reference(velo, temp, land, target, w_first, w_middle, w_last):
    fields = jnp.concatenate([velo, temp[None]], 0)
    rows = fields.shape[2]
    cols = fields.shape[3]
    coarse = fields.reshape(3, LEV, rows // COARSE, COARSE, cols // COARSE, COARSE).mean(axis=(3, 5)).astype(jnp.bfloat16)
    count = 2.0 * LEV * (rows // COARSE) * (cols // COARSE)
    coarse_levels = jnp.transpose(coarse, (1, 0, 2, 3))
    target_levels = jnp.transpose(target, (1, 0, 2, 3))

    def member_pass(weights):
        wf, wm, wl = weights

        def level_pass(inputs):
            x_level, goal = inputs
            xpad = pad_coarse(x_level)
            hidden_one = jnp.tanh(conv_sum(xpad, wf, 1)).astype(jnp.bfloat16)
            hpad_one = pad_coarse(hidden_one)
            hidden_two = jnp.tanh(conv_sum(hpad_one, wm, 1)).astype(jnp.bfloat16)
            hpad_two = pad_coarse(hidden_two)
            predict = conv_sum(hpad_two, wl, 1)
            cot_three = ((predict - goal.astype(jnp.float32)) * (2.0 / count)).astype(jnp.bfloat16)
            grad_three = weight_grad(cot_three, hpad_two)
            two_f = hidden_two.astype(jnp.float32)
            cot_two = (conv_sum(pad_coarse(cot_three), wl, -1) * (1.0 - two_f * two_f)).astype(jnp.bfloat16)
            grad_two = weight_grad(cot_two, hpad_one)
            one_f = hidden_one.astype(jnp.float32)
            cot_one = (conv_sum(pad_coarse(cot_two), wm, -1) * (1.0 - one_f * one_f)).astype(jnp.bfloat16)
            grad_one = weight_grad(cot_one, xpad)
            return (predict, grad_one, grad_two, grad_three)
        preds, g_one, g_two, g_three = lax.map(level_pass, (coarse_levels, target_levels))
        return (preds, lax.optimization_barrier(jnp.sum(g_one, 0)), lax.optimization_barrier(jnp.sum(g_two, 0)), lax.optimization_barrier(jnp.sum(g_three, 0)))
    preds, grad_first, grad_middle, grad_last = lax.map(member_pass, (w_first, w_middle, w_last))
    members = w_first.shape[0]
    mean_force = jnp.transpose(lax.optimization_barrier(jnp.sum(preds, 0)), (1, 0, 2, 3)) / members
    force = jnp.repeat(jnp.repeat(mean_force, COARSE, axis=2), COARSE, axis=3)
    padded = jnp.pad(fields, ((0, 0), (0, 0), (1, 1), (0, 0)))
    padded = jnp.concatenate([padded[..., -1:], padded, padded[..., :1]], axis=-1)
    centre = padded[:, :, 1:-1, 1:-1]
    east = padded[:, :, 1:-1, 2:]
    west = padded[:, :, 1:-1, :-2]
    north = padded[:, :, 2:, 1:-1]
    south = padded[:, :, :-2, 1:-1]
    laplace = east + west + north + south - 4.0 * centre
    press = -jnp.cumsum(0.5 * padded[2], axis=0)
    grad_x = (press[:, 1:-1, 2:] - press[:, 1:-1, :-2]) / 2.0
    grad_y = (press[:, 2:, 1:-1] - press[:, :-2, 1:-1]) / 2.0
    row_ids = jnp.arange(rows).astype(jnp.float32)
    coriolis = jnp.sin(-math.pi / 2 + math.pi * (row_ids + 0.5) / rows)[:, None]
    wet = land.astype(jnp.float32)
    u_now = centre[0]
    v_now = centre[1]
    t_now = centre[2]
    u_next = u_now + 0.1 * wet * (coriolis * v_now - grad_x + 0.5 * laplace[0] + force[0])
    v_next = v_now + 0.1 * wet * (-coriolis * u_now - grad_y + 0.5 * laplace[1] + force[1])
    advect = u_now * (east[2] - west[2]) / 2.0 + v_now * (north[2] - south[2]) / 2.0
    t_next = t_now + 0.1 * wet * (-advect + 0.3 * laplace[2])
    return (jnp.stack([u_next, v_next], 0), t_next, grad_first, grad_middle, grad_last)
```

```python
import functools
import math

import jax
import jax.numpy as jnp
from jax import lax
from jax.experimental import pallas as pl
from jax.experimental.pallas import tpu as pltpu
from jax.sharding import PartitionSpec as P

LEV = 4
COARSE = 4
HID = 64
HALO = 5
MESH = pl.DeviceIdType.MESH
F32 = jnp.float32
BF16 = jnp.bfloat16
MID_ROWS = 9 * HID
SMALL_ROWS = 72
GRAD_ROWS = MID_ROWS + 2 * SMALL_ROWS
NT = (((1,), (1,)), ((), ()))


def chunking(group):
    tiles = GRAD_ROWS // 8
    per = -(-tiles // group)
    owners = -(-tiles // per)
    return per * 8, owners


def shift_cols(value, by):
    return pltpu.roll(value, by % value.shape[-1], axis=value.ndim - 1)


def kernel(
    n_lat, n_lon, n_mem,
    velo, temp, land, target, w1, w2, w2t, wl, w3t,
    velo_out, temp_out, grads,
    narrow, tall, staged, send_buf, rx, s0, s1, h2s, g3s, d2s, pred_buf, force_rx, force_up, pad,
    row_send, row_rx, col_send, col_rx, acc_mid, acc_first, acc_last, partial, scattered,
    cs_sem, cr_sem, os_sem, or_sem, fs_sem, fr_sem, fl_sem, rs_send, rs_recv, ag_send, ag_recv,
):
    lat = lax.axis_index("lat")
    lon = lax.axis_index("lon")
    mem = lax.axis_index("mem")
    rows = temp.shape[1]
    cols = temp.shape[2]
    rc = rows // COARSE
    cc = cols // COARSE
    width = cc * n_lon
    nyc = rc * n_lat
    group = n_lat * n_lon
    chunk, owners = chunking(group)
    me = lat * n_lon + lon

    def at(lat_to, lon_to, mem_to):
        return {"lat": lat_to, "lon": lon_to, "mem": mem_to}

    def of_group(index):
        return at(index // n_lon, lax.rem(index, n_lon), mem)

    barrier = pltpu.get_barrier_semaphore()

    def greet(i, carry):
        pl.semaphore_signal(
            barrier, inc=1, device_id=of_group(lax.rem(me + i, group)), device_id_type=MESH
        )
        return carry

    lax.fori_loop(1, group, greet, 0)
    for other in range(1, n_mem):
        for l in range(n_lon):
            pl.semaphore_signal(
                barrier, inc=1, device_id=at(lat, l, lax.rem(mem + other, n_mem)), device_id_type=MESH
            )

    q_ids = lax.broadcasted_iota(jnp.int32, (cc, cols), 0)
    i_ids = lax.broadcasted_iota(jnp.int32, (cc, cols), 1)
    expand = jnp.where(i_ids // COARSE == q_ids, 1.0, 0.0).astype(F32)

    def field(c, l, where):
        return velo[c, l, where, :] if c < 2 else temp[l, where, :]

    staged[...] = jnp.zeros_like(staged)
    for c in range(3):
        fine = (velo[c] if c < 2 else temp[...]).reshape(LEV * rows, cols)
        narrow[...] = lax.dot_general(
            fine * (1.0 / COARSE**2), expand, NT,
            precision=lax.Precision.HIGHEST, preferred_element_type=F32,
        )
        pooled = narrow[pl.ds(0, LEV * rc, stride=COARSE), :]
        for r in range(1, COARSE):
            pooled = pooled + narrow[pl.ds(r, LEV * rc, stride=COARSE), :]
        staged[pl.ds(c, LEV * rc, stride=8), :] = pooled
    for c in range(2):
        goal = target[c].astype(F32).reshape(LEV * rc, cc)
        staged[pl.ds(4 + c, LEV * rc, stride=8), :] = goal
        staged[pl.ds(6 + c, LEV * rc, stride=8), :] = goal
    send_buf[...] = staged[...].astype(BF16).reshape(send_buf.shape)

    lane = lax.broadcasted_iota(jnp.int32, (rows, 128), 1)
    west_cols = jnp.zeros((rows, 128), F32)
    east_cols = jnp.zeros((rows, 128), F32)
    for c in range(3):
        for l in range(LEV):
            q = c * LEV + l
            first = velo[c, l, :, 0:128] if c < 2 else temp[l, :, 0:128]
            last = velo[c, l, :, cols - 128 : cols] if c < 2 else temp[l, :, cols - 128 : cols]
            west_cols = jnp.where(lane == q, jnp.broadcast_to(first[:, 0:1], (rows, 128)), west_cols)
            east_cols = jnp.where(lane == q, jnp.broadcast_to(last[:, 127:128], (rows, 128)), east_cols)
            row_send[0, q : q + 1, :] = field(c, l, pl.ds(0, 1))
            row_send[1, q : q + 1, :] = field(c, l, pl.ds(rows - 1, 1))
            pad[q, 8 : 8 + rows, :] = field(c, l, pl.ds(0, rows))
    col_send[0] = west_cols
    col_send[1] = east_cols

    @pl.when(lat == 0)
    def _():
        rx[:, 0:HALO] = jnp.zeros((n_lon, HALO, 8, cc), BF16)
        row_rx[0] = jnp.zeros_like(row_rx[0])

    @pl.when(lat == n_lat - 1)
    def _():
        rx[:, HALO + rc : 2 * HALO + rc] = jnp.zeros((n_lon, HALO, 8, cc), BF16)
        row_rx[1] = jnp.zeros_like(row_rx[1])

    pl.semaphore_wait(barrier, group - 1 + (n_mem - 1) * n_lon)

    def own_copy(l):
        return pltpu.make_async_remote_copy(
            src_ref=send_buf.at[l], dst_ref=rx.at[lon, pl.ds(HALO, rc)],
            send_sem=cs_sem.at[0, l], recv_sem=cr_sem.at[0, lon],
            device_id=at(lat, l, mem), device_id_type=MESH,
        )

    def up_copy(l):
        return pltpu.make_async_remote_copy(
            src_ref=send_buf.at[l, pl.ds(rc - HALO, HALO)], dst_ref=rx.at[lon, pl.ds(0, HALO)],
            send_sem=cs_sem.at[1, l], recv_sem=cr_sem.at[1, lon],
            device_id=at(lat + 1, l, mem), device_id_type=MESH,
        )

    def down_copy(l):
        return pltpu.make_async_remote_copy(
            src_ref=send_buf.at[l, pl.ds(0, HALO)], dst_ref=rx.at[lon, pl.ds(HALO + rc, HALO)],
            send_sem=cs_sem.at[2, l], recv_sem=cr_sem.at[2, lon],
            device_id=at(lat - 1, l, mem), device_id_type=MESH,
        )

    def row_up():
        return pltpu.make_async_remote_copy(
            src_ref=row_send.at[1], dst_ref=row_rx.at[0], send_sem=os_sem.at[0], recv_sem=or_sem.at[0],
            device_id=at(lat + 1, lon, mem), device_id_type=MESH,
        )

    def row_down():
        return pltpu.make_async_remote_copy(
            src_ref=row_send.at[0], dst_ref=row_rx.at[1], send_sem=os_sem.at[1], recv_sem=or_sem.at[1],
            device_id=at(lat - 1, lon, mem), device_id_type=MESH,
        )

    def col_east():
        return pltpu.make_async_remote_copy(
            src_ref=col_send.at[1], dst_ref=col_rx.at[0], send_sem=os_sem.at[2], recv_sem=or_sem.at[2],
            device_id=at(lat, lax.rem(lon + 1, n_lon), mem), device_id_type=MESH,
        )

    def col_west():
        return pltpu.make_async_remote_copy(
            src_ref=col_send.at[0], dst_ref=col_rx.at[1], send_sem=os_sem.at[3], recv_sem=or_sem.at[3],
            device_id=at(lat, lax.rem(lon + n_lon - 1, n_lon), mem), device_id_type=MESH,
        )

    for l in range(n_lon):
        @pl.when(lat < n_lat - 1)
        def _(l=l):
            up_copy(l).start()

        @pl.when(lat > 0)
        def _(l=l):
            down_copy(l).start()

        @pl.when(lon != l)
        def _(l=l):
            own_copy(l).start()

    @pl.when(lat < n_lat - 1)
    def _():
        row_up().start()

    @pl.when(lat > 0)
    def _():
        row_down().start()

    col_east().start()
    col_west().start()

    rx[lon, HALO : HALO + rc] = send_buf[lon]
    acc_mid[...] = jnp.zeros_like(acc_mid)
    acc_first[...] = jnp.zeros_like(acc_first)
    acc_last[...] = jnp.zeros_like(acc_last)

    def arrived(kind, l, src, dst):
        pltpu.make_async_copy(src, dst, cr_sem.at[kind, l]).wait()

    for l in range(n_lon):
        @pl.when(lon != l)
        def _(l=l):
            arrived(0, l, send_buf.at[l], rx.at[l, pl.ds(HALO, rc)])

        @pl.when(lat > 0)
        def _(l=l):
            arrived(1, l, send_buf.at[l, pl.ds(0, HALO)], rx.at[l, pl.ds(0, HALO)])

        @pl.when(lat < n_lat - 1)
        def _(l=l):
            arrived(2, l, send_buf.at[l, pl.ds(0, HALO)], rx.at[l, pl.ds(HALO + rc, HALO)])

    def inside(g):
        return jnp.where(jnp.logical_and(g >= 0, g < nyc), 1.0, 0.0).astype(F32)

    def received(x):
        return jnp.concatenate([rx[l, x].astype(F32) for l in range(n_lon)], axis=-1)

    def fill_s0(x, carry):
        v = received(x)
        s0[x] = jnp.concatenate(
            [shift_cols(v, 1), v, shift_cols(v, -1), jnp.zeros_like(v)], axis=0
        ).astype(BF16)
        return carry

    lax.fori_loop(0, rc + 2 * HALO, fill_s0, 0)

    def first_layer(r, carry):
        block = s0[pl.ds(r, 3)].reshape(96, width)
        h = jnp.tanh(jnp.dot(w1[...], block, preferred_element_type=F32)) * inside(lat * rc - 4 + r)
        for m in range(2):
            hm = h[m * HID : (m + 1) * HID]
            s1[m, r, 0:HID] = shift_cols(hm, 1).astype(BF16)
            s1[m, r, HID : 2 * HID] = hm.astype(BF16)
            s1[m, r, 2 * HID : 3 * HID] = shift_cols(hm, -1).astype(BF16)
        return carry

    lax.fori_loop(0, rc + 8, first_layer, 0)

    def second_layer(r, carry):
        keep = inside(lat * rc - 3 + r)
        for m in range(2):
            block = s1[m, pl.ds(r, 3)].reshape(9 * HID, width)
            h = jnp.tanh(jnp.dot(w2[m], block, preferred_element_type=F32)) * keep
            h2s[r, m * HID : (m + 1) * HID] = h.astype(BF16)
        return carry

    lax.fori_loop(0, rc + 6, second_layer, 0)

    scale = 2.0 / (2.0 * LEV * nyc * width)
    sub = lax.broadcasted_iota(jnp.int32, (8, width), 0)

    def last_layer(r, carry):
        block = h2s[pl.ds(r, 3)].reshape(6 * HID, width)
        u = jnp.dot(wl[...], block, preferred_element_type=F32)
        pred = shift_cols(u[0:8], 1) + u[8:16] + shift_cols(u[16:24], -1)
        g3 = jnp.where(sub >= 4, (pred - received(r + 3)) * scale, 0.0) * inside(lat * rc - 2 + r)
        g3s[r] = jnp.concatenate(
            [shift_cols(g3, -1), g3, shift_cols(g3, 1), jnp.zeros_like(g3)], axis=0
        ).astype(BF16)
        both = pred[4:6] + pred[6:8]

        @pl.when(jnp.logical_and(r >= 2, r < 2 + rc))
        def _():
            for o in range(2):
                pred_buf[o, pl.ds(r - 2, 1), :] = both[o : o + 1]

        return carry

    lax.fori_loop(0, rc + 4, last_layer, 0)

    def force_copy(l, m):
        return pltpu.make_async_remote_copy(
            src_ref=pred_buf.at[:, :, pl.ds(l * cc, cc)], dst_ref=force_rx.at[mem, lon],
            send_sem=fs_sem.at[m, l], recv_sem=fr_sem.at[mem, lon],
            device_id=at(lat, l, m), device_id_type=MESH,
        )

    def force_own():
        return pltpu.make_async_copy(
            pred_buf.at[:, :, pl.ds(pl.multiple_of(lon * cc, cc), cc)], force_rx.at[mem, lon], fl_sem
        )

    def elsewhere(l, m):
        return jnp.logical_or(lon != l, mem != m)

    for m in range(n_mem):
        for l in range(n_lon):
            @pl.when(elsewhere(l, m))
            def _(l=l, m=m):
                force_copy(l, m).start()

    force_own().start()

    def back_second(r, carry):
        block = g3s[pl.ds(r, 3)].reshape(96, width)
        h = h2s[r + 2].astype(F32)
        d = jnp.dot(w3t[...], block, preferred_element_type=F32) * (1.0 - h * h)
        d = d * inside(lat * rc - 1 + r)
        for m in range(2):
            dm = d[m * HID : (m + 1) * HID]
            d2s[m, r, 0:HID] = shift_cols(dm, -1).astype(BF16)
            d2s[m, r, HID : 2 * HID] = dm.astype(BF16)
            d2s[m, r, 2 * HID : 3 * HID] = shift_cols(dm, 1).astype(BF16)
        return carry

    lax.fori_loop(0, rc + 2, back_second, 0)

    def own_row(r, carry):
        ups = g3s[pl.ds(r + 1, 3)].reshape(96, width)
        acc_last[...] += lax.dot_general(ups, h2s[r + 3], NT, preferred_element_type=F32)
        parts = []
        for m in range(2):
            hidden = s1[m, pl.ds(r + 3, 3), HID : 2 * HID]
            acc_mid[m] += lax.dot_general(
                d2s[m, r + 1], hidden.reshape(3 * HID, width), NT, preferred_element_type=F32
            )
            block = d2s[m, pl.ds(r, 3)].reshape(9 * HID, width)
            h = s1[m, r + 4, HID : 2 * HID].astype(F32)
            d = jnp.dot(w2t[m], block, preferred_element_type=F32) * (1.0 - h * h)
            parts.append(d.astype(BF16))
        d1 = jnp.concatenate(parts, axis=0)
        xs = s0[pl.ds(r + 4, 3)].reshape(96, width)
        acc_first[...] += lax.dot_general(xs, d1, NT, preferred_element_type=F32)
        return carry

    lax.fori_loop(0, rc, own_row, 0)

    for a in range(3):
        partial[a * 192 : (a + 1) * 192, :] = jnp.concatenate(
            [acc_mid[m, :, a * HID : (a + 1) * HID] for m in range(2)], axis=-1
        )
        partial[MID_ROWS + 24 * a : MID_ROWS + 24 * a + 24, :] = acc_first[32 * a : 32 * a + 24, :]
        at_row = MID_ROWS + SMALL_ROWS + 24 * a
        partial[at_row : at_row + 24, :] = acc_last[32 * a : 32 * a + 24, :]
    if owners * chunk > GRAD_ROWS:
        partial[GRAD_ROWS:, :] = jnp.zeros((owners * chunk - GRAD_ROWS, 128), F32)

    def piece(ref, index):
        return ref.at[pl.ds(pl.multiple_of(index * chunk, chunk), chunk)]

    def scatter(i, carry):
        to = lax.rem(me + i, group)

        @pl.when(to < owners)
        def _():
            pltpu.make_async_remote_copy(
                src_ref=piece(partial, to), dst_ref=scattered.at[i - 1],
                send_sem=rs_send, recv_sem=rs_recv, device_id=of_group(to), device_id_type=MESH,
            ).start()

        return carry

    lax.fori_loop(1, group, scatter, 0)

    for m in range(n_mem):
        for l in range(n_lon):
            @pl.when(elsewhere(l, m))
            def _(l=l, m=m):
                pltpu.make_async_copy(
                    pred_buf.at[:, :, pl.ds(0, cc)], force_rx.at[m, l], fr_sem.at[m, l]
                ).wait()

    force_own().wait()

    @pl.when(lat > 0)
    def _():
        pltpu.make_async_copy(row_send.at[0], row_rx.at[0], or_sem.at[0]).wait()

    @pl.when(lat < n_lat - 1)
    def _():
        pltpu.make_async_copy(row_send.at[0], row_rx.at[1], or_sem.at[1]).wait()

    pltpu.make_async_copy(col_send.at[0], col_rx.at[0], or_sem.at[2]).wait()
    pltpu.make_async_copy(col_send.at[0], col_rx.at[1], or_sem.at[3]).wait()

    summed = force_rx[0]
    for m in range(1, n_mem):
        summed = summed + force_rx[m]
    mean = (summed * (1.0 / (2 * n_mem))).reshape(LEV * 2 * rc, cc)
    for r in range(COARSE):
        tall[pl.ds(r, LEV * 2 * rc, stride=COARSE), :] = mean
    force_up[...] = jnp.dot(
        tall[...], expand, precision=lax.Precision.HIGHEST, preferred_element_type=F32
    ).reshape(force_up.shape)
    for q in range(3 * LEV):
        pad[q, 7:8, :] = row_rx[0, q : q + 1, :]
        pad[q, 8 + rows : 9 + rows, :] = row_rx[1, q : q + 1, :]

    lane_ids = lax.broadcasted_iota(jnp.int32, (8, cols), 1)
    for s in range(rows // 8):
        base = 8 + 8 * s
        ids = (lat * rows + 8 * s + lax.broadcasted_iota(jnp.int32, (8, cols), 0)).astype(F32)
        coriolis = jnp.sin(-math.pi / 2 + math.pi * (ids + 0.5) / (rows * n_lat))
        wet = 0.1 * land[8 * s : 8 * s + 8, :].astype(F32)
        sum_x = jnp.zeros((8, cols), F32)
        sum_y = jnp.zeros((8, cols), F32)
        for l in range(LEV):
            got = []
            for c in range(3):
                q = c * LEV + l
                centre = pad[q, base : base + 8, :]
                south = pad[q, base - 1 : base + 7, :]
                north = pad[q, base + 1 : base + 9, :]
                before = col_rx[0, 8 * s : 8 * s + 8, q : q + 1]
                after = col_rx[1, 8 * s : 8 * s + 8, q : q + 1]
                west = jnp.where(lane_ids == 0, before, shift_cols(centre, 1))
                east = jnp.where(lane_ids == cols - 1, after, shift_cols(centre, -1))
                got.append((centre, east, west, north, south))
            laps = [e + w + n + so - 4.0 * ce for ce, e, w, n, so in got]
            u, v, t = got[0][0], got[1][0], got[2][0]
            dx = got[2][1] - got[2][2]
            dy = got[2][3] - got[2][4]
            sum_x = sum_x + dx
            sum_y = sum_y + dy
            fu = force_up[l * 2, 8 * s : 8 * s + 8, :]
            fv = force_up[l * 2 + 1, 8 * s : 8 * s + 8, :]
            velo_out[0, l, 8 * s : 8 * s + 8, :] = u + wet * (
                coriolis * v + 0.25 * sum_x + 0.5 * laps[0] + fu
            )
            velo_out[1, l, 8 * s : 8 * s + 8, :] = v + wet * (
                -coriolis * u + 0.25 * sum_y + 0.5 * laps[1] + fv
            )
            temp_out[l, 8 * s : 8 * s + 8, :] = t + wet * (
                -0.5 * (u * dx + v * dy) + 0.3 * laps[2]
            )

    def passed(ref, count, sem):
        pltpu.make_async_copy(ref.at[pl.ds(0, count)], ref.at[pl.ds(0, count)], sem).wait()

    @pl.when(me < owners)
    def _():
        passed(scattered, group - 1, rs_recv)

        def add(i, total):
            return total + scattered[i]

        start = pl.multiple_of(me * chunk, chunk)
        grads[pl.ds(start, chunk), :] = lax.fori_loop(
            0, group - 1, add, partial[pl.ds(start, chunk), :]
        )

        def gather(i, carry):
            pltpu.make_async_remote_copy(
                src_ref=piece(grads, me), dst_ref=piece(grads, me),
                send_sem=ag_send, recv_sem=ag_recv,
                device_id=of_group(lax.rem(me + i, group)), device_id_type=MESH,
            ).start()
            return carry

        lax.fori_loop(1, group, gather, 0)

    for l in range(n_lon):
        @pl.when(lat < n_lat - 1)
        def _(l=l):
            up_copy(l).wait_send()

        @pl.when(lat > 0)
        def _(l=l):
            down_copy(l).wait_send()

        @pl.when(lon != l)
        def _(l=l):
            own_copy(l).wait_send()

        for m in range(n_mem):
            @pl.when(elsewhere(l, m))
            def _(l=l, m=m):
                force_copy(l, m).wait_send()

    @pl.when(lat < n_lat - 1)
    def _():
        row_up().wait_send()

    @pl.when(lat > 0)
    def _():
        row_down().wait_send()

    col_east().wait_send()
    col_west().wait_send()

    @pl.when(me < owners)
    def _():
        passed(partial, (owners - 1) * chunk, rs_send)
        passed(grads, (owners - 1) * chunk, ag_recv)
        passed(scattered, group - 1, ag_send)

    @pl.when(me >= owners)
    def _():
        passed(partial, owners * chunk, rs_send)
        passed(grads, owners * chunk, ag_recv)


def per_device(n_lat, n_lon, n_mem, velo, temp, land, target, w_first, w_middle, w_last):
    rows, cols = temp.shape[1], temp.shape[2]
    rc, cc = rows // COARSE, cols // COARSE
    width = cc * n_lon
    group = n_lat * n_lon
    chunk, owners = chunking(group)
    mine = w_first.shape[0]

    wf = w_first.reshape(mine, 3, 3, HID, 3)
    wm = w_middle.reshape(mine, 3, 3, HID, HID)
    wo = w_last.reshape(mine, 3, 3, 2, HID)
    w1 = jnp.pad(jnp.transpose(wf, (0, 3, 1, 2, 4)), ((0, 0), (0, 0), (0, 0), (0, 1), (0, 5)))
    w1 = w1.reshape(mine * HID, 96)
    w2 = jnp.transpose(wm, (0, 3, 1, 2, 4)).reshape(mine, HID, 9 * HID)
    w2t = jnp.transpose(wm[:, ::-1], (0, 4, 1, 2, 3)).reshape(mine, HID, 9 * HID)
    eye = jnp.eye(mine, dtype=BF16)
    wl = jnp.pad(
        jnp.einsum("mabox,mn->bnoamx", wo, eye).reshape(3, 4, 6 * HID), ((0, 0), (4, 0), (0, 0))
    ).reshape(24, 6 * HID)
    w3t = jnp.pad(
        jnp.einsum("mabox,mn->mxabno", wo[:, ::-1], eye).reshape(mine * HID, 3, 3, 4),
        ((0, 0), (0, 0), (0, 1), (4, 0)),
    ).reshape(mine * HID, 96)

    vmem = pl.BlockSpec(memory_space=pltpu.VMEM)
    dma = pltpu.SemaphoreType.DMA
    velo_next, temp_next, grads = pl.pallas_call(
        functools.partial(kernel, n_lat, n_lon, n_mem),
        out_shape=(
            jax.ShapeDtypeStruct(velo.shape, F32),
            jax.ShapeDtypeStruct(temp.shape, F32),
            jax.ShapeDtypeStruct((owners * chunk, 128), F32),
        ),
        in_specs=[vmem] * 9,
        out_specs=(vmem, vmem, vmem),
        scratch_shapes=[
            pltpu.VMEM((LEV * rows, cc), F32),
            pltpu.VMEM((LEV * 2 * rows, cc), F32),
            pltpu.VMEM((LEV * rc * 8, cc), F32),
            pltpu.VMEM((LEV, rc, 8, cc), BF16),
            pltpu.VMEM((n_lon, rc + 2 * HALO, 8, cc), BF16),
            pltpu.VMEM((rc + 2 * HALO, 32, width), BF16),
            pltpu.VMEM((2, rc + 8, 3 * HID, width), BF16),
            pltpu.VMEM((rc + 6, 2 * HID, width), BF16),
            pltpu.VMEM((rc + 4, 32, width), BF16),
            pltpu.VMEM((2, rc + 2, 3 * HID, width), BF16),
            pltpu.VMEM((2, rc, width), F32),
            pltpu.VMEM((n_mem, n_lon, 2, rc, cc), F32),
            pltpu.VMEM((LEV * 2, rows, cols), F32),
            pltpu.VMEM((3 * LEV, rows + 16, cols), F32),
            pltpu.VMEM((2, 16, cols), F32),
            pltpu.VMEM((2, 16, cols), F32),
            pltpu.VMEM((2, rows, 128), F32),
            pltpu.VMEM((2, rows, 128), F32),
            pltpu.VMEM((2, 3 * HID, 3 * HID), F32),
            pltpu.VMEM((96, 128), F32),
            pltpu.VMEM((96, 128), F32),
            pltpu.VMEM((owners * chunk, 128), F32),
            pltpu.VMEM((group - 1, chunk, 128), F32),
            dma((3, n_lon)),
            dma((3, n_lon)),
            dma((4,)),
            dma((4,)),
            dma((n_mem, n_lon)),
            dma((n_mem, n_lon)),
            dma,
            dma,
            dma,
            dma,
            dma,
        ],
        compiler_params=pltpu.CompilerParams(
            collective_id=0, has_side_effects=True, vmem_limit_bytes=56 * 1024 * 1024
        ),
        name="ocean_step",
    )(velo, temp, land, target, w1, w2, w2t, wl, w3t)

    mid = grads[:MID_ROWS].reshape(3, 3, HID, mine, HID)
    grad_middle = jnp.transpose(mid, (3, 0, 1, 2, 4)).reshape(mine, 9, HID, HID)
    first = grads[MID_ROWS : MID_ROWS + SMALL_ROWS].reshape(9, 8, mine, HID)[:, :3]
    grad_first = jnp.transpose(first, (2, 0, 3, 1))
    last = grads[MID_ROWS + SMALL_ROWS : GRAD_ROWS].reshape(3, 3, 8, mine, HID)[::-1, :, 4:]
    last = last.reshape(9, mine, 2, mine, HID)
    grad_last = jnp.stack([last[:, m, :, m] for m in range(mine)], 0)
    return (velo_next, temp_next, grad_first, grad_middle, grad_last)


def solution(mesh):
    return jax.shard_map(
        functools.partial(per_device, mesh.shape["lat"], mesh.shape["lon"], mesh.shape["mem"]),
        mesh=mesh,
        in_specs=(
            P(None, None, "lat", "lon"),
            P(None, "lat", "lon"),
            P("lat", "lon"),
            P(None, None, "lat", "lon"),
            P("mem", None, None, None),
            P("mem", None, None, None),
            P("mem", None, None, None),
        ),
        out_specs=(
            P(None, None, "lat", "lon"),
            P(None, "lat", "lon"),
            P("mem", None, None, None),
            P("mem", None, None, None),
            P("mem", None, None, None),
        ),
        check_vma=False,
    )
```

```python
import functools
import math

import jax
import jax.numpy as jnp
from jax import lax
from jax.experimental import pallas as pl
from jax.experimental.pallas import tpu as pltpu
from jax.sharding import PartitionSpec as P

LEV = 4
COARSE = 4
HID = 64
HALO = 5
MESH = pl.DeviceIdType.MESH
F32 = jnp.float32
BF16 = jnp.bfloat16
MID_ROWS = 9 * HID
SMALL_ROWS = 72
GRAD_ROWS = MID_ROWS + 2 * SMALL_ROWS
NT = (((1,), (1,)), ((), ()))


def chunking(group):
    tiles = GRAD_ROWS // 8
    per = -(-tiles // group)
    owners = -(-tiles // per)
    return per * 8, owners


def shift_cols(value, by):
    return pltpu.roll(value, by % value.shape[-1], axis=value.ndim - 1)


def kernel(
    n_lat, n_lon, n_mem,
    velo_in, temp_in, land_in, target_in, w_first, w_middle, w_last,
    velo_out, temp_out, grads,
    velo_new, temp_new, land, target,
    narrow, tall, staged, send_buf, rx, s0, s1, h2s, g3s, d2s, pred_buf, force_rx, force_up, pad,
    row_send, row_rx, col_send, col_rx, w1_rows, wl_rows, partial, scattered,
    in_sem, out_sem,
    cs_sem, cr_sem, os_sem, or_sem, fs_sem, fr_sem, fl_sem, rs_send, rs_recv, ag_send, ag_recv,
):
    lat = lax.axis_index("lat")
    lon = lax.axis_index("lon")
    mem = lax.axis_index("mem")
    rows = temp_in.shape[1]
    cols = temp_in.shape[2]
    rc = rows // COARSE
    cc = cols // COARSE
    width = cc * n_lon
    nyc = rc * n_lat
    group = n_lat * n_lon
    chunk, owners = chunking(group)
    me = lat * n_lon + lon

    def at(lat_to, lon_to, mem_to):
        return {"lat": lat_to, "lon": lon_to, "mem": mem_to}

    def of_group(index):
        return at(index // n_lon, lax.rem(index, n_lon), mem)

    inner = pl.ds(8, rows)
    loads = [
        pltpu.make_async_copy(velo_in.at[c], pad.at[pl.ds(c * LEV, LEV), inner], in_sem.at[c])
        for c in range(2)
    ]
    loads.append(
        pltpu.make_async_copy(temp_in, pad.at[pl.ds(2 * LEV, LEV), inner], in_sem.at[2])
    )
    loads.append(pltpu.make_async_copy(target_in, target, in_sem.at[3]))
    loads.append(pltpu.make_async_copy(land_in, land, in_sem.at[4]))
    for load in loads:
        load.start()

    barrier = pltpu.get_barrier_semaphore()

    def greet(i, carry):
        pl.semaphore_signal(
            barrier, inc=1, device_id=of_group(lax.rem(me + i, group)), device_id_type=MESH
        )
        return carry

    lax.fori_loop(1, group, greet, 0)
    for other in range(1, n_mem):
        for l in range(n_lon):
            pl.semaphore_signal(
                barrier, inc=1, device_id=at(lat, l, lax.rem(mem + other, n_mem)), device_id_type=MESH
            )

    q_ids = lax.broadcasted_iota(jnp.int32, (cc, cols), 0)
    i_ids = lax.broadcasted_iota(jnp.int32, (cc, cols), 1)
    expand = jnp.where(i_ids // COARSE == q_ids, 1.0, 0.0).astype(F32)

    for load in loads[:4]:
        load.wait()
    staged[...] = jnp.zeros_like(staged)
    for c in range(3):
        fine = pad[c * LEV : (c + 1) * LEV, 8 : 8 + rows, :].reshape(LEV * rows, cols)
        narrow[...] = lax.dot_general(
            fine * (1.0 / COARSE**2), expand, NT,
            precision=lax.Precision.HIGHEST, preferred_element_type=F32,
        )
        pooled = narrow[pl.ds(0, LEV * rc, stride=COARSE), :]
        for r in range(1, COARSE):
            pooled = pooled + narrow[pl.ds(r, LEV * rc, stride=COARSE), :]
        staged[pl.ds(c, LEV * rc, stride=8), :] = pooled
    for c in range(2):
        goal = target[c].astype(F32).reshape(LEV * rc, cc)
        staged[pl.ds(4 + c, LEV * rc, stride=8), :] = goal
        staged[pl.ds(6 + c, LEV * rc, stride=8), :] = goal
    send_buf[...] = staged[...].astype(BF16).reshape(send_buf.shape)

    lane = lax.broadcasted_iota(jnp.int32, (rows, 128), 1)
    west_cols = jnp.zeros((rows, 128), F32)
    east_cols = jnp.zeros((rows, 128), F32)
    for q in range(3 * LEV):
        first = pad[q, 8 : 8 + rows, 0:128]
        last = pad[q, 8 : 8 + rows, cols - 128 : cols]
        west_cols = jnp.where(lane == q, jnp.broadcast_to(first[:, 0:1], (rows, 128)), west_cols)
        east_cols = jnp.where(lane == q, jnp.broadcast_to(last[:, 127:128], (rows, 128)), east_cols)
        row_send[0, q : q + 1, :] = pad[q, 8:9, :]
        row_send[1, q : q + 1, :] = pad[q, 7 + rows : 8 + rows, :]
    col_send[0] = west_cols
    col_send[1] = east_cols

    @pl.when(lat == 0)
    def _():
        rx[:, 0:HALO] = jnp.zeros((n_lon, HALO, 8, cc), BF16)
        row_rx[0] = jnp.zeros_like(row_rx[0])

    @pl.when(lat == n_lat - 1)
    def _():
        rx[:, HALO + rc : 2 * HALO + rc] = jnp.zeros((n_lon, HALO, 8, cc), BF16)
        row_rx[1] = jnp.zeros_like(row_rx[1])

    pl.semaphore_wait(barrier, group - 1 + (n_mem - 1) * n_lon)

    def own_copy(l):
        return pltpu.make_async_remote_copy(
            src_ref=send_buf.at[l], dst_ref=rx.at[lon, pl.ds(HALO, rc)],
            send_sem=cs_sem.at[0, l], recv_sem=cr_sem.at[0, lon],
            device_id=at(lat, l, mem), device_id_type=MESH,
        )

    def up_copy(l):
        return pltpu.make_async_remote_copy(
            src_ref=send_buf.at[l, pl.ds(rc - HALO, HALO)], dst_ref=rx.at[lon, pl.ds(0, HALO)],
            send_sem=cs_sem.at[1, l], recv_sem=cr_sem.at[1, lon],
            device_id=at(lat + 1, l, mem), device_id_type=MESH,
        )

    def down_copy(l):
        return pltpu.make_async_remote_copy(
            src_ref=send_buf.at[l, pl.ds(0, HALO)], dst_ref=rx.at[lon, pl.ds(HALO + rc, HALO)],
            send_sem=cs_sem.at[2, l], recv_sem=cr_sem.at[2, lon],
            device_id=at(lat - 1, l, mem), device_id_type=MESH,
        )

    def row_up():
        return pltpu.make_async_remote_copy(
            src_ref=row_send.at[1], dst_ref=row_rx.at[0], send_sem=os_sem.at[0], recv_sem=or_sem.at[0],
            device_id=at(lat + 1, lon, mem), device_id_type=MESH,
        )

    def row_down():
        return pltpu.make_async_remote_copy(
            src_ref=row_send.at[0], dst_ref=row_rx.at[1], send_sem=os_sem.at[1], recv_sem=or_sem.at[1],
            device_id=at(lat - 1, lon, mem), device_id_type=MESH,
        )

    def col_east():
        return pltpu.make_async_remote_copy(
            src_ref=col_send.at[1], dst_ref=col_rx.at[0], send_sem=os_sem.at[2], recv_sem=or_sem.at[2],
            device_id=at(lat, lax.rem(lon + 1, n_lon), mem), device_id_type=MESH,
        )

    def col_west():
        return pltpu.make_async_remote_copy(
            src_ref=col_send.at[0], dst_ref=col_rx.at[1], send_sem=os_sem.at[3], recv_sem=or_sem.at[3],
            device_id=at(lat, lax.rem(lon + n_lon - 1, n_lon), mem), device_id_type=MESH,
        )

    for l in range(n_lon):
        @pl.when(lat < n_lat - 1)
        def _(l=l):
            up_copy(l).start()

        @pl.when(lat > 0)
        def _(l=l):
            down_copy(l).start()

        @pl.when(lon != l)
        def _(l=l):
            own_copy(l).start()

    @pl.when(lat < n_lat - 1)
    def _():
        row_up().start()

    @pl.when(lat > 0)
    def _():
        row_down().start()

    col_east().start()
    col_west().start()

    rx[lon, HALO : HALO + rc] = send_buf[lon]
    def flip(matrix):
        size = matrix.shape[1]
        eye = jnp.where(
            lax.broadcasted_iota(jnp.int32, (size, size), 0)
            == lax.broadcasted_iota(jnp.int32, (size, size), 1),
            1.0, 0.0,
        ).astype(BF16)
        return lax.dot_general(eye, matrix, NT, preferred_element_type=F32).astype(BF16)

    def beside(blocks):
        return jnp.concatenate(blocks, axis=1)

    w1_rows[...] = jnp.zeros_like(w1_rows)
    wl_rows[...] = jnp.zeros_like(wl_rows)
    for a in range(3):
        for b in range(3):
            k = 3 * a + b
            for c in range(3):
                pair = w_first[k, c].astype(F32)
                for m in range(2):
                    at_row = a * 32 + b * 8 + c
                    w1_rows[at_row : at_row + 1, m * HID : (m + 1) * HID] = pair[m : m + 1]
            for m in range(2):
                at_row = a * 24 + b * 8 + 4 + 2 * m
                wl_rows[at_row : at_row + 2, m * HID : (m + 1) * HID] = w_last[m, k].astype(F32)
    w1 = flip(w1_rows[...].astype(BF16))
    wl = wl_rows[...].astype(BF16)
    gap = jnp.zeros((8, 2 * HID), F32)
    w3 = jnp.concatenate([p for t in (2, 1, 0) for p in (wl_rows[24 * t : 24 * t + 24, :], gap)], axis=0)
    w3t = flip(w3.astype(BF16))
    w2 = [
        jnp.concatenate([beside([w_middle[m, 3 * a + b] for b in range(3)]) for a in range(3)], axis=0)
        for m in range(2)
    ]
    w2t = [
        flip(jnp.concatenate([beside([w_middle[m, 3 * a + b] for a in range(3)]) for b in range(3)], axis=0))
        for m in range(2)
    ]

    def arrived(kind, l, src, dst):
        pltpu.make_async_copy(src, dst, cr_sem.at[kind, l]).wait()

    for l in range(n_lon):
        @pl.when(lon != l)
        def _(l=l):
            arrived(0, l, send_buf.at[l], rx.at[l, pl.ds(HALO, rc)])

        @pl.when(lat > 0)
        def _(l=l):
            arrived(1, l, send_buf.at[l, pl.ds(0, HALO)], rx.at[l, pl.ds(0, HALO)])

        @pl.when(lat < n_lat - 1)
        def _(l=l):
            arrived(2, l, send_buf.at[l, pl.ds(0, HALO)], rx.at[l, pl.ds(HALO + rc, HALO)])

    def inside(g):
        return jnp.where(jnp.logical_and(g >= 0, g < nyc), 1.0, 0.0).astype(F32)

    def received(x):
        return jnp.concatenate([rx[l, x].astype(F32) for l in range(n_lon)], axis=-1)

    def three(v):
        return jnp.concatenate([shift_cols(v, 1), v, shift_cols(v, -1), jnp.zeros_like(v)], axis=0)

    for x in range(rc + 2 * HALO):
        s0[x] = three(received(x)).astype(BF16)

    for r in range(rc + 8):
        block = s0[r : r + 3].reshape(96, width)
        h = jnp.tanh(jnp.dot(w1, block, preferred_element_type=F32)) * inside(lat * rc - 4 + r)
        for m in range(2):
            hm = h[m * HID : (m + 1) * HID]
            s1[m, r, 0:HID] = shift_cols(hm, 1).astype(BF16)
            s1[m, r, HID : 2 * HID] = hm.astype(BF16)
            s1[m, r, 2 * HID : 3 * HID] = shift_cols(hm, -1).astype(BF16)

    def taps(products, r, order):
        return sum(
            products[r + i][j * HID : (j + 1) * HID] for i, j in enumerate(order)
        )

    for m in range(2):
        products = [
            jnp.dot(w2[m], s1[m, x], preferred_element_type=F32) for x in range(rc + 8)
        ]
        for r in range(rc + 6):
            h = jnp.tanh(taps(products, r, (0, 1, 2))) * inside(lat * rc - 3 + r)
            h2s[r, m * HID : (m + 1) * HID] = h.astype(BF16)

    scale = 2.0 / (2.0 * LEV * nyc * width)
    sub = lax.broadcasted_iota(jnp.int32, (8, width), 0)
    outs = [jnp.dot(wl, h2s[x], preferred_element_type=F32) for x in range(rc + 6)]
    for r in range(rc + 4):
        u = [sum(outs[r + a][24 * a + 8 * b : 24 * a + 8 * b + 8] for a in range(3)) for b in range(3)]
        pred = shift_cols(u[0], 1) + u[1] + shift_cols(u[2], -1)
        g3 = jnp.where(sub >= 4, (pred - received(r + 3)) * scale, 0.0) * inside(lat * rc - 2 + r)
        g3s[r] = jnp.concatenate(
            [shift_cols(g3, -1), g3, shift_cols(g3, 1), jnp.zeros_like(g3)], axis=0
        ).astype(BF16)
        if 2 <= r < 2 + rc:
            both = pred[4:6] + pred[6:8]
            for o in range(2):
                pred_buf[o, r - 2 : r - 1, :] = both[o : o + 1]

    def force_copy(l, m):
        return pltpu.make_async_remote_copy(
            src_ref=pred_buf.at[:, :, pl.ds(l * cc, cc)], dst_ref=force_rx.at[mem, lon],
            send_sem=fs_sem.at[m, l], recv_sem=fr_sem.at[mem, lon],
            device_id=at(lat, l, m), device_id_type=MESH,
        )

    def force_own():
        return pltpu.make_async_copy(
            pred_buf.at[:, :, pl.ds(pl.multiple_of(lon * cc, cc), cc)], force_rx.at[mem, lon], fl_sem
        )

    def elsewhere(l, m):
        return jnp.logical_or(lon != l, mem != m)

    for m in range(n_mem):
        for l in range(n_lon):
            @pl.when(elsewhere(l, m))
            def _(l=l, m=m):
                force_copy(l, m).start()

    force_own().start()

    for r in range(rc + 2):
        block = g3s[r : r + 3].reshape(96, width)
        h = h2s[r + 2].astype(F32)
        d = jnp.dot(w3t, block, preferred_element_type=F32) * (1.0 - h * h)
        d = d * inside(lat * rc - 1 + r)
        for m in range(2):
            dm = d[m * HID : (m + 1) * HID]
            d2s[m, r, 0:HID] = shift_cols(dm, -1).astype(BF16)
            d2s[m, r, HID : 2 * HID] = dm.astype(BF16)
            d2s[m, r, 2 * HID : 3 * HID] = shift_cols(dm, 1).astype(BF16)

    def over_rows(left, right):
        return lax.dot_general(
            beside([left(r) for r in range(rc)]), beside([right(r) for r in range(rc)]), NT,
            preferred_element_type=F32,
        )

    mids = [
        over_rows(
            lambda r: d2s[m, r + 1],
            lambda r: s1[m, r + 3 : r + 6, HID : 2 * HID].reshape(3 * HID, width),
        )
        for m in range(2)
    ]
    for a in range(3):
        partial[a * 192 : (a + 1) * 192, :] = beside(
            [mids[m][:, a * HID : (a + 1) * HID] for m in range(2)]
        )
    last = over_rows(lambda r: g3s[r + 1 : r + 4].reshape(96, width), lambda r: h2s[r + 3])
    for a in range(3):
        at_row = MID_ROWS + 24 * a
        partial[at_row : at_row + 24, :] = last[32 * a : 32 * a + 24, :]

    def piece(ref, index):
        return ref.at[pl.ds(pl.multiple_of(index * chunk, chunk), chunk)]

    def scatter(low, high):
        def send(i, carry):
            to = low + lax.rem(me + i, high - low)

            @pl.when(to != me)
            def _():
                pltpu.make_async_remote_copy(
                    src_ref=piece(partial, to), dst_ref=scattered.at[me],
                    send_sem=rs_send, recv_sem=rs_recv, device_id=of_group(to), device_id_type=MESH,
                ).start()

            return carry

        lax.fori_loop(0, high - low, send, 0)

    early = (MID_ROWS + SMALL_ROWS) // chunk
    scatter(0, early)

    d1s = []
    for m in range(2):
        products = [
            jnp.dot(w2t[m], d2s[m, x], preferred_element_type=F32) for x in range(rc + 2)
        ]
        own = []
        for r in range(rc):
            h = s1[m, r + 4, HID : 2 * HID].astype(F32)
            own.append((taps(products, r, (2, 1, 0)) * (1.0 - h * h)).astype(BF16))
        d1s.append(own)
    first = over_rows(
        lambda r: s0[r + 4 : r + 7].reshape(96, width),
        lambda r: jnp.concatenate([d1s[0][r], d1s[1][r]], axis=0),
    )
    for a in range(3):
        at_row = MID_ROWS + SMALL_ROWS + 24 * a
        partial[at_row : at_row + 24, :] = first[32 * a : 32 * a + 24, :]
    if owners * chunk > GRAD_ROWS:
        partial[GRAD_ROWS:, :] = jnp.zeros((owners * chunk - GRAD_ROWS, 128), F32)
    scatter(early, owners)

    for m in range(n_mem):
        for l in range(n_lon):
            @pl.when(elsewhere(l, m))
            def _(l=l, m=m):
                pltpu.make_async_copy(
                    pred_buf.at[:, :, pl.ds(0, cc)], force_rx.at[m, l], fr_sem.at[m, l]
                ).wait()

    force_own().wait()

    @pl.when(lat > 0)
    def _():
        pltpu.make_async_copy(row_send.at[0], row_rx.at[0], or_sem.at[0]).wait()

    @pl.when(lat < n_lat - 1)
    def _():
        pltpu.make_async_copy(row_send.at[0], row_rx.at[1], or_sem.at[1]).wait()

    pltpu.make_async_copy(col_send.at[0], col_rx.at[0], or_sem.at[2]).wait()
    pltpu.make_async_copy(col_send.at[0], col_rx.at[1], or_sem.at[3]).wait()

    summed = force_rx[0]
    for m in range(1, n_mem):
        summed = summed + force_rx[m]
    mean = (summed * (1.0 / (2 * n_mem))).reshape(LEV * 2 * rc, cc)
    for r in range(COARSE):
        tall[pl.ds(r, LEV * 2 * rc, stride=COARSE), :] = mean
    force_up[...] = jnp.dot(
        tall[...], expand, precision=lax.Precision.HIGHEST, preferred_element_type=F32
    ).reshape(force_up.shape)
    for q in range(3 * LEV):
        pad[q, 7:8, :] = row_rx[0, q : q + 1, :]
        pad[q, 8 + rows : 9 + rows, :] = row_rx[1, q : q + 1, :]

    loads[4].wait()
    lane_ids = lax.broadcasted_iota(jnp.int32, (8, cols), 1)
    for s in range(rows // 8):
        base = 8 + 8 * s
        ids = (lat * rows + 8 * s + lax.broadcasted_iota(jnp.int32, (8, cols), 0)).astype(F32)
        coriolis = jnp.sin(-math.pi / 2 + math.pi * (ids + 0.5) / (rows * n_lat))
        wet = 0.1 * land[8 * s : 8 * s + 8, :].astype(F32)
        sum_x = jnp.zeros((8, cols), F32)
        sum_y = jnp.zeros((8, cols), F32)
        for l in range(LEV):
            got = []
            for c in range(3):
                q = c * LEV + l
                centre = pad[q, base : base + 8, :]
                south = pad[q, base - 1 : base + 7, :]
                north = pad[q, base + 1 : base + 9, :]
                before = col_rx[0, 8 * s : 8 * s + 8, q : q + 1]
                after = col_rx[1, 8 * s : 8 * s + 8, q : q + 1]
                west = jnp.where(lane_ids == 0, before, shift_cols(centre, 1))
                east = jnp.where(lane_ids == cols - 1, after, shift_cols(centre, -1))
                got.append((centre, east, west, north, south))
            laps = [e + w + n + so - 4.0 * ce for ce, e, w, n, so in got]
            u, v, t = got[0][0], got[1][0], got[2][0]
            dx = got[2][1] - got[2][2]
            dy = got[2][3] - got[2][4]
            sum_x = sum_x + dx
            sum_y = sum_y + dy
            fu = force_up[l * 2, 8 * s : 8 * s + 8, :]
            fv = force_up[l * 2 + 1, 8 * s : 8 * s + 8, :]
            velo_new[0, l, 8 * s : 8 * s + 8, :] = u + wet * (
                coriolis * v + 0.25 * sum_x + 0.5 * laps[0] + fu
            )
            velo_new[1, l, 8 * s : 8 * s + 8, :] = v + wet * (
                -coriolis * u + 0.25 * sum_y + 0.5 * laps[1] + fv
            )
            temp_new[l, 8 * s : 8 * s + 8, :] = t + wet * (
                -0.5 * (u * dx + v * dy) + 0.3 * laps[2]
            )

    stores = [
        pltpu.make_async_copy(velo_new, velo_out, out_sem.at[0]),
        pltpu.make_async_copy(temp_new, temp_out, out_sem.at[1]),
    ]
    for store in stores:
        store.start()

    def passed(ref, count, sem):
        pltpu.make_async_copy(ref.at[pl.ds(0, count)], ref.at[pl.ds(0, count)], sem).wait()

    @pl.when(me < owners)
    def _():
        passed(scattered, group - 1, rs_recv)

        def add(i, total):
            return total + scattered[lax.rem(me + i, group)]

        start = pl.multiple_of(me * chunk, chunk)
        grads[pl.ds(start, chunk), :] = lax.fori_loop(
            1, group, add, partial[pl.ds(start, chunk), :]
        )

        def gather(i, carry):
            pltpu.make_async_remote_copy(
                src_ref=piece(grads, me), dst_ref=piece(grads, me),
                send_sem=ag_send, recv_sem=ag_recv,
                device_id=of_group(lax.rem(me + i, group)), device_id_type=MESH,
            ).start()
            return carry

        lax.fori_loop(1, group, gather, 0)

    for store in stores:
        store.wait()
    for l in range(n_lon):
        @pl.when(lat < n_lat - 1)
        def _(l=l):
            up_copy(l).wait_send()

        @pl.when(lat > 0)
        def _(l=l):
            down_copy(l).wait_send()

        @pl.when(lon != l)
        def _(l=l):
            own_copy(l).wait_send()

        for m in range(n_mem):
            @pl.when(elsewhere(l, m))
            def _(l=l, m=m):
                force_copy(l, m).wait_send()

    @pl.when(lat < n_lat - 1)
    def _():
        row_up().wait_send()

    @pl.when(lat > 0)
    def _():
        row_down().wait_send()

    col_east().wait_send()
    col_west().wait_send()

    @pl.when(me < owners)
    def _():
        passed(partial, (owners - 1) * chunk, rs_send)
        passed(grads, (owners - 1) * chunk, ag_recv)
        passed(scattered, group - 1, ag_send)

    @pl.when(me >= owners)
    def _():
        passed(partial, owners * chunk, rs_send)
        passed(grads, owners * chunk, ag_recv)


def finish(velo_in, temp_in, grads, velo_out, temp_out, first, middle, last, sems):
    moves = [
        pltpu.make_async_copy(velo_in.at[c], velo_out.at[c], sems.at[c]) for c in range(2)
    ]
    moves.append(pltpu.make_async_copy(temp_in, temp_out, sems.at[2]))
    for move in moves:
        move.start()
    for a in range(3):
        for b in range(3):
            k = 3 * a + b
            for m in range(2):
                cols = slice(m * HID, (m + 1) * HID)
                middle[m, k] = grads[a * 192 + b * HID : a * 192 + (b + 1) * HID, cols]
                at_row = MID_ROWS + (2 - a) * 24 + b * 8 + 4 + 2 * m
                last[m, k] = grads[at_row : at_row + 2, cols]
                for c in range(3):
                    at_row = MID_ROWS + SMALL_ROWS + a * 24 + b * 8 + c
                    first[k, c, m : m + 1, :] = grads[at_row : at_row + 1, cols]
    for move in moves:
        move.wait()


def per_device(n_lat, n_lon, n_mem, velo, temp, land, target, w_first, w_middle, w_last):
    rows, cols = temp.shape[1], temp.shape[2]
    rc, cc = rows // COARSE, cols // COARSE
    width = cc * n_lon
    group = n_lat * n_lon
    chunk, owners = chunking(group)
    mine = w_first.shape[0]

    vmem = pl.BlockSpec(memory_space=pltpu.VMEM)
    hbm = pl.BlockSpec(memory_space=pl.ANY)
    dma = pltpu.SemaphoreType.DMA
    fields = [jax.ShapeDtypeStruct(velo.shape, F32), jax.ShapeDtypeStruct(temp.shape, F32)]
    velo_next, temp_next, grads = pl.pallas_call(
        functools.partial(kernel, n_lat, n_lon, n_mem),
        out_shape=(*fields, jax.ShapeDtypeStruct((owners * chunk, 128), F32)),
        in_specs=[hbm] * 4 + [vmem] * 3,
        out_specs=(hbm, hbm, vmem),
        scratch_shapes=[
            pltpu.VMEM(velo.shape, F32),
            pltpu.VMEM(temp.shape, F32),
            pltpu.VMEM(land.shape, jnp.int32),
            pltpu.VMEM(target.shape, BF16),
            pltpu.VMEM((LEV * rows, cc), F32),
            pltpu.VMEM((LEV * 2 * rows, cc), F32),
            pltpu.VMEM((LEV * rc * 8, cc), F32),
            pltpu.VMEM((LEV, rc, 8, cc), BF16),
            pltpu.VMEM((n_lon, rc + 2 * HALO, 8, cc), BF16),
            pltpu.VMEM((rc + 2 * HALO, 32, width), BF16),
            pltpu.VMEM((2, rc + 8, 3 * HID, width), BF16),
            pltpu.VMEM((rc + 6, 2 * HID, width), BF16),
            pltpu.VMEM((rc + 4, 32, width), BF16),
            pltpu.VMEM((2, rc + 2, 3 * HID, width), BF16),
            pltpu.VMEM((2, rc, width), F32),
            pltpu.VMEM((n_mem, n_lon, 2, rc, cc), F32),
            pltpu.VMEM((LEV * 2, rows, cols), F32),
            pltpu.VMEM((3 * LEV, rows + 16, cols), F32),
            pltpu.VMEM((2, 16, cols), F32),
            pltpu.VMEM((2, 16, cols), F32),
            pltpu.VMEM((2, rows, 128), F32),
            pltpu.VMEM((2, rows, 128), F32),
            pltpu.VMEM((96, 128), F32),
            pltpu.VMEM((72, 128), F32),
            pltpu.VMEM((owners * chunk, 128), F32),
            pltpu.VMEM((group, chunk, 128), F32),
            dma((5,)),
            dma((2,)),
            dma((3, n_lon)),
            dma((3, n_lon)),
            dma((4,)),
            dma((4,)),
            dma((n_mem, n_lon)),
            dma((n_mem, n_lon)),
            dma,
            dma,
            dma,
            dma,
            dma,
        ],
        compiler_params=pltpu.CompilerParams(
            collective_id=0, has_side_effects=True, vmem_limit_bytes=56 * 1024 * 1024
        ),
        name="ocean_step",
    )(velo, temp, land, target, jnp.transpose(w_first, (1, 3, 0, 2)), w_middle, w_last)
    velo_next, temp_next, first, middle, last = pl.pallas_call(
        finish,
        out_shape=(
            *fields,
            jax.ShapeDtypeStruct((9, 3, mine, HID), F32),
            jax.ShapeDtypeStruct(w_middle.shape, F32),
            jax.ShapeDtypeStruct(w_last.shape, F32),
        ),
        in_specs=[hbm, hbm, vmem],
        out_specs=(hbm, hbm, vmem, vmem, vmem),
        scratch_shapes=[dma((3,))],
        name="finish",
    )(velo_next, temp_next, grads)
    return (velo_next, temp_next, jnp.transpose(first, (2, 0, 3, 1)), middle, last)


def solution(mesh):
    return jax.shard_map(
        functools.partial(per_device, mesh.shape["lat"], mesh.shape["lon"], mesh.shape["mem"]),
        mesh=mesh,
        in_specs=(
            P(None, None, "lat", "lon"),
            P(None, "lat", "lon"),
            P("lat", "lon"),
            P(None, None, "lat", "lon"),
            P("mem", None, None, None),
            P("mem", None, None, None),
            P("mem", None, None, None),
        ),
        out_specs=(
            P(None, None, "lat", "lon"),
            P(None, "lat", "lon"),
            P("mem", None, None, None),
            P("mem", None, None, None),
            P("mem", None, None, None),
        ),
        check_vma=False,
    )
```

```python
import functools
import math

import jax
import jax.numpy as jnp
from jax import lax
from jax.experimental import pallas as pl
from jax.experimental.pallas import tpu as pltpu
from jax.sharding import PartitionSpec as P

LEV = 4
COARSE = 4
HID = 64
HALO = 5
MESH = pl.DeviceIdType.MESH
F32 = jnp.float32
BF16 = jnp.bfloat16
MID_ROWS = 9 * HID
SMALL_ROWS = 72
GRAD_ROWS = MID_ROWS + 2 * SMALL_ROWS
NT = (((1,), (1,)), ((), ()))


def chunking(plane):
    tiles = -(-GRAD_ROWS // 16)
    per = -(-tiles // plane)
    owners = -(-tiles // per)
    return per * 8, owners


def shift_cols(value, by):
    return pltpu.roll(value, by % value.shape[-1], axis=value.ndim - 1)


def kernel(
    n_lat, n_lon, n_mem,
    velo_in, temp_in, land_in, target_in, w_first, w_middle, w_last,
    velo_out, temp_out, grads,
    velo_new, temp_new, land, target,
    narrow, tall, staged, send_buf, rx, s0, s1, h2s, g3s, d2s, pred_buf, force_rx, force_up, pad,
    row_send, row_rx, col_send, col_rx, w1_rows, wl_rows, partial, theirs, halved, scattered, gathered,
    in_sem, out_sem,
    cp_send, cp_recv, cs_sem, cr_sem, os_sem, or_sem, fs_sem, fr_sem, fl_sem, rs_send, rs_recv, ag_send, ag_recv,
):
    lat = lax.axis_index("lat")
    lon = lax.axis_index("lon")
    mem = lax.axis_index("mem")
    rows = temp_in.shape[1]
    cols = temp_in.shape[2]
    rc = rows // COARSE
    cc = cols // COARSE
    width = cc * n_lon
    nyc = rc * n_lat
    group = n_lat * n_lon
    planes = n_lon // 2
    plane = n_lat * planes
    chunk, owners = chunking(plane)
    half = chunk * owners
    core = lax.rem(lon, 2)
    partner = lon + 1 - 2 * core
    me = lat * n_lon + lon
    rank = lat * planes + lon // 2

    def at(lat_to, lon_to, mem_to):
        return {"lat": lat_to, "lon": lon_to, "mem": mem_to}

    def of_group(index):
        return at(index // n_lon, lax.rem(index, n_lon), mem)

    inner = pl.ds(8, rows)
    loads = [
        pltpu.make_async_copy(velo_in.at[c], pad.at[pl.ds(c * LEV, LEV), inner], in_sem.at[c])
        for c in range(2)
    ]
    loads.append(
        pltpu.make_async_copy(temp_in, pad.at[pl.ds(2 * LEV, LEV), inner], in_sem.at[2])
    )
    loads.append(pltpu.make_async_copy(target_in, target, in_sem.at[3]))
    loads.append(pltpu.make_async_copy(land_in, land, in_sem.at[4]))
    for load in loads:
        load.start()

    def of_plane(index):
        return at(index // planes, 2 * lax.rem(index, planes) + core, mem)

    barrier = pltpu.get_barrier_semaphore()

    def greet(i, carry):
        pl.semaphore_signal(
            barrier, inc=1, device_id=of_group(lax.rem(me + i, group)), device_id_type=MESH
        )
        return carry

    lax.fori_loop(1, group, greet, 0)
    for other in range(1, n_mem):
        for l in range(n_lon):
            pl.semaphore_signal(
                barrier, inc=1, device_id=at(lat, l, lax.rem(mem + other, n_mem)), device_id_type=MESH
            )

    q_ids = lax.broadcasted_iota(jnp.int32, (cc, cols), 0)
    i_ids = lax.broadcasted_iota(jnp.int32, (cc, cols), 1)
    expand = jnp.where(i_ids // COARSE == q_ids, 1.0, 0.0).astype(F32)

    for load in loads[:4]:
        load.wait()
    staged[...] = jnp.zeros_like(staged)
    for c in range(3):
        fine = pad[c * LEV : (c + 1) * LEV, 8 : 8 + rows, :].reshape(LEV * rows, cols)
        narrow[...] = lax.dot_general(
            fine * (1.0 / COARSE**2), expand, NT,
            precision=lax.Precision.HIGHEST, preferred_element_type=F32,
        )
        pooled = narrow[pl.ds(0, LEV * rc, stride=COARSE), :]
        for r in range(1, COARSE):
            pooled = pooled + narrow[pl.ds(r, LEV * rc, stride=COARSE), :]
        staged[pl.ds(c, LEV * rc, stride=8), :] = pooled
    for c in range(2):
        goal = target[c].astype(F32).reshape(LEV * rc, cc)
        staged[pl.ds(4 + c, LEV * rc, stride=8), :] = goal
        staged[pl.ds(6 + c, LEV * rc, stride=8), :] = goal
    send_buf[...] = staged[...].astype(BF16).reshape(send_buf.shape)

    lane = lax.broadcasted_iota(jnp.int32, (rows, 128), 1)
    west_cols = jnp.zeros((rows, 128), F32)
    east_cols = jnp.zeros((rows, 128), F32)
    for q in range(3 * LEV):
        first = pad[q, 8 : 8 + rows, 0:128]
        last = pad[q, 8 : 8 + rows, cols - 128 : cols]
        west_cols = jnp.where(lane == q, jnp.broadcast_to(first[:, 0:1], (rows, 128)), west_cols)
        east_cols = jnp.where(lane == q, jnp.broadcast_to(last[:, 127:128], (rows, 128)), east_cols)
        row_send[0, q : q + 1, :] = pad[q, 8:9, :]
        row_send[1, q : q + 1, :] = pad[q, 7 + rows : 8 + rows, :]
    col_send[0] = west_cols
    col_send[1] = east_cols

    @pl.when(lat == 0)
    def _():
        rx[:, 0:HALO] = jnp.zeros((n_lon, HALO, 8, cc), BF16)
        row_rx[0] = jnp.zeros_like(row_rx[0])

    @pl.when(lat == n_lat - 1)
    def _():
        rx[:, HALO + rc : 2 * HALO + rc] = jnp.zeros((n_lon, HALO, 8, cc), BF16)
        row_rx[1] = jnp.zeros_like(row_rx[1])

    pl.semaphore_wait(barrier, group - 1 + (n_mem - 1) * n_lon)

    def own_copy(l):
        return pltpu.make_async_remote_copy(
            src_ref=send_buf.at[l], dst_ref=rx.at[lon, pl.ds(HALO, rc)],
            send_sem=cs_sem.at[0, l], recv_sem=cr_sem.at[0, lon],
            device_id=at(lat, l, mem), device_id_type=MESH,
        )

    def up_copy(l):
        return pltpu.make_async_remote_copy(
            src_ref=send_buf.at[l, pl.ds(rc - HALO, HALO)], dst_ref=rx.at[lon, pl.ds(0, HALO)],
            send_sem=cs_sem.at[1, l], recv_sem=cr_sem.at[1, lon],
            device_id=at(lat + 1, l, mem), device_id_type=MESH,
        )

    def down_copy(l):
        return pltpu.make_async_remote_copy(
            src_ref=send_buf.at[l, pl.ds(0, HALO)], dst_ref=rx.at[lon, pl.ds(HALO + rc, HALO)],
            send_sem=cs_sem.at[2, l], recv_sem=cr_sem.at[2, lon],
            device_id=at(lat - 1, l, mem), device_id_type=MESH,
        )

    def row_up():
        return pltpu.make_async_remote_copy(
            src_ref=row_send.at[1], dst_ref=row_rx.at[0], send_sem=os_sem.at[0], recv_sem=or_sem.at[0],
            device_id=at(lat + 1, lon, mem), device_id_type=MESH,
        )

    def row_down():
        return pltpu.make_async_remote_copy(
            src_ref=row_send.at[0], dst_ref=row_rx.at[1], send_sem=os_sem.at[1], recv_sem=or_sem.at[1],
            device_id=at(lat - 1, lon, mem), device_id_type=MESH,
        )

    def col_east():
        return pltpu.make_async_remote_copy(
            src_ref=col_send.at[1], dst_ref=col_rx.at[0], send_sem=os_sem.at[2], recv_sem=or_sem.at[2],
            device_id=at(lat, lax.rem(lon + 1, n_lon), mem), device_id_type=MESH,
        )

    def col_west():
        return pltpu.make_async_remote_copy(
            src_ref=col_send.at[0], dst_ref=col_rx.at[1], send_sem=os_sem.at[3], recv_sem=or_sem.at[3],
            device_id=at(lat, lax.rem(lon + n_lon - 1, n_lon), mem), device_id_type=MESH,
        )

    for l in range(n_lon):
        @pl.when(lat < n_lat - 1)
        def _(l=l):
            up_copy(l).start()

        @pl.when(lat > 0)
        def _(l=l):
            down_copy(l).start()

        @pl.when(lon != l)
        def _(l=l):
            own_copy(l).start()

    @pl.when(lat < n_lat - 1)
    def _():
        row_up().start()

    @pl.when(lat > 0)
    def _():
        row_down().start()

    col_east().start()
    col_west().start()

    rx[lon, HALO : HALO + rc] = send_buf[lon]
    def flip(matrix):
        size = matrix.shape[1]
        eye = jnp.where(
            lax.broadcasted_iota(jnp.int32, (size, size), 0)
            == lax.broadcasted_iota(jnp.int32, (size, size), 1),
            1.0, 0.0,
        ).astype(BF16)
        return lax.dot_general(eye, matrix, NT, preferred_element_type=F32).astype(BF16)

    def beside(blocks):
        return jnp.concatenate(blocks, axis=1)

    w1_rows[...] = jnp.zeros_like(w1_rows)
    wl_rows[...] = jnp.zeros_like(wl_rows)
    for a in range(3):
        for b in range(3):
            k = 3 * a + b
            for c in range(3):
                pair = w_first[k, c].astype(F32)
                for m in range(2):
                    at_row = a * 32 + b * 8 + c
                    w1_rows[at_row : at_row + 1, m * HID : (m + 1) * HID] = pair[m : m + 1]
            for m in range(2):
                at_row = a * 24 + b * 8 + 4 + 2 * m
                wl_rows[at_row : at_row + 2, m * HID : (m + 1) * HID] = w_last[m, k].astype(F32)
    w1 = flip(w1_rows[...].astype(BF16))
    wl = wl_rows[...].astype(BF16)
    gap = jnp.zeros((8, 2 * HID), F32)
    w3 = jnp.concatenate([p for t in (2, 1, 0) for p in (wl_rows[24 * t : 24 * t + 24, :], gap)], axis=0)
    w3t = flip(w3.astype(BF16))
    w2 = [
        jnp.concatenate([beside([w_middle[m, 3 * a + b] for b in range(3)]) for a in range(3)], axis=0)
        for m in range(2)
    ]
    w2t = [
        flip(jnp.concatenate([beside([w_middle[m, 3 * a + b] for a in range(3)]) for b in range(3)], axis=0))
        for m in range(2)
    ]

    def arrived(kind, l, src, dst):
        pltpu.make_async_copy(src, dst, cr_sem.at[kind, l]).wait()

    for l in range(n_lon):
        @pl.when(lon != l)
        def _(l=l):
            arrived(0, l, send_buf.at[l], rx.at[l, pl.ds(HALO, rc)])

        @pl.when(lat > 0)
        def _(l=l):
            arrived(1, l, send_buf.at[l, pl.ds(0, HALO)], rx.at[l, pl.ds(0, HALO)])

        @pl.when(lat < n_lat - 1)
        def _(l=l):
            arrived(2, l, send_buf.at[l, pl.ds(0, HALO)], rx.at[l, pl.ds(HALO + rc, HALO)])

    def inside(g):
        return jnp.where(jnp.logical_and(g >= 0, g < nyc), 1.0, 0.0).astype(F32)

    def received(x):
        return jnp.concatenate([rx[l, x].astype(F32) for l in range(n_lon)], axis=-1)

    def three(v):
        return jnp.concatenate([shift_cols(v, 1), v, shift_cols(v, -1), jnp.zeros_like(v)], axis=0)

    for x in range(rc + 2 * HALO):
        s0[x] = three(received(x)).astype(BF16)

    for r in range(rc + 8):
        block = s0[r : r + 3].reshape(96, width)
        h = jnp.tanh(jnp.dot(w1, block, preferred_element_type=F32)) * inside(lat * rc - 4 + r)
        for m in range(2):
            hm = h[m * HID : (m + 1) * HID]
            s1[m, r, 0:HID] = shift_cols(hm, 1).astype(BF16)
            s1[m, r, HID : 2 * HID] = hm.astype(BF16)
            s1[m, r, 2 * HID : 3 * HID] = shift_cols(hm, -1).astype(BF16)

    def taps(products, r, order):
        return sum(
            products[r + i][j * HID : (j + 1) * HID] for i, j in enumerate(order)
        )

    for m in range(2):
        products = [
            jnp.dot(w2[m], s1[m, x], preferred_element_type=F32) for x in range(rc + 8)
        ]
        for r in range(rc + 6):
            h = jnp.tanh(taps(products, r, (0, 1, 2))) * inside(lat * rc - 3 + r)
            h2s[r, m * HID : (m + 1) * HID] = h.astype(BF16)

    scale = 2.0 / (2.0 * LEV * nyc * width)
    sub = lax.broadcasted_iota(jnp.int32, (8, width), 0)
    outs = [jnp.dot(wl, h2s[x], preferred_element_type=F32) for x in range(rc + 6)]
    for r in range(rc + 4):
        u = [sum(outs[r + a][24 * a + 8 * b : 24 * a + 8 * b + 8] for a in range(3)) for b in range(3)]
        pred = shift_cols(u[0], 1) + u[1] + shift_cols(u[2], -1)
        g3 = jnp.where(sub >= 4, (pred - received(r + 3)) * scale, 0.0) * inside(lat * rc - 2 + r)
        g3s[r] = jnp.concatenate(
            [shift_cols(g3, -1), g3, shift_cols(g3, 1), jnp.zeros_like(g3)], axis=0
        ).astype(BF16)
        if 2 <= r < 2 + rc:
            both = pred[4:6] + pred[6:8]
            for o in range(2):
                pred_buf[o, r - 2 : r - 1, :] = both[o : o + 1]

    def force_copy(l, m):
        return pltpu.make_async_remote_copy(
            src_ref=pred_buf.at[:, :, pl.ds(l * cc, cc)], dst_ref=force_rx.at[mem, lon],
            send_sem=fs_sem.at[m, l], recv_sem=fr_sem.at[mem, lon],
            device_id=at(lat, l, m), device_id_type=MESH,
        )

    def force_own():
        return pltpu.make_async_copy(
            pred_buf.at[:, :, pl.ds(pl.multiple_of(lon * cc, cc), cc)], force_rx.at[mem, lon], fl_sem
        )

    def elsewhere(l, m):
        return jnp.logical_or(lon != l, mem != m)

    for m in range(n_mem):
        for l in range(n_lon):
            @pl.when(elsewhere(l, m))
            def _(l=l, m=m):
                force_copy(l, m).start()

    force_own().start()

    for r in range(rc + 2):
        block = g3s[r : r + 3].reshape(96, width)
        h = h2s[r + 2].astype(F32)
        d = jnp.dot(w3t, block, preferred_element_type=F32) * (1.0 - h * h)
        d = d * inside(lat * rc - 1 + r)
        for m in range(2):
            dm = d[m * HID : (m + 1) * HID]
            d2s[m, r, 0:HID] = shift_cols(dm, -1).astype(BF16)
            d2s[m, r, HID : 2 * HID] = dm.astype(BF16)
            d2s[m, r, 2 * HID : 3 * HID] = shift_cols(dm, 1).astype(BF16)

    def over_rows(left, right):
        return lax.dot_general(
            beside([left(r) for r in range(rc)]), beside([right(r) for r in range(rc)]), NT,
            preferred_element_type=F32,
        )

    mids = [
        over_rows(
            lambda r: d2s[m, r + 1],
            lambda r: s1[m, r + 3 : r + 6, HID : 2 * HID].reshape(3 * HID, width),
        )
        for m in range(2)
    ]
    def put(start, value):
        low = min(max(half - start, 0), value.shape[0])
        if low > 0:
            partial[0, start : start + low, :] = value[:low]
        if low < value.shape[0]:
            partial[1, start + low - half : start + value.shape[0] - half, :] = value[low:]

    for a in range(3):
        put(a * 192, beside([mids[m][:, a * HID : (a + 1) * HID] for m in range(2)]))
    last = over_rows(lambda r: g3s[r + 1 : r + 4].reshape(96, width), lambda r: h2s[r + 3])
    for a in range(3):
        at_row = MID_ROWS + 24 * a
        put(at_row, last[32 * a : 32 * a + 24, :])

    def core_copy(which):
        start, size = ((0, split), (split, half - split))[which]
        return pltpu.make_async_remote_copy(
            src_ref=partial.at[1 - core, pl.ds(start, size)], dst_ref=theirs.at[pl.ds(start, size)],
            send_sem=cp_send.at[which], recv_sem=cp_recv.at[which],
            device_id=at(lat, partner, mem), device_id_type=MESH,
        )

    split = (MID_ROWS + SMALL_ROWS - half) // 8 * 8
    core_copy(0).start()

    d1s = []
    for m in range(2):
        products = [
            jnp.dot(w2t[m], d2s[m, x], preferred_element_type=F32) for x in range(rc + 2)
        ]
        own = []
        for r in range(rc):
            h = s1[m, r + 4, HID : 2 * HID].astype(F32)
            own.append((taps(products, r, (2, 1, 0)) * (1.0 - h * h)).astype(BF16))
        d1s.append(own)
    first = over_rows(
        lambda r: s0[r + 4 : r + 7].reshape(96, width),
        lambda r: jnp.concatenate([d1s[0][r], d1s[1][r]], axis=0),
    )
    for a in range(3):
        at_row = MID_ROWS + SMALL_ROWS + 24 * a
        put(at_row, first[32 * a : 32 * a + 24, :])
    if 2 * half > GRAD_ROWS:
        put(GRAD_ROWS, jnp.zeros((2 * half - GRAD_ROWS, 128), F32))
    core_copy(1).start()
    for which in range(2):
        core_copy(which).wait()
    halved[...] = partial[core] + theirs[...]

    def piece(ref, index):
        return ref.at[pl.ds(pl.multiple_of(index * chunk, chunk), chunk)]

    for i in range(owners):
        to = lax.rem(rank + i, owners)

        @pl.when(to != rank)
        def _(to=to):
            pltpu.make_async_remote_copy(
                src_ref=piece(halved, to), dst_ref=scattered.at[rank],
                send_sem=rs_send, recv_sem=rs_recv, device_id=of_plane(to), device_id_type=MESH,
            ).start()


    for m in range(n_mem):
        for l in range(n_lon):
            @pl.when(elsewhere(l, m))
            def _(l=l, m=m):
                pltpu.make_async_copy(
                    pred_buf.at[:, :, pl.ds(0, cc)], force_rx.at[m, l], fr_sem.at[m, l]
                ).wait()

    force_own().wait()

    @pl.when(lat > 0)
    def _():
        pltpu.make_async_copy(row_send.at[0], row_rx.at[0], or_sem.at[0]).wait()

    @pl.when(lat < n_lat - 1)
    def _():
        pltpu.make_async_copy(row_send.at[0], row_rx.at[1], or_sem.at[1]).wait()

    pltpu.make_async_copy(col_send.at[0], col_rx.at[0], or_sem.at[2]).wait()
    pltpu.make_async_copy(col_send.at[0], col_rx.at[1], or_sem.at[3]).wait()

    summed = force_rx[0]
    for m in range(1, n_mem):
        summed = summed + force_rx[m]
    mean = (summed * (1.0 / (2 * n_mem))).reshape(LEV * 2 * rc, cc)
    for r in range(COARSE):
        tall[pl.ds(r, LEV * 2 * rc, stride=COARSE), :] = mean
    force_up[...] = jnp.dot(
        tall[...], expand, precision=lax.Precision.HIGHEST, preferred_element_type=F32
    ).reshape(force_up.shape)
    for q in range(3 * LEV):
        pad[q, 7:8, :] = row_rx[0, q : q + 1, :]
        pad[q, 8 + rows : 9 + rows, :] = row_rx[1, q : q + 1, :]

    loads[4].wait()
    lane_ids = lax.broadcasted_iota(jnp.int32, (8, cols), 1)
    for s in range(rows // 8):
        base = 8 + 8 * s
        ids = (lat * rows + 8 * s + lax.broadcasted_iota(jnp.int32, (8, cols), 0)).astype(F32)
        coriolis = jnp.sin(-math.pi / 2 + math.pi * (ids + 0.5) / (rows * n_lat))
        wet = 0.1 * land[8 * s : 8 * s + 8, :].astype(F32)
        sum_x = jnp.zeros((8, cols), F32)
        sum_y = jnp.zeros((8, cols), F32)
        for l in range(LEV):
            got = []
            for c in range(3):
                q = c * LEV + l
                centre = pad[q, base : base + 8, :]
                south = pad[q, base - 1 : base + 7, :]
                north = pad[q, base + 1 : base + 9, :]
                before = col_rx[0, 8 * s : 8 * s + 8, q : q + 1]
                after = col_rx[1, 8 * s : 8 * s + 8, q : q + 1]
                west = jnp.where(lane_ids == 0, before, shift_cols(centre, 1))
                east = jnp.where(lane_ids == cols - 1, after, shift_cols(centre, -1))
                got.append((centre, east, west, north, south))
            laps = [e + w + n + so - 4.0 * ce for ce, e, w, n, so in got]
            u, v, t = got[0][0], got[1][0], got[2][0]
            dx = got[2][1] - got[2][2]
            dy = got[2][3] - got[2][4]
            sum_x = sum_x + dx
            sum_y = sum_y + dy
            fu = force_up[l * 2, 8 * s : 8 * s + 8, :]
            fv = force_up[l * 2 + 1, 8 * s : 8 * s + 8, :]
            velo_new[0, l, 8 * s : 8 * s + 8, :] = u + wet * (
                coriolis * v + 0.25 * sum_x + 0.5 * laps[0] + fu
            )
            velo_new[1, l, 8 * s : 8 * s + 8, :] = v + wet * (
                -coriolis * u + 0.25 * sum_y + 0.5 * laps[1] + fv
            )
            temp_new[l, 8 * s : 8 * s + 8, :] = t + wet * (
                -0.5 * (u * dx + v * dy) + 0.3 * laps[2]
            )

    stores = [
        pltpu.make_async_copy(velo_new, velo_out, out_sem.at[0]),
        pltpu.make_async_copy(temp_new, temp_out, out_sem.at[1]),
    ]
    for store in stores:
        store.start()

    def passed(ref, count, sem):
        pltpu.make_async_copy(ref.at[pl.ds(0, count)], ref.at[pl.ds(0, count)], sem).wait()

    @pl.when(rank < owners)
    def _():
        passed(scattered, plane - 1, rs_recv)
        start = pl.multiple_of(rank * chunk, chunk)
        total = halved[pl.ds(start, chunk), :]
        for i in range(1, plane):
            total = total + scattered[lax.rem(rank + i, plane)]
        gathered[core, pl.ds(start, chunk), :] = total
        for i in range(1, plane):
            pltpu.make_async_remote_copy(
                src_ref=piece(gathered.at[core], rank), dst_ref=piece(gathered.at[core], rank),
                send_sem=ag_send, recv_sem=ag_recv,
                device_id=of_plane(lax.rem(rank + i, plane)), device_id_type=MESH,
            ).start()

    @pl.when(rank < owners)
    def _():
        passed(halved, (owners - 1) * chunk, ag_recv)

    @pl.when(rank >= owners)
    def _():
        passed(halved, owners * chunk, ag_recv)

    share = pltpu.make_async_remote_copy(
        src_ref=gathered.at[core], dst_ref=gathered.at[core],
        send_sem=cp_send.at[2], recv_sem=cp_recv.at[2],
        device_id=at(lat, partner, mem), device_id_type=MESH,
    )
    share.start()

    for store in stores:
        store.wait()
    for l in range(n_lon):
        @pl.when(lat < n_lat - 1)
        def _(l=l):
            up_copy(l).wait_send()

        @pl.when(lat > 0)
        def _(l=l):
            down_copy(l).wait_send()

        @pl.when(lon != l)
        def _(l=l):
            own_copy(l).wait_send()

        for m in range(n_mem):
            @pl.when(elsewhere(l, m))
            def _(l=l, m=m):
                force_copy(l, m).wait_send()

    @pl.when(lat < n_lat - 1)
    def _():
        row_up().wait_send()

    @pl.when(lat > 0)
    def _():
        row_down().wait_send()

    col_east().wait_send()
    col_west().wait_send()

    @pl.when(rank < owners)
    def _():
        passed(halved, (owners - 1) * chunk, rs_send)
        passed(scattered, plane - 1, ag_send)

    @pl.when(rank >= owners)
    def _():
        passed(halved, owners * chunk, rs_send)

    share.wait()
    grads[...] = gathered[...]


def finish(velo_in, temp_in, halves, velo_out, temp_out, first, middle, last, velo, temp, sems):
    blocks = [(velo_in.at[c], velo.at[c], velo_out.at[c]) for c in range(2)]
    blocks.append((temp_in, temp, temp_out))
    loads = [pltpu.make_async_copy(b[0], b[1], sems.at[i]) for i, b in enumerate(blocks)]
    stores = [pltpu.make_async_copy(b[1], b[2], sems.at[i]) for i, b in enumerate(blocks)]
    for load in loads:
        load.start()
    for load, store in zip(loads, stores):
        load.wait()
        store.start()
    half = halves.shape[1]

    def rows_of(start, size, cols):
        low = min(max(half - start, 0), size)
        parts = []
        if low > 0:
            parts.append(halves[0, start : start + low, cols])
        if low < size:
            parts.append(halves[1, start + low - half : start + size - half, cols])
        return parts[0] if len(parts) == 1 else jnp.concatenate(parts, axis=0)

    for a in range(3):
        for b in range(3):
            k = 3 * a + b
            for m in range(2):
                cols = slice(m * HID, (m + 1) * HID)
                middle[m, k] = rows_of(a * 192 + b * HID, HID, cols)
                at_row = MID_ROWS + (2 - a) * 24 + b * 8 + 4 + 2 * m
                last[m, k] = rows_of(at_row, 2, cols)
                for c in range(3):
                    at_row = MID_ROWS + SMALL_ROWS + a * 24 + b * 8 + c
                    first[k, c, m : m + 1, :] = rows_of(at_row, 1, cols)
    for store in stores:
        store.wait()


def per_device(n_lat, n_lon, n_mem, velo, temp, land, target, w_first, w_middle, w_last):
    rows, cols = temp.shape[1], temp.shape[2]
    rc, cc = rows // COARSE, cols // COARSE
    width = cc * n_lon
    plane = n_lat * (n_lon // 2)
    chunk, owners = chunking(plane)
    half = chunk * owners
    mine = w_first.shape[0]

    vmem = pl.BlockSpec(memory_space=pltpu.VMEM)
    hbm = pl.BlockSpec(memory_space=pl.ANY)
    dma = pltpu.SemaphoreType.DMA
    fields = [jax.ShapeDtypeStruct(velo.shape, F32), jax.ShapeDtypeStruct(temp.shape, F32)]
    velo_next, temp_next, grads = pl.pallas_call(
        functools.partial(kernel, n_lat, n_lon, n_mem),
        out_shape=(*fields, jax.ShapeDtypeStruct((2, half, 128), F32)),
        in_specs=[hbm] * 4 + [vmem] * 3,
        out_specs=(hbm, hbm, vmem),
        scratch_shapes=[
            pltpu.VMEM(velo.shape, F32),
            pltpu.VMEM(temp.shape, F32),
            pltpu.VMEM(land.shape, jnp.int32),
            pltpu.VMEM(target.shape, BF16),
            pltpu.VMEM((LEV * rows, cc), F32),
            pltpu.VMEM((LEV * 2 * rows, cc), F32),
            pltpu.VMEM((LEV * rc * 8, cc), F32),
            pltpu.VMEM((LEV, rc, 8, cc), BF16),
            pltpu.VMEM((n_lon, rc + 2 * HALO, 8, cc), BF16),
            pltpu.VMEM((rc + 2 * HALO, 32, width), BF16),
            pltpu.VMEM((2, rc + 8, 3 * HID, width), BF16),
            pltpu.VMEM((rc + 6, 2 * HID, width), BF16),
            pltpu.VMEM((rc + 4, 32, width), BF16),
            pltpu.VMEM((2, rc + 2, 3 * HID, width), BF16),
            pltpu.VMEM((2, rc, width), F32),
            pltpu.VMEM((n_mem, n_lon, 2, rc, cc), F32),
            pltpu.VMEM((LEV * 2, rows, cols), F32),
            pltpu.VMEM((3 * LEV, rows + 16, cols), F32),
            pltpu.VMEM((2, 16, cols), F32),
            pltpu.VMEM((2, 16, cols), F32),
            pltpu.VMEM((2, rows, 128), F32),
            pltpu.VMEM((2, rows, 128), F32),
            pltpu.VMEM((96, 128), F32),
            pltpu.VMEM((72, 128), F32),
            pltpu.VMEM((2, half, 128), F32),
            pltpu.VMEM((half, 128), F32),
            pltpu.VMEM((half, 128), F32),
            pltpu.VMEM((plane, chunk, 128), F32),
            pltpu.VMEM((2, half, 128), F32),
            dma((5,)),
            dma((2,)),
            dma((3,)),
            dma((3,)),
            dma((3, n_lon)),
            dma((3, n_lon)),
            dma((4,)),
            dma((4,)),
            dma((n_mem, n_lon)),
            dma((n_mem, n_lon)),
            dma,
            dma,
            dma,
            dma,
            dma,
        ],
        compiler_params=pltpu.CompilerParams(
            collective_id=0, has_side_effects=True, vmem_limit_bytes=56 * 1024 * 1024
        ),
        name="ocean_step",
    )(velo, temp, land, target, jnp.transpose(w_first, (1, 3, 0, 2)), w_middle, w_last)
    velo_next, temp_next, first, middle, last = pl.pallas_call(
        finish,
        out_shape=(
            *fields,
            jax.ShapeDtypeStruct((9, 3, mine, HID), F32),
            jax.ShapeDtypeStruct(w_middle.shape, F32),
            jax.ShapeDtypeStruct(w_last.shape, F32),
        ),
        in_specs=[hbm, hbm, vmem],
        out_specs=(hbm, hbm, vmem, vmem, vmem),
        scratch_shapes=[pltpu.VMEM(velo.shape, F32), pltpu.VMEM(temp.shape, F32), dma((3,))],
        name="finish",
    )(velo_next, temp_next, grads)
    return (velo_next, temp_next, jnp.transpose(first, (2, 0, 3, 1)), middle, last)


def solution(mesh):
    return jax.shard_map(
        functools.partial(per_device, mesh.shape["lat"], mesh.shape["lon"], mesh.shape["mem"]),
        mesh=mesh,
        in_specs=(
            P(None, None, "lat", "lon"),
            P(None, "lat", "lon"),
            P("lat", "lon"),
            P(None, None, "lat", "lon"),
            P("mem", None, None, None),
            P("mem", None, None, None),
            P("mem", None, None, None),
        ),
        out_specs=(
            P(None, None, "lat", "lon"),
            P(None, "lat", "lon"),
            P("mem", None, None, None),
            P("mem", None, None, None),
            P("mem", None, None, None),
        ),
        check_vma=False,
    )
```

```python
import functools
import math

import jax
import jax.numpy as jnp
from jax import lax
from jax.experimental import pallas as pl
from jax.experimental.pallas import tpu as pltpu
from jax.sharding import PartitionSpec as P

LEV = 4
COARSE = 4
HID = 64
HALO = 5
MESH = pl.DeviceIdType.MESH
F32 = jnp.float32
BF16 = jnp.bfloat16
MID_ROWS = 9 * HID
SMALL_ROWS = 72
GRAD_ROWS = MID_ROWS + 2 * SMALL_ROWS
NT = (((1,), (1,)), ((), ()))


def chunking(plane):
    tiles = -(-GRAD_ROWS // 16)
    per = -(-tiles // plane)
    owners = -(-tiles // per)
    return per * 8, owners


EARLY = (MID_ROWS + SMALL_ROWS) // 8
LOW_EARLY, LOW_LATE = (EARLY + 1) // 2, (SMALL_ROWS // 8 + 1) // 2


def place(tile):
    if tile < EARLY:
        return divmod_half(tile, LOW_EARLY, 0, 0)
    return divmod_half(tile - EARLY, LOW_LATE, LOW_EARLY, EARLY - LOW_EARLY)


def divmod_half(tile, low, base_low, base_high):
    return (0, 8 * (base_low + tile)) if tile < low else (1, 8 * (base_high + tile - low))


def shift_cols(value, by):
    return pltpu.roll(value, by % value.shape[-1], axis=value.ndim - 1)


def kernel(
    n_lat, n_lon, n_mem,
    velo_in, temp_in, land_in, target_in, first_in, middle_in, last_in,
    velo_out, temp_out, grads,
    velo_new, temp_new, land, target, w_first, w_middle, w_last,
    narrow, tall, staged, send_buf, rx, s0, s1, h2s, g3s, d2s, pred_buf, force_rx, force_up, pad,
    row_send, row_rx, col_send, col_rx, w1_rows, wl_rows, partial, theirs, halved, scattered, gathered,
    in_sem, out_sem,
    cp_send, cp_recv, cs_sem, cr_sem, os_sem, or_sem, fs_sem, fr_sem, fl_sem, rs_send, rs_recv, ag_send, ag_recv,
):
    lat = lax.axis_index("lat")
    lon = lax.axis_index("lon")
    mem = lax.axis_index("mem")
    rows = temp_in.shape[1]
    cols = temp_in.shape[2]
    rc = rows // COARSE
    cc = cols // COARSE
    width = cc * n_lon
    nyc = rc * n_lat
    group = n_lat * n_lon
    planes = n_lon // 2
    plane = n_lat * planes
    chunk, owners = chunking(plane)
    half = chunk * owners
    core = lax.rem(lon, 2)
    partner = lon + 1 - 2 * core
    me = lat * n_lon + lon
    rank = lat * planes + lon // 2

    def owner(turn_of):
        return (turn_of * plane) // owners

    turn = (rank * owners + plane - 1) // plane
    is_owner = jnp.logical_and(turn < owners, owner(turn) == rank)

    def at(lat_to, lon_to, mem_to):
        return {"lat": lat_to, "lon": lon_to, "mem": mem_to}

    def of_group(index):
        return at(index // n_lon, lax.rem(index, n_lon), mem)

    inner = pl.ds(8, rows)
    loads = [
        pltpu.make_async_copy(velo_in.at[c], pad.at[pl.ds(c * LEV, LEV), inner], in_sem.at[c])
        for c in range(2)
    ]
    loads.append(
        pltpu.make_async_copy(temp_in, pad.at[pl.ds(2 * LEV, LEV), inner], in_sem.at[2])
    )
    loads.append(pltpu.make_async_copy(target_in, target, in_sem.at[3]))
    loads.append(pltpu.make_async_copy(land_in, land, in_sem.at[4]))
    loads.append(pltpu.make_async_copy(first_in, w_first, in_sem.at[5]))
    loads.append(pltpu.make_async_copy(middle_in, w_middle, in_sem.at[6]))
    loads.append(pltpu.make_async_copy(last_in, w_last, in_sem.at[7]))
    for load in loads:
        load.start()

    def of_plane(index):
        return at(index // planes, 2 * lax.rem(index, planes) + core, mem)

    barrier = pltpu.get_barrier_semaphore()

    def greet(i, carry):
        pl.semaphore_signal(
            barrier, inc=1, device_id=of_group(lax.rem(me + i, group)), device_id_type=MESH
        )
        return carry

    lax.fori_loop(1, group, greet, 0)
    for other in range(1, n_mem):
        for l in range(n_lon):
            pl.semaphore_signal(
                barrier, inc=1, device_id=at(lat, l, lax.rem(mem + other, n_mem)), device_id_type=MESH
            )

    q_ids = lax.broadcasted_iota(jnp.int32, (cc, cols), 0)
    i_ids = lax.broadcasted_iota(jnp.int32, (cc, cols), 1)
    expand = jnp.where(i_ids // COARSE == q_ids, 1.0, 0.0).astype(F32)

    for load in loads[:4]:
        load.wait()
    staged[...] = jnp.zeros_like(staged)
    for c in range(3):
        fine = pad[c * LEV : (c + 1) * LEV, 8 : 8 + rows, :].reshape(LEV * rows, cols)
        fine = fine * (1.0 / COARSE**2)
        high = fine.astype(BF16)
        rest = fine - high.astype(F32)
        middle = rest.astype(BF16)
        low = (rest - middle.astype(F32)).astype(BF16)
        parts = lax.dot_general(
            jnp.concatenate([high, middle, low], axis=0), expand.astype(BF16), NT,
            preferred_element_type=F32,
        )
        n = LEV * rows
        narrow[...] = parts[0:n] + parts[n : 2 * n] + parts[2 * n : 3 * n]
        pooled = narrow[pl.ds(0, LEV * rc, stride=COARSE), :]
        for r in range(1, COARSE):
            pooled = pooled + narrow[pl.ds(r, LEV * rc, stride=COARSE), :]
        staged[pl.ds(c, LEV * rc, stride=8), :] = pooled
    for c in range(2):
        goal = target[c].astype(F32).reshape(LEV * rc, cc)
        staged[pl.ds(4 + c, LEV * rc, stride=8), :] = goal
        staged[pl.ds(6 + c, LEV * rc, stride=8), :] = goal
    send_buf[...] = staged[...].astype(BF16).reshape(send_buf.shape)

    @pl.when(lat == 0)
    def _():
        rx[:, 0:HALO] = jnp.zeros((n_lon, HALO, 8, cc), BF16)
        row_rx[0] = jnp.zeros_like(row_rx[0])

    @pl.when(lat == n_lat - 1)
    def _():
        rx[:, HALO + rc : 2 * HALO + rc] = jnp.zeros((n_lon, HALO, 8, cc), BF16)
        row_rx[1] = jnp.zeros_like(row_rx[1])

    pl.semaphore_wait(barrier, group - 1 + (n_mem - 1) * n_lon)

    def own_copy(l):
        return pltpu.make_async_remote_copy(
            src_ref=send_buf.at[l], dst_ref=rx.at[lon, pl.ds(HALO, rc)],
            send_sem=cs_sem.at[0, l], recv_sem=cr_sem.at[0, lon],
            device_id=at(lat, l, mem), device_id_type=MESH,
        )

    def up_copy(l):
        return pltpu.make_async_remote_copy(
            src_ref=send_buf.at[l, pl.ds(rc - HALO, HALO)], dst_ref=rx.at[lon, pl.ds(0, HALO)],
            send_sem=cs_sem.at[1, l], recv_sem=cr_sem.at[1, lon],
            device_id=at(lat + 1, l, mem), device_id_type=MESH,
        )

    def down_copy(l):
        return pltpu.make_async_remote_copy(
            src_ref=send_buf.at[l, pl.ds(0, HALO)], dst_ref=rx.at[lon, pl.ds(HALO + rc, HALO)],
            send_sem=cs_sem.at[2, l], recv_sem=cr_sem.at[2, lon],
            device_id=at(lat - 1, l, mem), device_id_type=MESH,
        )

    def row_up():
        return pltpu.make_async_remote_copy(
            src_ref=row_send.at[1], dst_ref=row_rx.at[0], send_sem=os_sem.at[0], recv_sem=or_sem.at[0],
            device_id=at(lat + 1, lon, mem), device_id_type=MESH,
        )

    def row_down():
        return pltpu.make_async_remote_copy(
            src_ref=row_send.at[0], dst_ref=row_rx.at[1], send_sem=os_sem.at[1], recv_sem=or_sem.at[1],
            device_id=at(lat - 1, lon, mem), device_id_type=MESH,
        )

    def col_east():
        return pltpu.make_async_remote_copy(
            src_ref=col_send.at[1], dst_ref=col_rx.at[0], send_sem=os_sem.at[2], recv_sem=or_sem.at[2],
            device_id=at(lat, lax.rem(lon + 1, n_lon), mem), device_id_type=MESH,
        )

    def col_west():
        return pltpu.make_async_remote_copy(
            src_ref=col_send.at[0], dst_ref=col_rx.at[1], send_sem=os_sem.at[3], recv_sem=or_sem.at[3],
            device_id=at(lat, lax.rem(lon + n_lon - 1, n_lon), mem), device_id_type=MESH,
        )

    for l in range(n_lon):
        @pl.when(lat < n_lat - 1)
        def _(l=l):
            up_copy(l).start()

        @pl.when(lat > 0)
        def _(l=l):
            down_copy(l).start()

        @pl.when(lon != l)
        def _(l=l):
            own_copy(l).start()

    lane = lax.broadcasted_iota(jnp.int32, (rows, 128), 1)
    west_cols = jnp.zeros((rows, 128), F32)
    east_cols = jnp.zeros((rows, 128), F32)
    for q in range(3 * LEV):
        first = pad[q, 8 : 8 + rows, 0:128]
        last = pad[q, 8 : 8 + rows, cols - 128 : cols]
        west_cols = jnp.where(lane == q, jnp.broadcast_to(first[:, 0:1], (rows, 128)), west_cols)
        east_cols = jnp.where(lane == q, jnp.broadcast_to(last[:, 127:128], (rows, 128)), east_cols)
        row_send[0, q : q + 1, :] = pad[q, 8:9, :]
        row_send[1, q : q + 1, :] = pad[q, 7 + rows : 8 + rows, :]
    col_send[0] = west_cols
    col_send[1] = east_cols

    @pl.when(lat < n_lat - 1)
    def _():
        row_up().start()

    @pl.when(lat > 0)
    def _():
        row_down().start()

    col_east().start()
    col_west().start()

    rx[lon, HALO : HALO + rc] = send_buf[lon]
    def flip(matrix):
        size = matrix.shape[1]
        eye = jnp.where(
            lax.broadcasted_iota(jnp.int32, (size, size), 0)
            == lax.broadcasted_iota(jnp.int32, (size, size), 1),
            1.0, 0.0,
        ).astype(BF16)
        return lax.dot_general(eye, matrix, NT, preferred_element_type=F32).astype(BF16)

    def beside(blocks):
        return jnp.concatenate(blocks, axis=1)

    for load in loads[5:]:
        load.wait()
    w1_rows[...] = jnp.zeros_like(w1_rows)
    wl_rows[...] = jnp.zeros_like(wl_rows)
    for a in range(3):
        for b in range(3):
            k = 3 * a + b
            for c in range(3):
                pair = w_first[k, c].astype(F32)
                for m in range(2):
                    at_row = a * 32 + b * 8 + c
                    w1_rows[at_row : at_row + 1, m * HID : (m + 1) * HID] = pair[m : m + 1]
            for m in range(2):
                at_row = a * 24 + b * 8 + 4 + 2 * m
                wl_rows[at_row : at_row + 2, m * HID : (m + 1) * HID] = w_last[m, k].astype(F32)
    w1 = flip(w1_rows[...].astype(BF16))
    wl = wl_rows[...].astype(BF16)
    gap = jnp.zeros((8, 2 * HID), F32)
    w3 = jnp.concatenate([p for t in (2, 1, 0) for p in (wl_rows[24 * t : 24 * t + 24, :], gap)], axis=0)
    w3t = flip(w3.astype(BF16))
    w2 = [
        jnp.concatenate([beside([w_middle[m, 3 * a + b] for b in range(3)]) for a in range(3)], axis=0)
        for m in range(2)
    ]
    w2t = [
        flip(jnp.concatenate([beside([w_middle[m, 3 * a + b] for a in range(3)]) for b in range(3)], axis=0))
        for m in range(2)
    ]

    def arrived(kind, l, src, dst):
        pltpu.make_async_copy(src, dst, cr_sem.at[kind, l]).wait()

    for l in range(n_lon):
        @pl.when(lon != l)
        def _(l=l):
            arrived(0, l, send_buf.at[l], rx.at[l, pl.ds(HALO, rc)])

        @pl.when(lat > 0)
        def _(l=l):
            arrived(1, l, send_buf.at[l, pl.ds(0, HALO)], rx.at[l, pl.ds(0, HALO)])

        @pl.when(lat < n_lat - 1)
        def _(l=l):
            arrived(2, l, send_buf.at[l, pl.ds(0, HALO)], rx.at[l, pl.ds(HALO + rc, HALO)])

    def inside(g):
        return jnp.where(jnp.logical_and(g >= 0, g < nyc), 1.0, 0.0).astype(F32)

    def received(x):
        return jnp.concatenate([rx[l, x].astype(F32) for l in range(n_lon)], axis=-1)

    def three(v):
        return jnp.concatenate([shift_cols(v, 1), v, shift_cols(v, -1), jnp.zeros_like(v)], axis=0)

    for x in range(rc + 2 * HALO):
        s0[x] = three(received(x)).astype(BF16)

    for r in range(rc + 8):
        block = s0[r : r + 3].reshape(96, width)
        h = jnp.tanh(jnp.dot(w1, block, preferred_element_type=F32)) * inside(lat * rc - 4 + r)
        for m in range(2):
            hm = h[m * HID : (m + 1) * HID]
            s1[m, r, 0:HID] = shift_cols(hm, 1).astype(BF16)
            s1[m, r, HID : 2 * HID] = hm.astype(BF16)
            s1[m, r, 2 * HID : 3 * HID] = shift_cols(hm, -1).astype(BF16)

    def taps(products, r, order):
        return sum(
            products[r + i][j * HID : (j + 1) * HID] for i, j in enumerate(order)
        )

    for m in range(2):
        products = [
            jnp.dot(w2[m], s1[m, x], preferred_element_type=F32) for x in range(rc + 8)
        ]
        for r in range(rc + 6):
            h = jnp.tanh(taps(products, r, (0, 1, 2))) * inside(lat * rc - 3 + r)
            h2s[r, m * HID : (m + 1) * HID] = h.astype(BF16)

    scale = 2.0 / (2.0 * LEV * nyc * width)
    sub = lax.broadcasted_iota(jnp.int32, (8, width), 0)
    outs = [jnp.dot(wl, h2s[x], preferred_element_type=F32) for x in range(rc + 6)]
    for r in range(rc + 4):
        u = [sum(outs[r + a][24 * a + 8 * b : 24 * a + 8 * b + 8] for a in range(3)) for b in range(3)]
        pred = shift_cols(u[0], 1) + u[1] + shift_cols(u[2], -1)
        g3 = jnp.where(sub >= 4, (pred - received(r + 3)) * scale, 0.0) * inside(lat * rc - 2 + r)
        g3s[r] = jnp.concatenate(
            [shift_cols(g3, -1), g3, shift_cols(g3, 1), jnp.zeros_like(g3)], axis=0
        ).astype(BF16)
        if 2 <= r < 2 + rc:
            both = pred[4:6] + pred[6:8]
            for o in range(2):
                pred_buf[o, r - 2 : r - 1, :] = both[o : o + 1]

    def force_copy(l, m):
        return pltpu.make_async_remote_copy(
            src_ref=pred_buf.at[:, :, pl.ds(l * cc, cc)], dst_ref=force_rx.at[mem, lon],
            send_sem=fs_sem.at[m, l], recv_sem=fr_sem.at[mem, lon],
            device_id=at(lat, l, m), device_id_type=MESH,
        )

    def force_own():
        return pltpu.make_async_copy(
            pred_buf.at[:, :, pl.ds(pl.multiple_of(lon * cc, cc), cc)], force_rx.at[mem, lon], fl_sem
        )

    def elsewhere(l, m):
        return jnp.logical_or(lon != l, mem != m)

    for m in range(n_mem):
        for l in range(n_lon):
            @pl.when(elsewhere(l, m))
            def _(l=l, m=m):
                force_copy(l, m).start()

    force_own().start()

    for r in range(rc + 2):
        block = g3s[r : r + 3].reshape(96, width)
        h = h2s[r + 2].astype(F32)
        d = jnp.dot(w3t, block, preferred_element_type=F32) * (1.0 - h * h)
        d = d * inside(lat * rc - 1 + r)
        for m in range(2):
            dm = d[m * HID : (m + 1) * HID]
            d2s[m, r, 0:HID] = shift_cols(dm, -1).astype(BF16)
            d2s[m, r, HID : 2 * HID] = dm.astype(BF16)
            d2s[m, r, 2 * HID : 3 * HID] = shift_cols(dm, 1).astype(BF16)

    def over_rows(left, right):
        return lax.dot_general(
            beside([left(r) for r in range(rc)]), beside([right(r) for r in range(rc)]), NT,
            preferred_element_type=F32,
        )

    mids = [
        over_rows(
            lambda r: d2s[m, r + 1],
            lambda r: s1[m, r + 3 : r + 6, HID : 2 * HID].reshape(3 * HID, width),
        )
        for m in range(2)
    ]
    def put(start, value):
        for i in range(value.shape[0] // 8):
            side, row = place(start // 8 + i)
            partial[side, row : row + 8, :] = value[8 * i : 8 * i + 8]

    for a in range(3):
        put(a * 192, beside([mids[m][:, a * HID : (a + 1) * HID] for m in range(2)]))
    last = over_rows(lambda r: g3s[r + 1 : r + 4].reshape(96, width), lambda r: h2s[r + 3])
    for a in range(3):
        at_row = MID_ROWS + 24 * a
        put(at_row, last[32 * a : 32 * a + 24, :])

    def core_copy(which):
        start, size = ((0, split), (split, half - split))[which]
        return pltpu.make_async_remote_copy(
            src_ref=partial.at[1 - core, pl.ds(start, size)], dst_ref=theirs.at[pl.ds(start, size)],
            send_sem=cp_send.at[which], recv_sem=cp_recv.at[which],
            device_id=at(lat, partner, mem), device_id_type=MESH,
        )

    early = 8 * (EARLY - LOW_EARLY) // chunk
    split = early * chunk
    core_copy(0).start()

    def piece(ref, index):
        return ref.at[pl.ds(pl.multiple_of(index * chunk, chunk), chunk)]

    def reduce_rows(which):
        core_copy(which).wait()
        start, count = ((0, early), (early, owners - early))[which]
        span = slice(start * chunk, (start + count) * chunk)
        halved[span, :] = partial[core, span, :] + theirs[span, :]
        for i in range(count):
            to = start + lax.rem(rank + i, count)

            @pl.when(owner(to) != rank)
            def _(to=to):
                pltpu.make_async_remote_copy(
                    src_ref=piece(halved, to), dst_ref=scattered.at[rank],
                    send_sem=rs_send, recv_sem=rs_recv,
                    device_id=of_plane(owner(to)), device_id_type=MESH,
                ).start()

    d1s = []
    for m in range(2):
        products = [
            jnp.dot(w2t[m], d2s[m, x], preferred_element_type=F32) for x in range(rc + 2)
        ]
        own = []
        for r in range(rc):
            h = s1[m, r + 4, HID : 2 * HID].astype(F32)
            own.append((taps(products, r, (2, 1, 0)) * (1.0 - h * h)).astype(BF16))
        d1s.append(own)
        if m == 0:
            reduce_rows(0)
    first = over_rows(
        lambda r: s0[r + 4 : r + 7].reshape(96, width),
        lambda r: jnp.concatenate([d1s[0][r], d1s[1][r]], axis=0),
    )
    for a in range(3):
        at_row = MID_ROWS + SMALL_ROWS + 24 * a
        put(at_row, first[32 * a : 32 * a + 24, :])
    used = 8 * (EARLY - LOW_EARLY + SMALL_ROWS // 8 - LOW_LATE)
    if half > used:
        partial[1, used:, :] = jnp.zeros((half - used, 128), F32)
    core_copy(1).start()
    reduce_rows(1)

    for m in range(n_mem):
        for l in range(n_lon):
            @pl.when(elsewhere(l, m))
            def _(l=l, m=m):
                pltpu.make_async_copy(
                    pred_buf.at[:, :, pl.ds(0, cc)], force_rx.at[m, l], fr_sem.at[m, l]
                ).wait()

    force_own().wait()

    @pl.when(lat > 0)
    def _():
        pltpu.make_async_copy(row_send.at[0], row_rx.at[0], or_sem.at[0]).wait()

    @pl.when(lat < n_lat - 1)
    def _():
        pltpu.make_async_copy(row_send.at[0], row_rx.at[1], or_sem.at[1]).wait()

    pltpu.make_async_copy(col_send.at[0], col_rx.at[0], or_sem.at[2]).wait()
    pltpu.make_async_copy(col_send.at[0], col_rx.at[1], or_sem.at[3]).wait()

    summed = force_rx[0]
    for m in range(1, n_mem):
        summed = summed + force_rx[m]
    mean = (summed * (1.0 / (2 * n_mem))).reshape(LEV * 2 * rc, cc)
    for r in range(COARSE):
        tall[pl.ds(r, LEV * 2 * rc, stride=COARSE), :] = mean
    force_up[...] = jnp.dot(
        tall[...], expand, precision=lax.Precision.HIGHEST, preferred_element_type=F32
    ).reshape(force_up.shape)
    for q in range(3 * LEV):
        pad[q, 7:8, :] = row_rx[0, q : q + 1, :]
        pad[q, 8 + rows : 9 + rows, :] = row_rx[1, q : q + 1, :]

    loads[4].wait()
    lane_ids = lax.broadcasted_iota(jnp.int32, (8, cols), 1)
    for s in range(rows // 8):
        base = 8 + 8 * s
        ids = (lat * rows + 8 * s + lax.broadcasted_iota(jnp.int32, (8, cols), 0)).astype(F32)
        coriolis = jnp.sin(-math.pi / 2 + math.pi * (ids + 0.5) / (rows * n_lat))
        wet = 0.1 * land[8 * s : 8 * s + 8, :].astype(F32)
        sum_x = jnp.zeros((8, cols), F32)
        sum_y = jnp.zeros((8, cols), F32)
        for l in range(LEV):
            got = []
            for c in range(3):
                q = c * LEV + l
                centre = pad[q, base : base + 8, :]
                south = pad[q, base - 1 : base + 7, :]
                north = pad[q, base + 1 : base + 9, :]
                before = col_rx[0, 8 * s : 8 * s + 8, q : q + 1]
                after = col_rx[1, 8 * s : 8 * s + 8, q : q + 1]
                west = jnp.where(lane_ids == 0, before, shift_cols(centre, 1))
                east = jnp.where(lane_ids == cols - 1, after, shift_cols(centre, -1))
                got.append((centre, east, west, north, south))
            laps = [e + w + n + so - 4.0 * ce for ce, e, w, n, so in got]
            u, v, t = got[0][0], got[1][0], got[2][0]
            dx = got[2][1] - got[2][2]
            dy = got[2][3] - got[2][4]
            sum_x = sum_x + dx
            sum_y = sum_y + dy
            fu = force_up[l * 2, 8 * s : 8 * s + 8, :]
            fv = force_up[l * 2 + 1, 8 * s : 8 * s + 8, :]
            velo_new[0, l, 8 * s : 8 * s + 8, :] = u + wet * (
                coriolis * v + 0.25 * sum_x + 0.5 * laps[0] + fu
            )
            velo_new[1, l, 8 * s : 8 * s + 8, :] = v + wet * (
                -coriolis * u + 0.25 * sum_y + 0.5 * laps[1] + fv
            )
            temp_new[l, 8 * s : 8 * s + 8, :] = t + wet * (
                -0.5 * (u * dx + v * dy) + 0.3 * laps[2]
            )

    stores = [
        pltpu.make_async_copy(velo_new, velo_out, out_sem.at[0]),
        pltpu.make_async_copy(temp_new, temp_out, out_sem.at[1]),
    ]
    for store in stores:
        store.start()

    def passed(ref, count, sem):
        pltpu.make_async_copy(ref.at[pl.ds(0, count)], ref.at[pl.ds(0, count)], sem).wait()

    @pl.when(is_owner)
    def _():
        passed(scattered, plane - 1, rs_recv)
        start = pl.multiple_of(turn * chunk, chunk)
        total = halved[pl.ds(start, chunk), :]
        for i in range(1, plane):
            total = total + scattered[lax.rem(rank + i, plane)]
        gathered[core, pl.ds(start, chunk), :] = total
        for i in range(1, plane):
            pltpu.make_async_remote_copy(
                src_ref=piece(gathered.at[core], turn), dst_ref=piece(gathered.at[core], turn),
                send_sem=ag_send, recv_sem=ag_recv,
                device_id=of_plane(lax.rem(rank + i, plane)), device_id_type=MESH,
            ).start()

    @pl.when(is_owner)
    def _():
        passed(halved, (owners - 1) * chunk, ag_recv)

    @pl.when(jnp.logical_not(is_owner))
    def _():
        passed(halved, owners * chunk, ag_recv)

    share = pltpu.make_async_remote_copy(
        src_ref=gathered.at[core], dst_ref=gathered.at[core],
        send_sem=cp_send.at[2], recv_sem=cp_recv.at[2],
        device_id=at(lat, partner, mem), device_id_type=MESH,
    )
    share.start()
    keep = pltpu.make_async_copy(gathered.at[core], grads.at[core], out_sem.at[2])
    keep.start()

    for store in stores:
        store.wait()
    for l in range(n_lon):
        @pl.when(lat < n_lat - 1)
        def _(l=l):
            up_copy(l).wait_send()

        @pl.when(lat > 0)
        def _(l=l):
            down_copy(l).wait_send()

        @pl.when(lon != l)
        def _(l=l):
            own_copy(l).wait_send()

        for m in range(n_mem):
            @pl.when(elsewhere(l, m))
            def _(l=l, m=m):
                force_copy(l, m).wait_send()

    @pl.when(lat < n_lat - 1)
    def _():
        row_up().wait_send()

    @pl.when(lat > 0)
    def _():
        row_down().wait_send()

    col_east().wait_send()
    col_west().wait_send()

    @pl.when(is_owner)
    def _():
        passed(halved, (owners - 1) * chunk, rs_send)
        passed(scattered, plane - 1, ag_send)

    @pl.when(jnp.logical_not(is_owner))
    def _():
        passed(halved, owners * chunk, rs_send)

    share.wait()
    fetched = pltpu.make_async_copy(gathered.at[1 - core], grads.at[1 - core], out_sem.at[3])
    fetched.start()
    keep.wait()
    fetched.wait()


def finish(
    velo_in, temp_in, halves_in, velo_out, temp_out, first_out, middle_out, last_out,
    velo, temp, halves, first, middle, last, sems,
):
    load = pltpu.make_async_copy(halves_in, halves, sems.at[0])
    load.start()
    blocks = [(velo_in.at[c], velo.at[c], velo_out.at[c]) for c in range(2)]
    blocks.append((temp_in, temp, temp_out))
    moves = [pltpu.make_async_copy(b[0], b[1], sems.at[1 + i]) for i, b in enumerate(blocks)]
    for move in moves:
        move.start()
    load.wait()

    def rows_of(start, size, cols):
        side, row = place(start // 8)
        return halves[side, row + start % 8 : row + start % 8 + size, cols]

    stores = []
    for m in range(2):
        cols = slice(m * HID, (m + 1) * HID)
        for a in range(3):
            for b in range(3):
                k = 3 * a + b
                for i in range(HID // 8):
                    middle[m, k, 8 * i : 8 * i + 8] = rows_of(a * 192 + b * HID + 8 * i, 8, cols)
                at_row = MID_ROWS + (2 - a) * 24 + b * 8 + 4 + 2 * m
                last[m, k] = rows_of(at_row, 2, cols)
                for c in range(3):
                    at_row = MID_ROWS + SMALL_ROWS + a * 24 + b * 8 + c
                    first[k, c, m : m + 1, :] = rows_of(at_row, 1, cols)
        stores.append(pltpu.make_async_copy(middle.at[m], middle_out.at[m], sems.at[4 + m]))
        stores[-1].start()
    stores.append(pltpu.make_async_copy(first, first_out, sems.at[6]))
    stores.append(pltpu.make_async_copy(last, last_out, sems.at[7]))
    for store in stores[2:]:
        store.start()
    for i, (move, b) in enumerate(zip(moves, blocks)):
        move.wait()
        stores.append(pltpu.make_async_copy(b[1], b[2], sems.at[8 + i]))
        stores[-1].start()
    for store in stores:
        store.wait()


def per_device(n_lat, n_lon, n_mem, velo, temp, land, target, w_first, w_middle, w_last):
    rows, cols = temp.shape[1], temp.shape[2]
    rc, cc = rows // COARSE, cols // COARSE
    width = cc * n_lon
    plane = n_lat * (n_lon // 2)
    chunk, owners = chunking(plane)
    half = chunk * owners
    mine = w_first.shape[0]

    hbm = pl.BlockSpec(memory_space=pl.ANY)
    dma = pltpu.SemaphoreType.DMA
    fields = [jax.ShapeDtypeStruct(velo.shape, F32), jax.ShapeDtypeStruct(temp.shape, F32)]
    velo_next, temp_next, grads = pl.pallas_call(
        functools.partial(kernel, n_lat, n_lon, n_mem),
        out_shape=(*fields, jax.ShapeDtypeStruct((2, half, 128), F32)),
        in_specs=[hbm] * 7,
        out_specs=(hbm, hbm, hbm),
        scratch_shapes=[
            pltpu.VMEM(velo.shape, F32),
            pltpu.VMEM(temp.shape, F32),
            pltpu.VMEM(land.shape, jnp.int32),
            pltpu.VMEM(target.shape, BF16),
            pltpu.VMEM((9, 3, mine, HID), BF16),
            pltpu.VMEM(w_middle.shape, BF16),
            pltpu.VMEM(w_last.shape, BF16),
            pltpu.VMEM((LEV * rows, cc), F32),
            pltpu.VMEM((LEV * 2 * rows, cc), F32),
            pltpu.VMEM((LEV * rc * 8, cc), F32),
            pltpu.VMEM((LEV, rc, 8, cc), BF16),
            pltpu.VMEM((n_lon, rc + 2 * HALO, 8, cc), BF16),
            pltpu.VMEM((rc + 2 * HALO, 32, width), BF16),
            pltpu.VMEM((2, rc + 8, 3 * HID, width), BF16),
            pltpu.VMEM((rc + 6, 2 * HID, width), BF16),
            pltpu.VMEM((rc + 4, 32, width), BF16),
            pltpu.VMEM((2, rc + 2, 3 * HID, width), BF16),
            pltpu.VMEM((2, rc, width), F32),
            pltpu.VMEM((n_mem, n_lon, 2, rc, cc), F32),
            pltpu.VMEM((LEV * 2, rows, cols), F32),
            pltpu.VMEM((3 * LEV, rows + 16, cols), F32),
            pltpu.VMEM((2, 16, cols), F32),
            pltpu.VMEM((2, 16, cols), F32),
            pltpu.VMEM((2, rows, 128), F32),
            pltpu.VMEM((2, rows, 128), F32),
            pltpu.VMEM((96, 128), F32),
            pltpu.VMEM((72, 128), F32),
            pltpu.VMEM((2, half, 128), F32),
            pltpu.VMEM((half, 128), F32),
            pltpu.VMEM((half, 128), F32),
            pltpu.VMEM((plane, chunk, 128), F32),
            pltpu.VMEM((2, half, 128), F32),
            dma((8,)),
            dma((4,)),
            dma((3,)),
            dma((3,)),
            dma((3, n_lon)),
            dma((3, n_lon)),
            dma((4,)),
            dma((4,)),
            dma((n_mem, n_lon)),
            dma((n_mem, n_lon)),
            dma,
            dma,
            dma,
            dma,
            dma,
        ],
        compiler_params=pltpu.CompilerParams(
            collective_id=0, has_side_effects=True, vmem_limit_bytes=56 * 1024 * 1024
        ),
        name="ocean_step",
    )(velo, temp, land, target, jnp.transpose(w_first, (1, 3, 0, 2)), w_middle, w_last)
    velo_next, temp_next, first, middle, last = pl.pallas_call(
        finish,
        out_shape=(
            *fields,
            jax.ShapeDtypeStruct((9, 3, mine, HID), F32),
            jax.ShapeDtypeStruct(w_middle.shape, F32),
            jax.ShapeDtypeStruct(w_last.shape, F32),
        ),
        in_specs=[hbm] * 3,
        out_specs=(hbm,) * 5,
        scratch_shapes=[
            pltpu.VMEM(velo.shape, F32),
            pltpu.VMEM(temp.shape, F32),
            pltpu.VMEM((2, half, 128), F32),
            pltpu.VMEM((9, 3, mine, HID), F32),
            pltpu.VMEM(w_middle.shape, F32),
            pltpu.VMEM(w_last.shape, F32),
            dma((11,)),
        ],
        name="finish",
    )(velo_next, temp_next, grads)
    return (velo_next, temp_next, jnp.transpose(first, (2, 0, 3, 1)), middle, last)


def solution(mesh):
    return jax.shard_map(
        functools.partial(per_device, mesh.shape["lat"], mesh.shape["lon"], mesh.shape["mem"]),
        mesh=mesh,
        in_specs=(
            P(None, None, "lat", "lon"),
            P(None, "lat", "lon"),
            P("lat", "lon"),
            P(None, None, "lat", "lon"),
            P("mem", None, None, None),
            P("mem", None, None, None),
            P("mem", None, None, None),
        ),
        out_specs=(
            P(None, None, "lat", "lon"),
            P(None, "lat", "lon"),
            P("mem", None, None, None),
            P("mem", None, None, None),
            P("mem", None, None, None),
        ),
        check_vma=False,
    )
```

```python
import functools
import math

import jax
import jax.numpy as jnp
from jax import lax
from jax.experimental import pallas as pl
from jax.experimental.pallas import tpu as pltpu
from jax.sharding import PartitionSpec as P

LEV = 4
COARSE = 4
HID = 64
HALO = 5
MESH = pl.DeviceIdType.MESH
F32 = jnp.float32
BF16 = jnp.bfloat16
MID_ROWS = 9 * HID
SMALL_ROWS = 72
GRAD_ROWS = MID_ROWS + 2 * SMALL_ROWS
NT = (((1,), (1,)), ((), ()))


def chunking(n_lat, planes):
    tiles = -(-GRAD_ROWS // 16)
    owners = (n_lat // 4 * 3 if n_lat % 4 == 0 else n_lat) * planes
    return -(-tiles // owners) * 8, owners


EARLY = (MID_ROWS + SMALL_ROWS) // 8
LOW_EARLY, LOW_LATE = (EARLY + 1) // 2, (SMALL_ROWS // 8 + 1) // 2


def place(tile):
    if tile < EARLY:
        return divmod_half(tile, LOW_EARLY, 0, 0)
    return divmod_half(tile - EARLY, LOW_LATE, LOW_EARLY, EARLY - LOW_EARLY)


def divmod_half(tile, low, base_low, base_high):
    return (0, 8 * (base_low + tile)) if tile < low else (1, 8 * (base_high + tile - low))


def shift_cols(value, by):
    return pltpu.roll(value, by % value.shape[-1], axis=value.ndim - 1)


def kernel(
    n_lat, n_lon, n_mem,
    velo_in, temp_in, land_in, target_in, first_in, middle_in, last_in,
    velo_out, temp_out, grads,
    velo_new, temp_new, land, target, w_first, w_middle, w_last,
    narrow, tall, staged, send_buf, rx, s0, s1, h2s, g3s, d2s, pred_buf, force_rx, force_up, pad,
    row_send, row_rx, col_send, col_rx, w1_rows, wl_rows, partial, theirs, halved, scattered, gathered,
    in_sem, out_sem,
    cp_send, cp_recv, cs_sem, cr_sem, os_sem, or_sem, fs_sem, fr_sem, fl_sem, rs_send, rs_recv, ag_send, ag_recv,
):
    lat = lax.axis_index("lat")
    lon = lax.axis_index("lon")
    mem = lax.axis_index("mem")
    rows = temp_in.shape[1]
    cols = temp_in.shape[2]
    rc = rows // COARSE
    cc = cols // COARSE
    width = cc * n_lon
    nyc = rc * n_lat
    group = n_lat * n_lon
    planes = n_lon // 2
    plane = n_lat * planes
    chunk, owners = chunking(n_lat, planes)
    half = chunk * owners
    core = lax.rem(lon, 2)
    partner = lon + 1 - 2 * core
    me = lat * n_lon + lon
    place_z = lax.div(lon, 2)
    rank = lat * planes + place_z

    def owns(lat_of):
        return lax.rem(lat_of, 4) != 3 if n_lat % 4 == 0 else lat_of >= 0

    def turn_of(lat_of, z_of):
        return (lat_of - lax.div(lat_of, 4) if n_lat % 4 == 0 else lat_of) * planes + z_of

    turn = turn_of(lat, place_z)
    is_owner = owns(lat)

    def wrapped(value, size):
        return jnp.where(value >= size, value - size, value)

    def around(which):
        for i in list(range(1, n_lat)) + [0]:
            for k in range(planes):
                z = wrapped(place_z + (k + 1 if i == 0 else k), planes)
                if i > 0 or k < planes - 1:
                    which(wrapped(lat + i, n_lat), z)

    def at(lat_to, lon_to, mem_to):
        return {"lat": lat_to, "lon": lon_to, "mem": mem_to}

    def of_group(index):
        return at(index // n_lon, lax.rem(index, n_lon), mem)

    inner = pl.ds(8, rows)
    loads = [
        pltpu.make_async_copy(velo_in.at[c], pad.at[pl.ds(c * LEV, LEV), inner], in_sem.at[c])
        for c in range(2)
    ]
    loads.append(
        pltpu.make_async_copy(temp_in, pad.at[pl.ds(2 * LEV, LEV), inner], in_sem.at[2])
    )
    loads.append(pltpu.make_async_copy(target_in, target, in_sem.at[3]))
    loads.append(pltpu.make_async_copy(land_in, land, in_sem.at[4]))
    loads.append(pltpu.make_async_copy(first_in, w_first, in_sem.at[5]))
    loads.append(pltpu.make_async_copy(middle_in, w_middle, in_sem.at[6]))
    loads.append(pltpu.make_async_copy(last_in, w_last, in_sem.at[7]))
    for load in loads:
        load.start()

    def of_plane(lat_to, z_to):
        return at(lat_to, 2 * z_to + core, mem)

    barrier = pltpu.get_barrier_semaphore()

    def greet(i, carry):
        pl.semaphore_signal(
            barrier, inc=1, device_id=of_group(lax.rem(me + i, group)), device_id_type=MESH
        )
        return carry

    lax.fori_loop(1, group, greet, 0)
    for other in range(1, n_mem):
        for l in range(n_lon):
            pl.semaphore_signal(
                barrier, inc=1, device_id=at(lat, l, lax.rem(mem + other, n_mem)), device_id_type=MESH
            )

    q_ids = lax.broadcasted_iota(jnp.int32, (cc, cols), 0)
    i_ids = lax.broadcasted_iota(jnp.int32, (cc, cols), 1)
    expand = jnp.where(i_ids // COARSE == q_ids, 1.0, 0.0).astype(F32)

    for load in loads[:4]:
        load.wait()
    staged[...] = jnp.zeros_like(staged)
    for c in range(3):
        fine = pad[c * LEV : (c + 1) * LEV, 8 : 8 + rows, :].reshape(LEV * rows, cols)
        fine = fine * (1.0 / COARSE**2)
        high = fine.astype(BF16)
        rest = fine - high.astype(F32)
        middle = rest.astype(BF16)
        low = (rest - middle.astype(F32)).astype(BF16)
        parts = lax.dot_general(
            jnp.concatenate([high, middle, low], axis=0), expand.astype(BF16), NT,
            preferred_element_type=F32,
        )
        n = LEV * rows
        narrow[...] = parts[0:n] + parts[n : 2 * n] + parts[2 * n : 3 * n]
        pooled = narrow[pl.ds(0, LEV * rc, stride=COARSE), :]
        for r in range(1, COARSE):
            pooled = pooled + narrow[pl.ds(r, LEV * rc, stride=COARSE), :]
        staged[pl.ds(c, LEV * rc, stride=8), :] = pooled
    for c in range(2):
        goal = target[c].astype(F32).reshape(LEV * rc, cc)
        staged[pl.ds(4 + c, LEV * rc, stride=8), :] = goal
        staged[pl.ds(6 + c, LEV * rc, stride=8), :] = goal
    send_buf[...] = staged[...].astype(BF16).reshape(send_buf.shape)

    @pl.when(lat == 0)
    def _():
        rx[:, 0:HALO] = jnp.zeros((n_lon, HALO, 8, cc), BF16)
        row_rx[0] = jnp.zeros_like(row_rx[0])

    @pl.when(lat == n_lat - 1)
    def _():
        rx[:, HALO + rc : 2 * HALO + rc] = jnp.zeros((n_lon, HALO, 8, cc), BF16)
        row_rx[1] = jnp.zeros_like(row_rx[1])

    pl.semaphore_wait(barrier, group - 1 + (n_mem - 1) * n_lon)

    def own_copy(l):
        return pltpu.make_async_remote_copy(
            src_ref=send_buf.at[l], dst_ref=rx.at[lon, pl.ds(HALO, rc)],
            send_sem=cs_sem.at[0, l], recv_sem=cr_sem.at[0, lon],
            device_id=at(lat, l, mem), device_id_type=MESH,
        )

    def up_copy(l):
        return pltpu.make_async_remote_copy(
            src_ref=send_buf.at[l, pl.ds(rc - HALO, HALO)], dst_ref=rx.at[lon, pl.ds(0, HALO)],
            send_sem=cs_sem.at[1, l], recv_sem=cr_sem.at[1, lon],
            device_id=at(lat + 1, l, mem), device_id_type=MESH,
        )

    def down_copy(l):
        return pltpu.make_async_remote_copy(
            src_ref=send_buf.at[l, pl.ds(0, HALO)], dst_ref=rx.at[lon, pl.ds(HALO + rc, HALO)],
            send_sem=cs_sem.at[2, l], recv_sem=cr_sem.at[2, lon],
            device_id=at(lat - 1, l, mem), device_id_type=MESH,
        )

    def row_up():
        return pltpu.make_async_remote_copy(
            src_ref=row_send.at[1], dst_ref=row_rx.at[0], send_sem=os_sem.at[0], recv_sem=or_sem.at[0],
            device_id=at(lat + 1, lon, mem), device_id_type=MESH,
        )

    def row_down():
        return pltpu.make_async_remote_copy(
            src_ref=row_send.at[0], dst_ref=row_rx.at[1], send_sem=os_sem.at[1], recv_sem=or_sem.at[1],
            device_id=at(lat - 1, lon, mem), device_id_type=MESH,
        )

    def col_east():
        return pltpu.make_async_remote_copy(
            src_ref=col_send.at[1], dst_ref=col_rx.at[0], send_sem=os_sem.at[2], recv_sem=or_sem.at[2],
            device_id=at(lat, lax.rem(lon + 1, n_lon), mem), device_id_type=MESH,
        )

    def col_west():
        return pltpu.make_async_remote_copy(
            src_ref=col_send.at[0], dst_ref=col_rx.at[1], send_sem=os_sem.at[3], recv_sem=or_sem.at[3],
            device_id=at(lat, lax.rem(lon + n_lon - 1, n_lon), mem), device_id_type=MESH,
        )

    for l in range(n_lon):
        @pl.when(lat < n_lat - 1)
        def _(l=l):
            up_copy(l).start()

        @pl.when(lat > 0)
        def _(l=l):
            down_copy(l).start()

        @pl.when(lon != l)
        def _(l=l):
            own_copy(l).start()

    lane = lax.broadcasted_iota(jnp.int32, (rows, 128), 1)
    west_cols = jnp.zeros((rows, 128), F32)
    east_cols = jnp.zeros((rows, 128), F32)
    for q in range(3 * LEV):
        first = pad[q, 8 : 8 + rows, 0:128]
        last = pad[q, 8 : 8 + rows, cols - 128 : cols]
        west_cols = jnp.where(lane == q, jnp.broadcast_to(first[:, 0:1], (rows, 128)), west_cols)
        east_cols = jnp.where(lane == q, jnp.broadcast_to(last[:, 127:128], (rows, 128)), east_cols)
        row_send[0, q : q + 1, :] = pad[q, 8:9, :]
        row_send[1, q : q + 1, :] = pad[q, 7 + rows : 8 + rows, :]
    col_send[0] = west_cols
    col_send[1] = east_cols

    @pl.when(lat < n_lat - 1)
    def _():
        row_up().start()

    @pl.when(lat > 0)
    def _():
        row_down().start()

    col_east().start()
    col_west().start()

    rx[lon, HALO : HALO + rc] = send_buf[lon]
    def flip(matrix):
        size = matrix.shape[1]
        eye = jnp.where(
            lax.broadcasted_iota(jnp.int32, (size, size), 0)
            == lax.broadcasted_iota(jnp.int32, (size, size), 1),
            1.0, 0.0,
        ).astype(BF16)
        return lax.dot_general(eye, matrix, NT, preferred_element_type=F32).astype(BF16)

    def beside(blocks):
        return jnp.concatenate(blocks, axis=1)

    for load in loads[5:]:
        load.wait()
    w1_rows[...] = jnp.zeros_like(w1_rows)
    wl_rows[...] = jnp.zeros_like(wl_rows)
    for a in range(3):
        for b in range(3):
            k = 3 * a + b
            for c in range(3):
                pair = w_first[k, c].astype(F32)
                for m in range(2):
                    at_row = a * 32 + b * 8 + c
                    w1_rows[at_row : at_row + 1, m * HID : (m + 1) * HID] = pair[m : m + 1]
            for m in range(2):
                at_row = a * 24 + b * 8 + 4 + 2 * m
                wl_rows[at_row : at_row + 2, m * HID : (m + 1) * HID] = w_last[m, k].astype(F32)
    w1 = flip(w1_rows[...].astype(BF16))
    wl = wl_rows[...].astype(BF16)
    gap = jnp.zeros((8, 2 * HID), F32)
    w3 = jnp.concatenate([p for t in (2, 1, 0) for p in (wl_rows[24 * t : 24 * t + 24, :], gap)], axis=0)
    w3t = flip(w3.astype(BF16))
    w2 = [
        jnp.concatenate([beside([w_middle[m, 3 * a + b] for b in range(3)]) for a in range(3)], axis=0)
        for m in range(2)
    ]
    w2t = [
        flip(jnp.concatenate([beside([w_middle[m, 3 * a + b] for a in range(3)]) for b in range(3)], axis=0))
        for m in range(2)
    ]

    def arrived(kind, l, src, dst):
        pltpu.make_async_copy(src, dst, cr_sem.at[kind, l]).wait()

    for l in range(n_lon):
        @pl.when(lon != l)
        def _(l=l):
            arrived(0, l, send_buf.at[l], rx.at[l, pl.ds(HALO, rc)])

        @pl.when(lat > 0)
        def _(l=l):
            arrived(1, l, send_buf.at[l, pl.ds(0, HALO)], rx.at[l, pl.ds(0, HALO)])

        @pl.when(lat < n_lat - 1)
        def _(l=l):
            arrived(2, l, send_buf.at[l, pl.ds(0, HALO)], rx.at[l, pl.ds(HALO + rc, HALO)])

    def inside(g):
        return jnp.where(jnp.logical_and(g >= 0, g < nyc), 1.0, 0.0).astype(F32)

    def received(x):
        return jnp.concatenate([rx[l, x].astype(F32) for l in range(n_lon)], axis=-1)

    def three(v):
        return jnp.concatenate([shift_cols(v, 1), v, shift_cols(v, -1), jnp.zeros_like(v)], axis=0)

    for x in range(rc + 2 * HALO):
        s0[x] = three(received(x)).astype(BF16)

    for r in range(rc + 8):
        block = s0[r : r + 3].reshape(96, width)
        h = jnp.tanh(jnp.dot(w1, block, preferred_element_type=F32)) * inside(lat * rc - 4 + r)
        for m in range(2):
            hm = h[m * HID : (m + 1) * HID]
            s1[m, r, 0:HID] = shift_cols(hm, 1).astype(BF16)
            s1[m, r, HID : 2 * HID] = hm.astype(BF16)
            s1[m, r, 2 * HID : 3 * HID] = shift_cols(hm, -1).astype(BF16)

    def taps(products, r, order):
        return sum(
            products[r + i][j * HID : (j + 1) * HID] for i, j in enumerate(order)
        )

    for m in range(2):
        products = [
            jnp.dot(w2[m], s1[m, x], preferred_element_type=F32) for x in range(rc + 8)
        ]
        for r in range(rc + 6):
            h = jnp.tanh(taps(products, r, (0, 1, 2))) * inside(lat * rc - 3 + r)
            h2s[r, m * HID : (m + 1) * HID] = h.astype(BF16)

    scale = 2.0 / (2.0 * LEV * nyc * width)
    sub = lax.broadcasted_iota(jnp.int32, (8, width), 0)
    outs = [jnp.dot(wl, h2s[x], preferred_element_type=F32) for x in range(rc + 6)]
    for r in range(rc + 4):
        u = [sum(outs[r + a][24 * a + 8 * b : 24 * a + 8 * b + 8] for a in range(3)) for b in range(3)]
        pred = shift_cols(u[0], 1) + u[1] + shift_cols(u[2], -1)
        g3 = jnp.where(sub >= 4, (pred - received(r + 3)) * scale, 0.0) * inside(lat * rc - 2 + r)
        g3s[r] = jnp.concatenate(
            [shift_cols(g3, -1), g3, shift_cols(g3, 1), jnp.zeros_like(g3)], axis=0
        ).astype(BF16)
        if 2 <= r < 2 + rc:
            both = pred[4:6] + pred[6:8]
            for o in range(2):
                pred_buf[o, r - 2 : r - 1, :] = both[o : o + 1]

    def force_copy(l, m):
        return pltpu.make_async_remote_copy(
            src_ref=pred_buf.at[:, :, pl.ds(l * cc, cc)], dst_ref=force_rx.at[mem, lon],
            send_sem=fs_sem.at[m, l], recv_sem=fr_sem.at[mem, lon],
            device_id=at(lat, l, m), device_id_type=MESH,
        )

    def force_own():
        return pltpu.make_async_copy(
            pred_buf.at[:, :, pl.ds(pl.multiple_of(lon * cc, cc), cc)], force_rx.at[mem, lon], fl_sem
        )

    def elsewhere(l, m):
        return jnp.logical_or(lon != l, mem != m)

    for m in range(n_mem):
        for l in range(n_lon):
            @pl.when(elsewhere(l, m))
            def _(l=l, m=m):
                force_copy(l, m).start()

    force_own().start()

    for r in range(rc + 2):
        block = g3s[r : r + 3].reshape(96, width)
        h = h2s[r + 2].astype(F32)
        d = jnp.dot(w3t, block, preferred_element_type=F32) * (1.0 - h * h)
        d = d * inside(lat * rc - 1 + r)
        for m in range(2):
            dm = d[m * HID : (m + 1) * HID]
            d2s[m, r, 0:HID] = shift_cols(dm, -1).astype(BF16)
            d2s[m, r, HID : 2 * HID] = dm.astype(BF16)
            d2s[m, r, 2 * HID : 3 * HID] = shift_cols(dm, 1).astype(BF16)

    def over_rows(left, right):
        return lax.dot_general(
            beside([left(r) for r in range(rc)]), beside([right(r) for r in range(rc)]), NT,
            preferred_element_type=F32,
        )

    mids = [
        over_rows(
            lambda r: d2s[m, r + 1],
            lambda r: s1[m, r + 3 : r + 6, HID : 2 * HID].reshape(3 * HID, width),
        )
        for m in range(2)
    ]
    def put(start, value):
        for i in range(value.shape[0] // 8):
            side, row = place(start // 8 + i)
            partial[side, row : row + 8, :] = value[8 * i : 8 * i + 8]

    for a in range(3):
        put(a * 192, beside([mids[m][:, a * HID : (a + 1) * HID] for m in range(2)]))
    last = over_rows(lambda r: g3s[r + 1 : r + 4].reshape(96, width), lambda r: h2s[r + 3])
    for a in range(3):
        at_row = MID_ROWS + 24 * a
        put(at_row, last[32 * a : 32 * a + 24, :])

    def core_copy(which):
        start, size = ((0, split), (split, half - split))[which]
        return pltpu.make_async_remote_copy(
            src_ref=partial.at[1 - core, pl.ds(start, size)], dst_ref=theirs.at[pl.ds(start, size)],
            send_sem=cp_send.at[which], recv_sem=cp_recv.at[which],
            device_id=at(lat, partner, mem), device_id_type=MESH,
        )

    early = 8 * (EARLY - LOW_EARLY) // chunk
    split = early * chunk
    core_copy(0).start()

    def piece(ref, index):
        return ref.at[pl.ds(pl.multiple_of(index * chunk, chunk), chunk)]

    def reduce_rows(which):
        core_copy(which).wait()
        start, count = ((0, early), (early, owners - early))[which]
        span = slice(start * chunk, (start + count) * chunk)
        halved[span, :] = partial[core, span, :] + theirs[span, :]

        def send(lat_to, z_to):
            to = turn_of(lat_to, z_to)
            wanted = jnp.logical_and(to >= start, to < start + count)

            @pl.when(jnp.logical_and(owns(lat_to), wanted))
            def _():
                pltpu.make_async_remote_copy(
                    src_ref=piece(halved, to), dst_ref=scattered.at[rank],
                    send_sem=rs_send, recv_sem=rs_recv,
                    device_id=of_plane(lat_to, z_to), device_id_type=MESH,
                ).start()

        around(send)

    d1s = []
    for m in range(2):
        products = [
            jnp.dot(w2t[m], d2s[m, x], preferred_element_type=F32) for x in range(rc + 2)
        ]
        own = []
        for r in range(rc):
            h = s1[m, r + 4, HID : 2 * HID].astype(F32)
            own.append((taps(products, r, (2, 1, 0)) * (1.0 - h * h)).astype(BF16))
        d1s.append(own)
        if m == 0:
            reduce_rows(0)
    first = over_rows(
        lambda r: s0[r + 4 : r + 7].reshape(96, width),
        lambda r: jnp.concatenate([d1s[0][r], d1s[1][r]], axis=0),
    )
    for a in range(3):
        at_row = MID_ROWS + SMALL_ROWS + 24 * a
        put(at_row, first[32 * a : 32 * a + 24, :])
    used = 8 * (EARLY - LOW_EARLY + SMALL_ROWS // 8 - LOW_LATE)
    if half > used:
        partial[1, used:, :] = jnp.zeros((half - used, 128), F32)
    core_copy(1).start()
    reduce_rows(1)

    def passed(ref, count, sem):
        pltpu.make_async_copy(ref.at[pl.ds(0, count)], ref.at[pl.ds(0, count)], sem).wait()

    @pl.when(is_owner)
    def _():
        passed(scattered, plane - 1, rs_recv)
        start = pl.multiple_of(turn * chunk, chunk)
        total = halved[pl.ds(start, chunk), :]
        for i in range(1, plane):
            total = total + scattered[lax.rem(rank + i, plane)]
        gathered[core, pl.ds(start, chunk), :] = total

        def spread(lat_to, z_to, sem):
            pltpu.make_async_remote_copy(
                src_ref=piece(gathered.at[core], turn), dst_ref=piece(gathered.at[core], turn),
                send_sem=ag_send, recv_sem=ag_recv.at[sem],
                device_id=of_plane(lat_to, z_to), device_id_type=MESH,
            ).start()

        @pl.when(turn < early)
        def _():
            around(functools.partial(spread, sem=0))

        @pl.when(turn >= early)
        def _():
            around(functools.partial(spread, sem=1))

    for m in range(n_mem):
        for l in range(n_lon):
            @pl.when(elsewhere(l, m))
            def _(l=l, m=m):
                pltpu.make_async_copy(
                    pred_buf.at[:, :, pl.ds(0, cc)], force_rx.at[m, l], fr_sem.at[m, l]
                ).wait()

    force_own().wait()

    @pl.when(lat > 0)
    def _():
        pltpu.make_async_copy(row_send.at[0], row_rx.at[0], or_sem.at[0]).wait()

    @pl.when(lat < n_lat - 1)
    def _():
        pltpu.make_async_copy(row_send.at[0], row_rx.at[1], or_sem.at[1]).wait()

    pltpu.make_async_copy(col_send.at[0], col_rx.at[0], or_sem.at[2]).wait()
    pltpu.make_async_copy(col_send.at[0], col_rx.at[1], or_sem.at[3]).wait()

    summed = force_rx[0]
    for m in range(1, n_mem):
        summed = summed + force_rx[m]
    mean = (summed * (1.0 / (2 * n_mem))).reshape(LEV * 2 * rc, cc)
    for r in range(COARSE):
        tall[pl.ds(r, LEV * 2 * rc, stride=COARSE), :] = mean
    force_up[...] = jnp.dot(
        tall[...], expand, precision=lax.Precision.HIGHEST, preferred_element_type=F32
    ).reshape(force_up.shape)
    for q in range(3 * LEV):
        pad[q, 7:8, :] = row_rx[0, q : q + 1, :]
        pad[q, 8 + rows : 9 + rows, :] = row_rx[1, q : q + 1, :]

    loads[4].wait()
    lane_ids = lax.broadcasted_iota(jnp.int32, (8, cols), 1)
    for s in range(rows // 8):
        base = 8 + 8 * s
        ids = (lat * rows + 8 * s + lax.broadcasted_iota(jnp.int32, (8, cols), 0)).astype(F32)
        coriolis = jnp.sin(-math.pi / 2 + math.pi * (ids + 0.5) / (rows * n_lat))
        wet = 0.1 * land[8 * s : 8 * s + 8, :].astype(F32)
        sum_x = jnp.zeros((8, cols), F32)
        sum_y = jnp.zeros((8, cols), F32)
        for l in range(LEV):
            got = []
            for c in range(3):
                q = c * LEV + l
                centre = pad[q, base : base + 8, :]
                south = pad[q, base - 1 : base + 7, :]
                north = pad[q, base + 1 : base + 9, :]
                before = col_rx[0, 8 * s : 8 * s + 8, q : q + 1]
                after = col_rx[1, 8 * s : 8 * s + 8, q : q + 1]
                west = jnp.where(lane_ids == 0, before, shift_cols(centre, 1))
                east = jnp.where(lane_ids == cols - 1, after, shift_cols(centre, -1))
                got.append((centre, east, west, north, south))
            laps = [e + w + n + so - 4.0 * ce for ce, e, w, n, so in got]
            u, v, t = got[0][0], got[1][0], got[2][0]
            dx = got[2][1] - got[2][2]
            dy = got[2][3] - got[2][4]
            sum_x = sum_x + dx
            sum_y = sum_y + dy
            fu = force_up[l * 2, 8 * s : 8 * s + 8, :]
            fv = force_up[l * 2 + 1, 8 * s : 8 * s + 8, :]
            velo_new[0, l, 8 * s : 8 * s + 8, :] = u + wet * (
                coriolis * v + 0.25 * sum_x + 0.5 * laps[0] + fu
            )
            velo_new[1, l, 8 * s : 8 * s + 8, :] = v + wet * (
                -coriolis * u + 0.25 * sum_y + 0.5 * laps[1] + fv
            )
            temp_new[l, 8 * s : 8 * s + 8, :] = t + wet * (
                -0.5 * (u * dx + v * dy) + 0.3 * laps[2]
            )

    stores = [
        pltpu.make_async_copy(velo_new, velo_out, out_sem.at[0]),
        pltpu.make_async_copy(temp_new, temp_out, out_sem.at[1]),
    ]
    for store in stores:
        store.start()

    def share(which):
        start, count = ((0, early), (early, owners - early))[which]
        span = pl.ds(start * chunk, count * chunk)
        inside_it = jnp.logical_and(is_owner, jnp.logical_and(turn >= start, turn < start + count))
        if count > 1:
            @pl.when(inside_it)
            def _():
                passed(halved, (count - 1) * chunk, ag_recv.at[which])

        @pl.when(jnp.logical_not(inside_it))
        def _():
            passed(halved, count * chunk, ag_recv.at[which])

        copy = pltpu.make_async_remote_copy(
            src_ref=gathered.at[core, span], dst_ref=gathered.at[core, span],
            send_sem=cp_send.at[2 + which], recv_sem=cp_recv.at[2 + which],
            device_id=at(lat, partner, mem), device_id_type=MESH,
        )
        copy.start()
        return copy, span

    shares = [share(0), share(1)]
    keep = pltpu.make_async_copy(gathered.at[core], grads.at[core], out_sem.at[2])
    keep.start()

    for store in stores:
        store.wait()
    for l in range(n_lon):
        @pl.when(lat < n_lat - 1)
        def _(l=l):
            up_copy(l).wait_send()

        @pl.when(lat > 0)
        def _(l=l):
            down_copy(l).wait_send()

        @pl.when(lon != l)
        def _(l=l):
            own_copy(l).wait_send()

        for m in range(n_mem):
            @pl.when(elsewhere(l, m))
            def _(l=l, m=m):
                force_copy(l, m).wait_send()

    @pl.when(lat < n_lat - 1)
    def _():
        row_up().wait_send()

    @pl.when(lat > 0)
    def _():
        row_down().wait_send()

    col_east().wait_send()
    col_west().wait_send()

    @pl.when(is_owner)
    def _():
        passed(halved, (owners - 1) * chunk, rs_send)
        passed(scattered, plane - 1, ag_send)

    @pl.when(jnp.logical_not(is_owner))
    def _():
        passed(halved, owners * chunk, rs_send)

    fetched = []
    for which, (copy, span) in enumerate(shares):
        copy.wait()
        fetched.append(
            pltpu.make_async_copy(
                gathered.at[1 - core, span], grads.at[1 - core, span], out_sem.at[3 + which]
            )
        )
        fetched[-1].start()
    keep.wait()
    for fetch in fetched:
        fetch.wait()


def finish(
    velo_in, temp_in, halves_in, velo_out, temp_out, first_out, middle_out, last_out,
    velo, temp, halves, first, middle, last, sems,
):
    load = pltpu.make_async_copy(halves_in, halves, sems.at[0])
    load.start()
    blocks = [(velo_in.at[c], velo.at[c], velo_out.at[c]) for c in range(2)]
    blocks.append((temp_in, temp, temp_out))
    moves = [pltpu.make_async_copy(b[0], b[1], sems.at[1 + i]) for i, b in enumerate(blocks)]
    for move in moves:
        move.start()
    load.wait()

    def rows_of(start, size, cols):
        side, row = place(start // 8)
        return halves[side, row + start % 8 : row + start % 8 + size, cols]

    stores = []
    for m in range(2):
        cols = slice(m * HID, (m + 1) * HID)
        for a in range(3):
            for b in range(3):
                k = 3 * a + b
                for i in range(HID // 8):
                    middle[m, k, 8 * i : 8 * i + 8] = rows_of(a * 192 + b * HID + 8 * i, 8, cols)
                at_row = MID_ROWS + (2 - a) * 24 + b * 8 + 4 + 2 * m
                last[m, k] = rows_of(at_row, 2, cols)
                for c in range(3):
                    at_row = MID_ROWS + SMALL_ROWS + a * 24 + b * 8 + c
                    first[k, c, m : m + 1, :] = rows_of(at_row, 1, cols)
        stores.append(pltpu.make_async_copy(middle.at[m], middle_out.at[m], sems.at[4 + m]))
        stores[-1].start()
    stores.append(pltpu.make_async_copy(first, first_out, sems.at[6]))
    stores.append(pltpu.make_async_copy(last, last_out, sems.at[7]))
    for store in stores[2:]:
        store.start()
    for i, (move, b) in enumerate(zip(moves, blocks)):
        move.wait()
        stores.append(pltpu.make_async_copy(b[1], b[2], sems.at[8 + i]))
        stores[-1].start()
    for store in stores:
        store.wait()


def per_device(n_lat, n_lon, n_mem, velo, temp, land, target, w_first, w_middle, w_last):
    rows, cols = temp.shape[1], temp.shape[2]
    rc, cc = rows // COARSE, cols // COARSE
    width = cc * n_lon
    plane = n_lat * (n_lon // 2)
    chunk, owners = chunking(n_lat, n_lon // 2)
    half = chunk * owners
    mine = w_first.shape[0]

    hbm = pl.BlockSpec(memory_space=pl.ANY)
    dma = pltpu.SemaphoreType.DMA
    fields = [jax.ShapeDtypeStruct(velo.shape, F32), jax.ShapeDtypeStruct(temp.shape, F32)]
    velo_next, temp_next, grads = pl.pallas_call(
        functools.partial(kernel, n_lat, n_lon, n_mem),
        out_shape=(*fields, jax.ShapeDtypeStruct((2, half, 128), F32)),
        in_specs=[hbm] * 7,
        out_specs=(hbm, hbm, hbm),
        scratch_shapes=[
            pltpu.VMEM(velo.shape, F32),
            pltpu.VMEM(temp.shape, F32),
            pltpu.VMEM(land.shape, jnp.int32),
            pltpu.VMEM(target.shape, BF16),
            pltpu.VMEM((9, 3, mine, HID), BF16),
            pltpu.VMEM(w_middle.shape, BF16),
            pltpu.VMEM(w_last.shape, BF16),
            pltpu.VMEM((LEV * rows, cc), F32),
            pltpu.VMEM((LEV * 2 * rows, cc), F32),
            pltpu.VMEM((LEV * rc * 8, cc), F32),
            pltpu.VMEM((LEV, rc, 8, cc), BF16),
            pltpu.VMEM((n_lon, rc + 2 * HALO, 8, cc), BF16),
            pltpu.VMEM((rc + 2 * HALO, 32, width), BF16),
            pltpu.VMEM((2, rc + 8, 3 * HID, width), BF16),
            pltpu.VMEM((rc + 6, 2 * HID, width), BF16),
            pltpu.VMEM((rc + 4, 32, width), BF16),
            pltpu.VMEM((2, rc + 2, 3 * HID, width), BF16),
            pltpu.VMEM((2, rc, width), F32),
            pltpu.VMEM((n_mem, n_lon, 2, rc, cc), F32),
            pltpu.VMEM((LEV * 2, rows, cols), F32),
            pltpu.VMEM((3 * LEV, rows + 16, cols), F32),
            pltpu.VMEM((2, 16, cols), F32),
            pltpu.VMEM((2, 16, cols), F32),
            pltpu.VMEM((2, rows, 128), F32),
            pltpu.VMEM((2, rows, 128), F32),
            pltpu.VMEM((96, 128), F32),
            pltpu.VMEM((72, 128), F32),
            pltpu.VMEM((2, half, 128), F32),
            pltpu.VMEM((half, 128), F32),
            pltpu.VMEM((half, 128), F32),
            pltpu.VMEM((plane, chunk, 128), F32),
            pltpu.VMEM((2, half, 128), F32),
            dma((8,)),
            dma((5,)),
            dma((4,)),
            dma((4,)),
            dma((3, n_lon)),
            dma((3, n_lon)),
            dma((4,)),
            dma((4,)),
            dma((n_mem, n_lon)),
            dma((n_mem, n_lon)),
            dma,
            dma,
            dma,
            dma,
            dma((2,)),
        ],
        compiler_params=pltpu.CompilerParams(
            collective_id=0, has_side_effects=True, vmem_limit_bytes=56 * 1024 * 1024
        ),
        name="ocean_step",
    )(velo, temp, land, target, jnp.transpose(w_first, (1, 3, 0, 2)), w_middle, w_last)
    velo_next, temp_next, first, middle, last = pl.pallas_call(
        finish,
        out_shape=(
            *fields,
            jax.ShapeDtypeStruct((9, 3, mine, HID), F32),
            jax.ShapeDtypeStruct(w_middle.shape, F32),
            jax.ShapeDtypeStruct(w_last.shape, F32),
        ),
        in_specs=[hbm] * 3,
        out_specs=(hbm,) * 5,
        scratch_shapes=[
            pltpu.VMEM(velo.shape, F32),
            pltpu.VMEM(temp.shape, F32),
            pltpu.VMEM((2, half, 128), F32),
            pltpu.VMEM((9, 3, mine, HID), F32),
            pltpu.VMEM(w_middle.shape, F32),
            pltpu.VMEM(w_last.shape, F32),
            dma((11,)),
        ],
        name="finish",
    )(velo_next, temp_next, grads)
    return (velo_next, temp_next, jnp.transpose(first, (2, 0, 3, 1)), middle, last)


def solution(mesh):
    return jax.shard_map(
        functools.partial(per_device, mesh.shape["lat"], mesh.shape["lon"], mesh.shape["mem"]),
        mesh=mesh,
        in_specs=(
            P(None, None, "lat", "lon"),
            P(None, "lat", "lon"),
            P("lat", "lon"),
            P(None, None, "lat", "lon"),
            P("mem", None, None, None),
            P("mem", None, None, None),
            P("mem", None, None, None),
        ),
        out_specs=(
            P(None, None, "lat", "lon"),
            P(None, "lat", "lon"),
            P("mem", None, None, None),
            P("mem", None, None, None),
            P("mem", None, None, None),
        ),
        check_vma=False,
    )
```

```python
import functools
import math

import jax
import jax.numpy as jnp
from jax import lax
from jax.experimental import pallas as pl
from jax.experimental.pallas import tpu as pltpu
from jax.sharding import PartitionSpec as P

LEV = 4
COARSE = 4
HID = 64
HALO = 5
MESH = pl.DeviceIdType.MESH
F32 = jnp.float32
BF16 = jnp.bfloat16
MID_ROWS = 9 * HID
SMALL_ROWS = 72
GRAD_ROWS = MID_ROWS + 2 * SMALL_ROWS
NT = (((1,), (1,)), ((), ()))


def chunking(n_lat, planes):
    tiles = -(-GRAD_ROWS // 16)
    owners = (n_lat // 4 * 3 if n_lat % 4 == 0 else n_lat) * planes
    return -(-tiles // owners) * 8, owners


EARLY = (MID_ROWS + SMALL_ROWS) // 8
LOW_EARLY, LOW_LATE = (EARLY + 1) // 2, (SMALL_ROWS // 8 + 1) // 2


def place(tile):
    if tile < EARLY:
        return divmod_half(tile, LOW_EARLY, 0, 0)
    return divmod_half(tile - EARLY, LOW_LATE, LOW_EARLY, EARLY - LOW_EARLY)


def divmod_half(tile, low, base_low, base_high):
    return (0, 8 * (base_low + tile)) if tile < low else (1, 8 * (base_high + tile - low))


def shift_cols(value, by):
    return pltpu.roll(value, by % value.shape[-1], axis=value.ndim - 1)


def kernel(
    n_lat, n_lon, n_mem,
    velo_in, temp_in, land_in, target_in, first_in, middle_in, last_in,
    velo_out, temp_out, grads,
    velo_new, temp_new, land, target, w_first, w_middle, w_last,
    narrow, tall, staged, send_buf, rx, s0, s1, h2s, g3s, d2s, pred_buf, force_rx, force_up, pad,
    row_send, row_rx, col_send, col_rx, w1_rows, wl_rows, partial, theirs, halved, scattered, gathered,
    in_sem, out_sem,
    entered, cp_send, cp_recv, cs_sem, cr_sem, os_sem, or_sem, fs_sem, fr_sem, fl_sem, rs_send, rs_recv, ag_send, ag_recv,
):
    lat = lax.axis_index("lat")
    lon = lax.axis_index("lon")
    mem = lax.axis_index("mem")
    rows = temp_in.shape[1]
    cols = temp_in.shape[2]
    rc = rows // COARSE
    cc = cols // COARSE
    width = cc * n_lon
    nyc = rc * n_lat
    planes = n_lon // 2
    plane = n_lat * planes
    chunk, owners = chunking(n_lat, planes)
    half = chunk * owners
    core = lax.rem(lon, 2)
    partner = lon + 1 - 2 * core
    place_z = lax.div(lon, 2)
    rank = lat * planes + place_z

    def owns(lat_of):
        return lax.rem(lat_of, 4) != 3 if n_lat % 4 == 0 else lat_of >= 0

    def turn_of(lat_of, z_of):
        return (lat_of - lax.div(lat_of, 4) if n_lat % 4 == 0 else lat_of) * planes + z_of

    turn = turn_of(lat, place_z)
    is_owner = owns(lat)

    def wrapped(value, size):
        return jnp.where(value >= size, value - size, value)

    def around(which):
        for i in list(range(1, n_lat)) + [0]:
            for k in range(planes):
                z = wrapped(place_z + (k + 1 if i == 0 else k), planes)
                if i > 0 or k < planes - 1:
                    which(wrapped(lat + i, n_lat), z)

    def at(lat_to, lon_to, mem_to):
        return {"lat": lat_to, "lon": lon_to, "mem": mem_to}

    inner = pl.ds(8, rows)
    loads = [
        pltpu.make_async_copy(velo_in.at[c], pad.at[pl.ds(c * LEV, LEV), inner], in_sem.at[c])
        for c in range(2)
    ]
    loads.append(
        pltpu.make_async_copy(temp_in, pad.at[pl.ds(2 * LEV, LEV), inner], in_sem.at[2])
    )
    loads.append(pltpu.make_async_copy(target_in, target, in_sem.at[3]))
    loads.append(pltpu.make_async_copy(land_in, land, in_sem.at[4]))
    loads.append(pltpu.make_async_copy(first_in, w_first, in_sem.at[5]))
    loads.append(pltpu.make_async_copy(middle_in, w_middle, in_sem.at[6]))
    loads.append(pltpu.make_async_copy(last_in, w_last, in_sem.at[7]))
    for load in loads:
        load.start()

    def of_plane(lat_to, z_to):
        return at(lat_to, 2 * z_to + core, mem)

    barrier = pltpu.get_barrier_semaphore()

    def greet(device):
        pl.semaphore_signal(barrier, inc=1, device_id=device, device_id_type=MESH)

    line = 4 if n_lat % 4 == 0 else n_lat
    line_start = lax.div(lat, line) * line
    greeted = 0
    for i in range(line, n_lat, line):
        for z in range(planes):
            greet(of_plane(wrapped(lat + i, n_lat), z))
            greeted += 1
    for i in range(1, line):
        for z in range(planes):
            greet(of_plane(line_start + wrapped(lat - line_start + i, line), z))
            greeted += 1
    for i in range(1, n_lon):
        greet(at(lat, wrapped(lon + i, n_lon), mem))
        greeted += 1
    for i in range(1, n_mem):
        for l in range(n_lon):
            greet(at(lat, l, wrapped(mem + i, n_mem)))
            greeted += 1

    @pl.when(lat > 0)
    def _():
        for l in range(n_lon):
            greet(at(lat - 1, l, mem))

    @pl.when(lat < n_lat - 1)
    def _():
        for l in range(n_lon):
            greet(at(lat + 1, l, mem))

    greeted = greeted + jnp.where(lat > 0, n_lon, 0) + jnp.where(lat < n_lat - 1, n_lon, 0)

    q_ids = lax.broadcasted_iota(jnp.int32, (cc, cols), 0)
    i_ids = lax.broadcasted_iota(jnp.int32, (cc, cols), 1)
    expand = jnp.where(i_ids // COARSE == q_ids, 1.0, 0.0).astype(F32)

    staged[...] = jnp.zeros_like(staged)
    for c in range(3):
        loads[c].wait()
        fine = pad[c * LEV : (c + 1) * LEV, 8 : 8 + rows, :].reshape(LEV * rows, cols)
        fine = fine * (1.0 / COARSE**2)
        high = fine.astype(BF16)
        rest = fine - high.astype(F32)
        middle = rest.astype(BF16)
        low = (rest - middle.astype(F32)).astype(BF16)
        parts = lax.dot_general(
            jnp.concatenate([high, middle, low], axis=0), expand.astype(BF16), NT,
            preferred_element_type=F32,
        )
        n = LEV * rows
        narrow[...] = parts[0:n] + parts[n : 2 * n] + parts[2 * n : 3 * n]
        pooled = narrow[pl.ds(0, LEV * rc, stride=COARSE), :]
        for r in range(1, COARSE):
            pooled = pooled + narrow[pl.ds(r, LEV * rc, stride=COARSE), :]
        staged[pl.ds(c, LEV * rc, stride=8), :] = pooled
    loads[3].wait()
    for c in range(2):
        goal = target[c].astype(F32).reshape(LEV * rc, cc)
        staged[pl.ds(4 + c, LEV * rc, stride=8), :] = goal
        staged[pl.ds(6 + c, LEV * rc, stride=8), :] = goal
    send_buf[...] = staged[...].astype(BF16).reshape(send_buf.shape)

    @pl.when(lat == 0)
    def _():
        rx[:, 0:HALO] = jnp.zeros((n_lon, HALO, 8, cc), BF16)
        row_rx[0] = jnp.zeros_like(row_rx[0])

    @pl.when(lat == n_lat - 1)
    def _():
        rx[:, HALO + rc : 2 * HALO + rc] = jnp.zeros((n_lon, HALO, 8, cc), BF16)
        row_rx[1] = jnp.zeros_like(row_rx[1])

    pl.semaphore_wait(barrier, greeted)

    def own_copy(l):
        return pltpu.make_async_remote_copy(
            src_ref=send_buf.at[l], dst_ref=rx.at[lon, pl.ds(HALO, rc)],
            send_sem=cs_sem.at[0, l], recv_sem=cr_sem.at[0, lon],
            device_id=at(lat, l, mem), device_id_type=MESH,
        )

    def up_copy(l):
        return pltpu.make_async_remote_copy(
            src_ref=send_buf.at[l, pl.ds(rc - HALO, HALO)], dst_ref=rx.at[lon, pl.ds(0, HALO)],
            send_sem=cs_sem.at[1, l], recv_sem=cr_sem.at[1, lon],
            device_id=at(lat + 1, l, mem), device_id_type=MESH,
        )

    def down_copy(l):
        return pltpu.make_async_remote_copy(
            src_ref=send_buf.at[l, pl.ds(0, HALO)], dst_ref=rx.at[lon, pl.ds(HALO + rc, HALO)],
            send_sem=cs_sem.at[2, l], recv_sem=cr_sem.at[2, lon],
            device_id=at(lat - 1, l, mem), device_id_type=MESH,
        )

    def row_up():
        return pltpu.make_async_remote_copy(
            src_ref=row_send.at[1], dst_ref=row_rx.at[0], send_sem=os_sem.at[0], recv_sem=or_sem.at[0],
            device_id=at(lat + 1, lon, mem), device_id_type=MESH,
        )

    def row_down():
        return pltpu.make_async_remote_copy(
            src_ref=row_send.at[0], dst_ref=row_rx.at[1], send_sem=os_sem.at[1], recv_sem=or_sem.at[1],
            device_id=at(lat - 1, lon, mem), device_id_type=MESH,
        )

    def col_east():
        return pltpu.make_async_remote_copy(
            src_ref=col_send.at[1], dst_ref=col_rx.at[0], send_sem=os_sem.at[2], recv_sem=or_sem.at[2],
            device_id=at(lat, lax.rem(lon + 1, n_lon), mem), device_id_type=MESH,
        )

    def col_west():
        return pltpu.make_async_remote_copy(
            src_ref=col_send.at[0], dst_ref=col_rx.at[1], send_sem=os_sem.at[3], recv_sem=or_sem.at[3],
            device_id=at(lat, lax.rem(lon + n_lon - 1, n_lon), mem), device_id_type=MESH,
        )

    for l in range(n_lon):
        @pl.when(lat < n_lat - 1)
        def _(l=l):
            up_copy(l).start()

        @pl.when(lat > 0)
        def _(l=l):
            down_copy(l).start()

        @pl.when(lon != l)
        def _(l=l):
            own_copy(l).start()

    for i in range(1, line):
        pl.semaphore_signal(
            entered, inc=1,
            device_id=of_plane(line_start + wrapped(lat - line_start + i, line), place_z),
            device_id_type=MESH,
        )

    lane = lax.broadcasted_iota(jnp.int32, (rows, 128), 1)
    west_cols = jnp.zeros((rows, 128), F32)
    east_cols = jnp.zeros((rows, 128), F32)
    for q in range(3 * LEV):
        first = pad[q, 8 : 8 + rows, 0:128]
        last = pad[q, 8 : 8 + rows, cols - 128 : cols]
        west_cols = jnp.where(lane == q, jnp.broadcast_to(first[:, 0:1], (rows, 128)), west_cols)
        east_cols = jnp.where(lane == q, jnp.broadcast_to(last[:, 127:128], (rows, 128)), east_cols)
        row_send[0, q : q + 1, :] = pad[q, 8:9, :]
        row_send[1, q : q + 1, :] = pad[q, 7 + rows : 8 + rows, :]
    col_send[0] = west_cols
    col_send[1] = east_cols

    @pl.when(lat < n_lat - 1)
    def _():
        row_up().start()

    @pl.when(lat > 0)
    def _():
        row_down().start()

    col_east().start()
    col_west().start()

    rx[lon, HALO : HALO + rc] = send_buf[lon]
    def flip(matrix):
        size = matrix.shape[1]
        eye = jnp.where(
            lax.broadcasted_iota(jnp.int32, (size, size), 0)
            == lax.broadcasted_iota(jnp.int32, (size, size), 1),
            1.0, 0.0,
        ).astype(BF16)
        return lax.dot_general(eye, matrix, NT, preferred_element_type=F32).astype(BF16)

    def beside(blocks):
        return jnp.concatenate(blocks, axis=1)

    for load in loads[5:]:
        load.wait()
    w1_rows[...] = jnp.zeros_like(w1_rows)
    wl_rows[...] = jnp.zeros_like(wl_rows)
    for a in range(3):
        for b in range(3):
            k = 3 * a + b
            for c in range(3):
                pair = w_first[k, c].astype(F32)
                for m in range(2):
                    at_row = a * 32 + b * 8 + c
                    w1_rows[at_row : at_row + 1, m * HID : (m + 1) * HID] = pair[m : m + 1]
            for m in range(2):
                at_row = a * 24 + b * 8 + 4 + 2 * m
                wl_rows[at_row : at_row + 2, m * HID : (m + 1) * HID] = w_last[m, k].astype(F32)
    w1 = flip(w1_rows[...].astype(BF16))
    wl = wl_rows[...].astype(BF16)
    gap = jnp.zeros((8, 2 * HID), F32)
    w3 = jnp.concatenate([p for t in (2, 1, 0) for p in (wl_rows[24 * t : 24 * t + 24, :], gap)], axis=0)
    w3t = flip(w3.astype(BF16))
    w2 = [
        jnp.concatenate([beside([w_middle[m, 3 * a + b] for b in range(3)]) for a in range(3)], axis=0)
        for m in range(2)
    ]
    w2t = [
        flip(jnp.concatenate([beside([w_middle[m, 3 * a + b] for a in range(3)]) for b in range(3)], axis=0))
        for m in range(2)
    ]

    def arrived(kind, l, src, dst):
        pltpu.make_async_copy(src, dst, cr_sem.at[kind, l]).wait()

    for l in range(n_lon):
        @pl.when(lon != l)
        def _(l=l):
            arrived(0, l, send_buf.at[l], rx.at[l, pl.ds(HALO, rc)])

        @pl.when(lat > 0)
        def _(l=l):
            arrived(1, l, send_buf.at[l, pl.ds(0, HALO)], rx.at[l, pl.ds(0, HALO)])

        @pl.when(lat < n_lat - 1)
        def _(l=l):
            arrived(2, l, send_buf.at[l, pl.ds(0, HALO)], rx.at[l, pl.ds(HALO + rc, HALO)])

    def inside(g):
        return jnp.where(jnp.logical_and(g >= 0, g < nyc), 1.0, 0.0).astype(F32)

    def received(x):
        return jnp.concatenate([rx[l, x].astype(F32) for l in range(n_lon)], axis=-1)

    def three(v):
        return jnp.concatenate([shift_cols(v, 1), v, shift_cols(v, -1), jnp.zeros_like(v)], axis=0)

    for x in range(rc + 2 * HALO):
        s0[x] = three(received(x)).astype(BF16)

    for r in range(rc + 8):
        block = s0[r : r + 3].reshape(96, width)
        h = jnp.tanh(jnp.dot(w1, block, preferred_element_type=F32)) * inside(lat * rc - 4 + r)
        for m in range(2):
            hm = h[m * HID : (m + 1) * HID]
            s1[m, r, 0:HID] = shift_cols(hm, 1).astype(BF16)
            s1[m, r, HID : 2 * HID] = hm.astype(BF16)
            s1[m, r, 2 * HID : 3 * HID] = shift_cols(hm, -1).astype(BF16)

    def taps(products, r, order):
        return sum(
            products[r + i][j * HID : (j + 1) * HID] for i, j in enumerate(order)
        )

    for m in range(2):
        products = [
            jnp.dot(w2[m], s1[m, x], preferred_element_type=F32) for x in range(rc + 8)
        ]
        for r in range(rc + 6):
            h = jnp.tanh(taps(products, r, (0, 1, 2))) * inside(lat * rc - 3 + r)
            h2s[r, m * HID : (m + 1) * HID] = h.astype(BF16)

    scale = 2.0 / (2.0 * LEV * nyc * width)
    sub = lax.broadcasted_iota(jnp.int32, (8, width), 0)
    outs = [jnp.dot(wl, h2s[x], preferred_element_type=F32) for x in range(rc + 6)]
    for r in range(rc + 4):
        u = [sum(outs[r + a][24 * a + 8 * b : 24 * a + 8 * b + 8] for a in range(3)) for b in range(3)]
        pred = shift_cols(u[0], 1) + u[1] + shift_cols(u[2], -1)
        g3 = jnp.where(sub >= 4, (pred - received(r + 3)) * scale, 0.0) * inside(lat * rc - 2 + r)
        g3s[r] = jnp.concatenate(
            [shift_cols(g3, -1), g3, shift_cols(g3, 1), jnp.zeros_like(g3)], axis=0
        ).astype(BF16)
        if 2 <= r < 2 + rc:
            both = pred[4:6] + pred[6:8]
            for o in range(2):
                pred_buf[o, r - 2 : r - 1, :] = both[o : o + 1]

    def force_copy(l, m):
        return pltpu.make_async_remote_copy(
            src_ref=pred_buf.at[:, :, pl.ds(l * cc, cc)], dst_ref=force_rx.at[mem, lon],
            send_sem=fs_sem.at[m, l], recv_sem=fr_sem.at[mem, lon],
            device_id=at(lat, l, m), device_id_type=MESH,
        )

    def force_own():
        return pltpu.make_async_copy(
            pred_buf.at[:, :, pl.ds(pl.multiple_of(lon * cc, cc), cc)], force_rx.at[mem, lon], fl_sem
        )

    def elsewhere(l, m):
        return jnp.logical_or(lon != l, mem != m)

    for m in range(n_mem):
        for l in range(n_lon):
            @pl.when(elsewhere(l, m))
            def _(l=l, m=m):
                force_copy(l, m).start()

    force_own().start()

    for r in range(rc + 2):
        block = g3s[r : r + 3].reshape(96, width)
        h = h2s[r + 2].astype(F32)
        d = jnp.dot(w3t, block, preferred_element_type=F32) * (1.0 - h * h)
        d = d * inside(lat * rc - 1 + r)
        for m in range(2):
            dm = d[m * HID : (m + 1) * HID]
            d2s[m, r, 0:HID] = shift_cols(dm, -1).astype(BF16)
            d2s[m, r, HID : 2 * HID] = dm.astype(BF16)
            d2s[m, r, 2 * HID : 3 * HID] = shift_cols(dm, 1).astype(BF16)

    def over_rows(left, right):
        return lax.dot_general(
            beside([left(r) for r in range(rc)]), beside([right(r) for r in range(rc)]), NT,
            preferred_element_type=F32,
        )

    mids = [
        over_rows(
            lambda r: d2s[m, r + 1],
            lambda r: s1[m, r + 3 : r + 6, HID : 2 * HID].reshape(3 * HID, width),
        )
        for m in range(2)
    ]
    def put(start, value):
        for i in range(value.shape[0] // 8):
            side, row = place(start // 8 + i)
            partial[side, row : row + 8, :] = value[8 * i : 8 * i + 8]

    for a in range(3):
        put(a * 192, beside([mids[m][:, a * HID : (a + 1) * HID] for m in range(2)]))
    last = over_rows(lambda r: g3s[r + 1 : r + 4].reshape(96, width), lambda r: h2s[r + 3])
    for a in range(3):
        at_row = MID_ROWS + 24 * a
        put(at_row, last[32 * a : 32 * a + 24, :])

    def core_copy(which):
        start, size = ((0, split), (split, half - split))[which]
        return pltpu.make_async_remote_copy(
            src_ref=partial.at[1 - core, pl.ds(start, size)], dst_ref=theirs.at[pl.ds(start, size)],
            send_sem=cp_send.at[which], recv_sem=cp_recv.at[which],
            device_id=at(lat, partner, mem), device_id_type=MESH,
        )

    early = 8 * (EARLY - LOW_EARLY) // chunk
    split = early * chunk
    core_copy(0).start()
    if line > 1:
        pl.semaphore_wait(entered, line - 1)

    def piece(ref, index):
        return ref.at[pl.ds(pl.multiple_of(index * chunk, chunk), chunk)]

    def reduce_rows(which):
        core_copy(which).wait()
        start, count = ((0, early), (early, owners - early))[which]
        span = slice(start * chunk, (start + count) * chunk)
        halved[span, :] = partial[core, span, :] + theirs[span, :]

        def send(lat_to, z_to):
            to = turn_of(lat_to, z_to)
            wanted = jnp.logical_and(to >= start, to < start + count)

            @pl.when(jnp.logical_and(owns(lat_to), wanted))
            def _():
                pltpu.make_async_remote_copy(
                    src_ref=piece(halved, to), dst_ref=scattered.at[rank],
                    send_sem=rs_send, recv_sem=rs_recv,
                    device_id=of_plane(lat_to, z_to), device_id_type=MESH,
                ).start()

        around(send)

    d1s = []
    for m in range(2):
        products = [
            jnp.dot(w2t[m], d2s[m, x], preferred_element_type=F32) for x in range(rc + 2)
        ]
        own = []
        for r in range(rc):
            h = s1[m, r + 4, HID : 2 * HID].astype(F32)
            own.append((taps(products, r, (2, 1, 0)) * (1.0 - h * h)).astype(BF16))
        d1s.append(own)
        if m == 0:
            reduce_rows(0)
    first = over_rows(
        lambda r: s0[r + 4 : r + 7].reshape(96, width),
        lambda r: jnp.concatenate([d1s[0][r], d1s[1][r]], axis=0),
    )
    for a in range(3):
        at_row = MID_ROWS + SMALL_ROWS + 24 * a
        put(at_row, first[32 * a : 32 * a + 24, :])
    used = 8 * (EARLY - LOW_EARLY + SMALL_ROWS // 8 - LOW_LATE)
    if half > used:
        partial[1, used:, :] = jnp.zeros((half - used, 128), F32)
    core_copy(1).start()
    reduce_rows(1)

    def passed(ref, count, sem):
        pltpu.make_async_copy(ref.at[pl.ds(0, count)], ref.at[pl.ds(0, count)], sem).wait()

    @pl.when(is_owner)
    def _():
        passed(scattered, plane - 1, rs_recv)
        start = pl.multiple_of(turn * chunk, chunk)
        total = halved[pl.ds(start, chunk), :]
        for i in range(1, plane):
            total = total + scattered[lax.rem(rank + i, plane)]
        gathered[core, pl.ds(start, chunk), :] = total

        def spread(lat_to, z_to, sem):
            pltpu.make_async_remote_copy(
                src_ref=piece(gathered.at[core], turn), dst_ref=piece(gathered.at[core], turn),
                send_sem=ag_send, recv_sem=ag_recv.at[sem],
                device_id=of_plane(lat_to, z_to), device_id_type=MESH,
            ).start()

        @pl.when(turn < early)
        def _():
            around(functools.partial(spread, sem=0))

        @pl.when(turn >= early)
        def _():
            around(functools.partial(spread, sem=1))

    for m in range(n_mem):
        for l in range(n_lon):
            @pl.when(elsewhere(l, m))
            def _(l=l, m=m):
                pltpu.make_async_copy(
                    pred_buf.at[:, :, pl.ds(0, cc)], force_rx.at[m, l], fr_sem.at[m, l]
                ).wait()

    force_own().wait()

    @pl.when(lat > 0)
    def _():
        pltpu.make_async_copy(row_send.at[0], row_rx.at[0], or_sem.at[0]).wait()

    @pl.when(lat < n_lat - 1)
    def _():
        pltpu.make_async_copy(row_send.at[0], row_rx.at[1], or_sem.at[1]).wait()

    pltpu.make_async_copy(col_send.at[0], col_rx.at[0], or_sem.at[2]).wait()
    pltpu.make_async_copy(col_send.at[0], col_rx.at[1], or_sem.at[3]).wait()

    summed = force_rx[0]
    for m in range(1, n_mem):
        summed = summed + force_rx[m]
    mean = (summed * (1.0 / (2 * n_mem))).reshape(LEV * 2 * rc, cc)
    for r in range(COARSE):
        tall[pl.ds(r, LEV * 2 * rc, stride=COARSE), :] = mean
    force_up[...] = jnp.dot(
        tall[...], expand, precision=lax.Precision.HIGHEST, preferred_element_type=F32
    ).reshape(force_up.shape)
    for q in range(3 * LEV):
        pad[q, 7:8, :] = row_rx[0, q : q + 1, :]
        pad[q, 8 + rows : 9 + rows, :] = row_rx[1, q : q + 1, :]

    loads[4].wait()
    lane_ids = lax.broadcasted_iota(jnp.int32, (8, cols), 1)
    for s in range(rows // 8):
        base = 8 + 8 * s
        ids = (lat * rows + 8 * s + lax.broadcasted_iota(jnp.int32, (8, cols), 0)).astype(F32)
        coriolis = jnp.sin(-math.pi / 2 + math.pi * (ids + 0.5) / (rows * n_lat))
        wet = 0.1 * land[8 * s : 8 * s + 8, :].astype(F32)
        sum_x = jnp.zeros((8, cols), F32)
        sum_y = jnp.zeros((8, cols), F32)
        for l in range(LEV):
            got = []
            for c in range(3):
                q = c * LEV + l
                centre = pad[q, base : base + 8, :]
                south = pad[q, base - 1 : base + 7, :]
                north = pad[q, base + 1 : base + 9, :]
                before = col_rx[0, 8 * s : 8 * s + 8, q : q + 1]
                after = col_rx[1, 8 * s : 8 * s + 8, q : q + 1]
                west = jnp.where(lane_ids == 0, before, shift_cols(centre, 1))
                east = jnp.where(lane_ids == cols - 1, after, shift_cols(centre, -1))
                got.append((centre, east, west, north, south))
            laps = [e + w + n + so - 4.0 * ce for ce, e, w, n, so in got]
            u, v, t = got[0][0], got[1][0], got[2][0]
            dx = got[2][1] - got[2][2]
            dy = got[2][3] - got[2][4]
            sum_x = sum_x + dx
            sum_y = sum_y + dy
            fu = force_up[l * 2, 8 * s : 8 * s + 8, :]
            fv = force_up[l * 2 + 1, 8 * s : 8 * s + 8, :]
            velo_new[0, l, 8 * s : 8 * s + 8, :] = u + wet * (
                coriolis * v + 0.25 * sum_x + 0.5 * laps[0] + fu
            )
            velo_new[1, l, 8 * s : 8 * s + 8, :] = v + wet * (
                -coriolis * u + 0.25 * sum_y + 0.5 * laps[1] + fv
            )
            temp_new[l, 8 * s : 8 * s + 8, :] = t + wet * (
                -0.5 * (u * dx + v * dy) + 0.3 * laps[2]
            )

    stores = [
        pltpu.make_async_copy(velo_new, velo_out, out_sem.at[0]),
        pltpu.make_async_copy(temp_new, temp_out, out_sem.at[1]),
    ]
    for store in stores:
        store.start()

    def share(which):
        start, count = ((0, early), (early, owners - early))[which]
        span = pl.ds(start * chunk, count * chunk)
        inside_it = jnp.logical_and(is_owner, jnp.logical_and(turn >= start, turn < start + count))
        if count > 1:
            @pl.when(inside_it)
            def _():
                passed(halved, (count - 1) * chunk, ag_recv.at[which])

        @pl.when(jnp.logical_not(inside_it))
        def _():
            passed(halved, count * chunk, ag_recv.at[which])

        copy = pltpu.make_async_remote_copy(
            src_ref=gathered.at[core, span], dst_ref=gathered.at[core, span],
            send_sem=cp_send.at[2 + which], recv_sem=cp_recv.at[2 + which],
            device_id=at(lat, partner, mem), device_id_type=MESH,
        )
        copy.start()
        return copy, span

    shares = [share(0), share(1)]
    keep = pltpu.make_async_copy(gathered.at[core], grads.at[core], out_sem.at[2])
    keep.start()

    for store in stores:
        store.wait()
    for l in range(n_lon):
        @pl.when(lat < n_lat - 1)
        def _(l=l):
            up_copy(l).wait_send()

        @pl.when(lat > 0)
        def _(l=l):
            down_copy(l).wait_send()

        @pl.when(lon != l)
        def _(l=l):
            own_copy(l).wait_send()

        for m in range(n_mem):
            @pl.when(elsewhere(l, m))
            def _(l=l, m=m):
                force_copy(l, m).wait_send()

    @pl.when(lat < n_lat - 1)
    def _():
        row_up().wait_send()

    @pl.when(lat > 0)
    def _():
        row_down().wait_send()

    col_east().wait_send()
    col_west().wait_send()

    @pl.when(is_owner)
    def _():
        passed(halved, (owners - 1) * chunk, rs_send)
        passed(scattered, plane - 1, ag_send)

    @pl.when(jnp.logical_not(is_owner))
    def _():
        passed(halved, owners * chunk, rs_send)

    fetched = []
    for which, (copy, span) in enumerate(shares):
        copy.wait()
        fetched.append(
            pltpu.make_async_copy(
                gathered.at[1 - core, span], grads.at[1 - core, span], out_sem.at[3 + which]
            )
        )
        fetched[-1].start()
    keep.wait()
    for fetch in fetched:
        fetch.wait()


def finish(
    velo_in, temp_in, halves_in, velo_out, temp_out, first_out, middle_out, last_out,
    velo, temp, halves, first, middle, last, sems,
):
    load = pltpu.make_async_copy(halves_in, halves, sems.at[0])
    load.start()
    blocks = [(velo_in.at[c], velo.at[c], velo_out.at[c]) for c in range(2)]
    blocks.append((temp_in, temp, temp_out))
    moves = [pltpu.make_async_copy(b[0], b[1], sems.at[1 + i]) for i, b in enumerate(blocks)]
    for move in moves:
        move.start()
    load.wait()

    def rows_of(start, size, cols):
        side, row = place(start // 8)
        return halves[side, row + start % 8 : row + start % 8 + size, cols]

    stores = []
    for m in range(2):
        cols = slice(m * HID, (m + 1) * HID)
        for a in range(3):
            for b in range(3):
                k = 3 * a + b
                for i in range(HID // 8):
                    middle[m, k, 8 * i : 8 * i + 8] = rows_of(a * 192 + b * HID + 8 * i, 8, cols)
                at_row = MID_ROWS + (2 - a) * 24 + b * 8 + 4 + 2 * m
                last[m, k] = rows_of(at_row, 2, cols)
                for c in range(3):
                    at_row = MID_ROWS + SMALL_ROWS + a * 24 + b * 8 + c
                    first[k, c, m : m + 1, :] = rows_of(at_row, 1, cols)
        stores.append(pltpu.make_async_copy(middle.at[m], middle_out.at[m], sems.at[4 + m]))
        stores[-1].start()
    stores.append(pltpu.make_async_copy(first, first_out, sems.at[6]))
    stores.append(pltpu.make_async_copy(last, last_out, sems.at[7]))
    for store in stores[2:]:
        store.start()
    for i, (move, b) in enumerate(zip(moves, blocks)):
        move.wait()
        stores.append(pltpu.make_async_copy(b[1], b[2], sems.at[8 + i]))
        stores[-1].start()
    for store in stores:
        store.wait()


def per_device(n_lat, n_lon, n_mem, velo, temp, land, target, w_first, w_middle, w_last):
    rows, cols = temp.shape[1], temp.shape[2]
    rc, cc = rows // COARSE, cols // COARSE
    width = cc * n_lon
    plane = n_lat * (n_lon // 2)
    chunk, owners = chunking(n_lat, n_lon // 2)
    half = chunk * owners
    mine = w_first.shape[0]

    hbm = pl.BlockSpec(memory_space=pl.ANY)
    dma = pltpu.SemaphoreType.DMA
    fields = [jax.ShapeDtypeStruct(velo.shape, F32), jax.ShapeDtypeStruct(temp.shape, F32)]
    velo_next, temp_next, grads = pl.pallas_call(
        functools.partial(kernel, n_lat, n_lon, n_mem),
        out_shape=(*fields, jax.ShapeDtypeStruct((2, half, 128), F32)),
        in_specs=[hbm] * 7,
        out_specs=(hbm, hbm, hbm),
        scratch_shapes=[
            pltpu.VMEM(velo.shape, F32),
            pltpu.VMEM(temp.shape, F32),
            pltpu.VMEM(land.shape, jnp.int32),
            pltpu.VMEM(target.shape, BF16),
            pltpu.VMEM((9, 3, mine, HID), BF16),
            pltpu.VMEM(w_middle.shape, BF16),
            pltpu.VMEM(w_last.shape, BF16),
            pltpu.VMEM((LEV * rows, cc), F32),
            pltpu.VMEM((LEV * 2 * rows, cc), F32),
            pltpu.VMEM((LEV * rc * 8, cc), F32),
            pltpu.VMEM((LEV, rc, 8, cc), BF16),
            pltpu.VMEM((n_lon, rc + 2 * HALO, 8, cc), BF16),
            pltpu.VMEM((rc + 2 * HALO, 32, width), BF16),
            pltpu.VMEM((2, rc + 8, 3 * HID, width), BF16),
            pltpu.VMEM((rc + 6, 2 * HID, width), BF16),
            pltpu.VMEM((rc + 4, 32, width), BF16),
            pltpu.VMEM((2, rc + 2, 3 * HID, width), BF16),
            pltpu.VMEM((2, rc, width), F32),
            pltpu.VMEM((n_mem, n_lon, 2, rc, cc), F32),
            pltpu.VMEM((LEV * 2, rows, cols), F32),
            pltpu.VMEM((3 * LEV, rows + 16, cols), F32),
            pltpu.VMEM((2, 16, cols), F32),
            pltpu.VMEM((2, 16, cols), F32),
            pltpu.VMEM((2, rows, 128), F32),
            pltpu.VMEM((2, rows, 128), F32),
            pltpu.VMEM((96, 128), F32),
            pltpu.VMEM((72, 128), F32),
            pltpu.VMEM((2, half, 128), F32),
            pltpu.VMEM((half, 128), F32),
            pltpu.VMEM((half, 128), F32),
            pltpu.VMEM((plane, chunk, 128), F32),
            pltpu.VMEM((2, half, 128), F32),
            dma((8,)),
            dma((5,)),
            pltpu.SemaphoreType.REGULAR,
            dma((4,)),
            dma((4,)),
            dma((3, n_lon)),
            dma((3, n_lon)),
            dma((4,)),
            dma((4,)),
            dma((n_mem, n_lon)),
            dma((n_mem, n_lon)),
            dma,
            dma,
            dma,
            dma,
            dma((2,)),
        ],
        compiler_params=pltpu.CompilerParams(
            collective_id=0, has_side_effects=True, vmem_limit_bytes=56 * 1024 * 1024
        ),
        name="ocean_step",
    )(velo, temp, land, target, jnp.transpose(w_first, (1, 3, 0, 2)), w_middle, w_last)
    velo_next, temp_next, first, middle, last = pl.pallas_call(
        finish,
        out_shape=(
            *fields,
            jax.ShapeDtypeStruct((9, 3, mine, HID), F32),
            jax.ShapeDtypeStruct(w_middle.shape, F32),
            jax.ShapeDtypeStruct(w_last.shape, F32),
        ),
        in_specs=[hbm] * 3,
        out_specs=(hbm,) * 5,
        scratch_shapes=[
            pltpu.VMEM(velo.shape, F32),
            pltpu.VMEM(temp.shape, F32),
            pltpu.VMEM((2, half, 128), F32),
            pltpu.VMEM((9, 3, mine, HID), F32),
            pltpu.VMEM(w_middle.shape, F32),
            pltpu.VMEM(w_last.shape, F32),
            dma((11,)),
        ],
        name="finish",
    )(velo_next, temp_next, grads)
    return (velo_next, temp_next, jnp.transpose(first, (2, 0, 3, 1)), middle, last)


def solution(mesh):
    return jax.shard_map(
        functools.partial(per_device, mesh.shape["lat"], mesh.shape["lon"], mesh.shape["mem"]),
        mesh=mesh,
        in_specs=(
            P(None, None, "lat", "lon"),
            P(None, "lat", "lon"),
            P("lat", "lon"),
            P(None, None, "lat", "lon"),
            P("mem", None, None, None),
            P("mem", None, None, None),
            P("mem", None, None, None),
        ),
        out_specs=(
            P(None, None, "lat", "lon"),
            P(None, "lat", "lon"),
            P("mem", None, None, None),
            P("mem", None, None, None),
            P("mem", None, None, None),
        ),
        check_vma=False,
    )
```

```python
import functools
import math

import jax
import jax.numpy as jnp
from jax import lax
from jax.experimental import pallas as pl
from jax.experimental.pallas import tpu as pltpu
from jax.sharding import PartitionSpec as P

LEV = 4
COARSE = 4
HID = 64
HALO = 5
MESH = pl.DeviceIdType.MESH
F32 = jnp.float32
BF16 = jnp.bfloat16
MID_ROWS = 9 * HID
SMALL_ROWS = 72
GRAD_ROWS = MID_ROWS + 2 * SMALL_ROWS
NT = (((1,), (1,)), ((), ()))


def chunking(n_lat, planes):
    tiles = -(-GRAD_ROWS // 16)
    owners = (n_lat // 4 * 3 if n_lat % 4 == 0 else n_lat) * planes
    return -(-tiles // owners) * 8, owners


EARLY = (MID_ROWS + SMALL_ROWS) // 8
LOW_EARLY, LOW_LATE = (EARLY + 1) // 2, (SMALL_ROWS // 8 + 1) // 2


def place(tile):
    if tile < EARLY:
        return divmod_half(tile, LOW_EARLY, 0, 0)
    return divmod_half(tile - EARLY, LOW_LATE, LOW_EARLY, EARLY - LOW_EARLY)


def divmod_half(tile, low, base_low, base_high):
    return (0, 8 * (base_low + tile)) if tile < low else (1, 8 * (base_high + tile - low))


def shift_cols(value, by):
    return pltpu.roll(value, by % value.shape[-1], axis=value.ndim - 1)


def kernel(
    n_lat, n_lon, n_mem,
    velo_in, temp_in, land_in, target_in, first_in, middle_in, last_in,
    velo_out, temp_out, grads,
    velo_new, temp_new, land, target, w_first, w_middle, w_last,
    narrow, tall, staged, send_buf, rx, s0, s1, h2s, g3s, d2s, pred_buf, force_rx, force_up, pad,
    row_send, row_rx, col_send, col_rx, w1_rows, wl_rows, partial, theirs, halved, scattered, gathered,
    in_sem, out_sem,
    entered, cp_send, cp_recv, cs_sem, cr_sem, os_sem, or_sem, fs_sem, fr_sem, fl_sem, rs_send, rs_recv, ag_send, ag_recv,
):
    lat = lax.axis_index("lat")
    lon = lax.axis_index("lon")
    mem = lax.axis_index("mem")
    rows = temp_in.shape[1]
    cols = temp_in.shape[2]
    rc = rows // COARSE
    cc = cols // COARSE
    width = cc * n_lon
    nyc = rc * n_lat
    planes = n_lon // 2
    plane = n_lat * planes
    chunk, owners = chunking(n_lat, planes)
    half = chunk * owners
    core = lax.rem(lon, 2)
    partner = lon + 1 - 2 * core
    place_z = lax.div(lon, 2)
    rank = lat * planes + place_z

    def owns(lat_of):
        return lax.rem(lat_of, 4) != 3 if n_lat % 4 == 0 else lat_of >= 0

    def turn_of(lat_of, z_of):
        return (lat_of - lax.div(lat_of, 4) if n_lat % 4 == 0 else lat_of) * planes + z_of

    turn = turn_of(lat, place_z)
    is_owner = owns(lat)

    def wrapped(value, size):
        return jnp.where(value >= size, value - size, value)

    def around(which):
        for i in list(range(1, n_lat)) + [0]:
            for k in range(planes):
                z = wrapped(place_z + (k + 1 if i == 0 else k), planes)
                if i > 0 or k < planes - 1:
                    which(wrapped(lat + i, n_lat), z)

    def at(lat_to, lon_to, mem_to):
        return {"lat": lat_to, "lon": lon_to, "mem": mem_to}

    inner = pl.ds(8, rows)
    loads = [
        pltpu.make_async_copy(velo_in.at[c], pad.at[pl.ds(c * LEV, LEV), inner], in_sem.at[c])
        for c in range(2)
    ]
    loads.append(
        pltpu.make_async_copy(temp_in, pad.at[pl.ds(2 * LEV, LEV), inner], in_sem.at[2])
    )
    loads.append(pltpu.make_async_copy(target_in, target, in_sem.at[3]))
    loads.append(pltpu.make_async_copy(land_in, land, in_sem.at[4]))
    loads.append(pltpu.make_async_copy(first_in, w_first, in_sem.at[5]))
    loads.append(pltpu.make_async_copy(middle_in, w_middle, in_sem.at[6]))
    loads.append(pltpu.make_async_copy(last_in, w_last, in_sem.at[7]))
    for load in loads:
        load.start()

    def of_plane(lat_to, z_to):
        return at(lat_to, 2 * z_to + core, mem)

    barrier = pltpu.get_barrier_semaphore()

    def greet(device):
        pl.semaphore_signal(barrier, inc=1, device_id=device, device_id_type=MESH)

    line = 4 if n_lat % 4 == 0 else n_lat
    line_start = lax.div(lat, line) * line
    greeted = 0
    for i in range(line, n_lat, line):
        for l in range(n_lon):
            greet(at(wrapped(lat + i, n_lat), l, mem))
            greeted += 1
    for i in range(1, line):
        for l in range(n_lon):
            greet(at(line_start + wrapped(lat - line_start + i, line), l, mem))
            greeted += 1
    for i in range(1, n_lon):
        greet(at(lat, wrapped(lon + i, n_lon), mem))
        greeted += 1
    for i in range(1, n_mem):
        for l in range(n_lon):
            greet(at(lat, l, wrapped(mem + i, n_mem)))
            greeted += 1

    @pl.when(lat > 0)
    def _():
        for l in range(n_lon):
            greet(at(lat - 1, l, mem))

    @pl.when(lat < n_lat - 1)
    def _():
        for l in range(n_lon):
            greet(at(lat + 1, l, mem))

    greeted = greeted + jnp.where(lat > 0, n_lon, 0) + jnp.where(lat < n_lat - 1, n_lon, 0)

    q_ids = lax.broadcasted_iota(jnp.int32, (cc, cols), 0)
    i_ids = lax.broadcasted_iota(jnp.int32, (cc, cols), 1)
    expand = jnp.where(i_ids // COARSE == q_ids, 1.0, 0.0).astype(F32)

    staged[...] = jnp.zeros_like(staged)
    for c in range(3):
        loads[c].wait()
        fine = pad[c * LEV : (c + 1) * LEV, 8 : 8 + rows, :].reshape(LEV * rows, cols)
        fine = fine * (1.0 / COARSE**2)
        high = fine.astype(BF16)
        rest = fine - high.astype(F32)
        middle = rest.astype(BF16)
        low = (rest - middle.astype(F32)).astype(BF16)
        parts = lax.dot_general(
            jnp.concatenate([high, middle, low], axis=0), expand.astype(BF16), NT,
            preferred_element_type=F32,
        )
        n = LEV * rows
        narrow[...] = parts[0:n] + parts[n : 2 * n] + parts[2 * n : 3 * n]
        pooled = narrow[pl.ds(0, LEV * rc, stride=COARSE), :]
        for r in range(1, COARSE):
            pooled = pooled + narrow[pl.ds(r, LEV * rc, stride=COARSE), :]
        staged[pl.ds(c, LEV * rc, stride=8), :] = pooled
    loads[3].wait()
    for c in range(2):
        goal = target[c].astype(F32).reshape(LEV * rc, cc)
        staged[pl.ds(4 + c, LEV * rc, stride=8), :] = goal
        staged[pl.ds(6 + c, LEV * rc, stride=8), :] = goal
    send_buf[...] = staged[...].astype(BF16).reshape(send_buf.shape)

    @pl.when(lat == 0)
    def _():
        rx[:, 0:HALO] = jnp.zeros((n_lon, HALO, 8, cc), BF16)
        row_rx[0] = jnp.zeros_like(row_rx[0])

    @pl.when(lat == n_lat - 1)
    def _():
        rx[:, HALO + rc : 2 * HALO + rc] = jnp.zeros((n_lon, HALO, 8, cc), BF16)
        row_rx[1] = jnp.zeros_like(row_rx[1])

    pl.semaphore_wait(barrier, greeted)

    def own_copy(l):
        return pltpu.make_async_remote_copy(
            src_ref=send_buf.at[l], dst_ref=rx.at[lon, pl.ds(HALO, rc)],
            send_sem=cs_sem.at[0, l], recv_sem=cr_sem.at[0, lon],
            device_id=at(lat, l, mem), device_id_type=MESH,
        )

    def up_copy(l):
        return pltpu.make_async_remote_copy(
            src_ref=send_buf.at[l, pl.ds(rc - HALO, HALO)], dst_ref=rx.at[lon, pl.ds(0, HALO)],
            send_sem=cs_sem.at[1, l], recv_sem=cr_sem.at[1, lon],
            device_id=at(lat + 1, l, mem), device_id_type=MESH,
        )

    def down_copy(l):
        return pltpu.make_async_remote_copy(
            src_ref=send_buf.at[l, pl.ds(0, HALO)], dst_ref=rx.at[lon, pl.ds(HALO + rc, HALO)],
            send_sem=cs_sem.at[2, l], recv_sem=cr_sem.at[2, lon],
            device_id=at(lat - 1, l, mem), device_id_type=MESH,
        )

    def row_up():
        return pltpu.make_async_remote_copy(
            src_ref=row_send.at[1], dst_ref=row_rx.at[0], send_sem=os_sem.at[0], recv_sem=or_sem.at[0],
            device_id=at(lat + 1, lon, mem), device_id_type=MESH,
        )

    def row_down():
        return pltpu.make_async_remote_copy(
            src_ref=row_send.at[0], dst_ref=row_rx.at[1], send_sem=os_sem.at[1], recv_sem=or_sem.at[1],
            device_id=at(lat - 1, lon, mem), device_id_type=MESH,
        )

    def col_east():
        return pltpu.make_async_remote_copy(
            src_ref=col_send.at[1], dst_ref=col_rx.at[0], send_sem=os_sem.at[2], recv_sem=or_sem.at[2],
            device_id=at(lat, lax.rem(lon + 1, n_lon), mem), device_id_type=MESH,
        )

    def col_west():
        return pltpu.make_async_remote_copy(
            src_ref=col_send.at[0], dst_ref=col_rx.at[1], send_sem=os_sem.at[3], recv_sem=or_sem.at[3],
            device_id=at(lat, lax.rem(lon + n_lon - 1, n_lon), mem), device_id_type=MESH,
        )

    for l in range(n_lon):
        @pl.when(lat < n_lat - 1)
        def _(l=l):
            up_copy(l).start()

        @pl.when(lat > 0)
        def _(l=l):
            down_copy(l).start()

        @pl.when(lon != l)
        def _(l=l):
            own_copy(l).start()

    for i in range(1, line):
        pl.semaphore_signal(
            entered, inc=1,
            device_id=of_plane(line_start + wrapped(lat - line_start + i, line), place_z),
            device_id_type=MESH,
        )

    lane = lax.broadcasted_iota(jnp.int32, (rows, 128), 1)
    west_cols = jnp.zeros((rows, 128), F32)
    east_cols = jnp.zeros((rows, 128), F32)
    for q in range(3 * LEV):
        first = pad[q, 8 : 8 + rows, 0:128]
        last = pad[q, 8 : 8 + rows, cols - 128 : cols]
        west_cols = jnp.where(lane == q, jnp.broadcast_to(first[:, 0:1], (rows, 128)), west_cols)
        east_cols = jnp.where(lane == q, jnp.broadcast_to(last[:, 127:128], (rows, 128)), east_cols)
        row_send[0, q : q + 1, :] = pad[q, 8:9, :]
        row_send[1, q : q + 1, :] = pad[q, 7 + rows : 8 + rows, :]
    col_send[0] = west_cols
    col_send[1] = east_cols

    @pl.when(lat < n_lat - 1)
    def _():
        row_up().start()

    @pl.when(lat > 0)
    def _():
        row_down().start()

    col_east().start()
    col_west().start()

    rx[lon, HALO : HALO + rc] = send_buf[lon]
    def flip(matrix):
        size = matrix.shape[1]
        eye = jnp.where(
            lax.broadcasted_iota(jnp.int32, (size, size), 0)
            == lax.broadcasted_iota(jnp.int32, (size, size), 1),
            1.0, 0.0,
        ).astype(BF16)
        return lax.dot_general(eye, matrix, NT, preferred_element_type=F32).astype(BF16)

    def beside(blocks):
        return jnp.concatenate(blocks, axis=1)

    for load in loads[5:]:
        load.wait()
    w1_rows[...] = jnp.zeros_like(w1_rows)
    wl_rows[...] = jnp.zeros_like(wl_rows)
    for a in range(3):
        for b in range(3):
            k = 3 * a + b
            for c in range(3):
                pair = w_first[k, c].astype(F32)
                for m in range(2):
                    at_row = a * 32 + b * 8 + c
                    w1_rows[at_row : at_row + 1, m * HID : (m + 1) * HID] = pair[m : m + 1]
            for m in range(2):
                at_row = a * 24 + b * 8 + 4 + 2 * m
                wl_rows[at_row : at_row + 2, m * HID : (m + 1) * HID] = w_last[m, k].astype(F32)
    w1 = flip(w1_rows[...].astype(BF16))
    wl = wl_rows[...].astype(BF16)
    gap = jnp.zeros((8, 2 * HID), F32)
    w3 = jnp.concatenate([p for t in (2, 1, 0) for p in (wl_rows[24 * t : 24 * t + 24, :], gap)], axis=0)
    w3t = flip(w3.astype(BF16))
    w2 = [
        jnp.concatenate([beside([w_middle[m, 3 * a + b] for b in range(3)]) for a in range(3)], axis=0)
        for m in range(2)
    ]
    w2t = [
        flip(jnp.concatenate([beside([w_middle[m, 3 * a + b] for a in range(3)]) for b in range(3)], axis=0))
        for m in range(2)
    ]

    def arrived(kind, l, src, dst):
        pltpu.make_async_copy(src, dst, cr_sem.at[kind, l]).wait()

    for l in range(n_lon):
        @pl.when(lon != l)
        def _(l=l):
            arrived(0, l, send_buf.at[l], rx.at[l, pl.ds(HALO, rc)])

        @pl.when(lat > 0)
        def _(l=l):
            arrived(1, l, send_buf.at[l, pl.ds(0, HALO)], rx.at[l, pl.ds(0, HALO)])

        @pl.when(lat < n_lat - 1)
        def _(l=l):
            arrived(2, l, send_buf.at[l, pl.ds(0, HALO)], rx.at[l, pl.ds(HALO + rc, HALO)])

    def inside(g):
        return jnp.where(jnp.logical_and(g >= 0, g < nyc), 1.0, 0.0).astype(F32)

    def received(x):
        return jnp.concatenate([rx[l, x].astype(F32) for l in range(n_lon)], axis=-1)

    def three(v):
        return jnp.concatenate([shift_cols(v, 1), v, shift_cols(v, -1), jnp.zeros_like(v)], axis=0)

    for x in range(rc + 2 * HALO):
        s0[x] = three(received(x)).astype(BF16)

    for r in range(rc + 8):
        block = s0[r : r + 3].reshape(96, width)
        h = jnp.tanh(jnp.dot(w1, block, preferred_element_type=F32)) * inside(lat * rc - 4 + r)
        for m in range(2):
            hm = h[m * HID : (m + 1) * HID]
            s1[m, r, 0:HID] = shift_cols(hm, 1).astype(BF16)
            s1[m, r, HID : 2 * HID] = hm.astype(BF16)
            s1[m, r, 2 * HID : 3 * HID] = shift_cols(hm, -1).astype(BF16)

    def taps(products, r, order):
        return sum(
            products[r + i][j * HID : (j + 1) * HID] for i, j in enumerate(order)
        )

    for m in range(2):
        products = [
            jnp.dot(w2[m], s1[m, x], preferred_element_type=F32) for x in range(rc + 8)
        ]
        for r in range(rc + 6):
            h = jnp.tanh(taps(products, r, (0, 1, 2))) * inside(lat * rc - 3 + r)
            h2s[r, m * HID : (m + 1) * HID] = h.astype(BF16)

    scale = 2.0 / (2.0 * LEV * nyc * width)
    sub = lax.broadcasted_iota(jnp.int32, (8, width), 0)
    outs = [jnp.dot(wl, h2s[x], preferred_element_type=F32) for x in range(rc + 6)]
    for r in range(rc + 4):
        u = [sum(outs[r + a][24 * a + 8 * b : 24 * a + 8 * b + 8] for a in range(3)) for b in range(3)]
        pred = shift_cols(u[0], 1) + u[1] + shift_cols(u[2], -1)
        g3 = jnp.where(sub >= 4, (pred - received(r + 3)) * scale, 0.0) * inside(lat * rc - 2 + r)
        g3s[r] = jnp.concatenate(
            [shift_cols(g3, -1), g3, shift_cols(g3, 1), jnp.zeros_like(g3)], axis=0
        ).astype(BF16)
        if 2 <= r < 2 + rc:
            both = pred[4:6] + pred[6:8]
            for o in range(2):
                pred_buf[o, r - 2 : r - 1, :] = both[o : o + 1]

    def force_copy(l, m):
        return pltpu.make_async_remote_copy(
            src_ref=pred_buf.at[:, :, pl.ds(l * cc, cc)], dst_ref=force_rx.at[mem, lon],
            send_sem=fs_sem.at[m, l], recv_sem=fr_sem.at[mem, lon],
            device_id=at(lat, l, m), device_id_type=MESH,
        )

    def force_own():
        return pltpu.make_async_copy(
            pred_buf.at[:, :, pl.ds(pl.multiple_of(lon * cc, cc), cc)], force_rx.at[mem, lon], fl_sem
        )

    def elsewhere(l, m):
        return jnp.logical_or(lon != l, mem != m)

    for m in range(n_mem):
        for l in range(n_lon):
            @pl.when(elsewhere(l, m))
            def _(l=l, m=m):
                force_copy(l, m).start()

    force_own().start()

    for r in range(rc + 2):
        block = g3s[r : r + 3].reshape(96, width)
        h = h2s[r + 2].astype(F32)
        d = jnp.dot(w3t, block, preferred_element_type=F32) * (1.0 - h * h)
        d = d * inside(lat * rc - 1 + r)
        for m in range(2):
            dm = d[m * HID : (m + 1) * HID]
            d2s[m, r, 0:HID] = shift_cols(dm, -1).astype(BF16)
            d2s[m, r, HID : 2 * HID] = dm.astype(BF16)
            d2s[m, r, 2 * HID : 3 * HID] = shift_cols(dm, 1).astype(BF16)

    def over_rows(left, right):
        return lax.dot_general(
            beside([left(r) for r in range(rc)]), beside([right(r) for r in range(rc)]), NT,
            preferred_element_type=F32,
        )

    mids = [
        over_rows(
            lambda r: d2s[m, r + 1],
            lambda r: s1[m, r + 3 : r + 6, HID : 2 * HID].reshape(3 * HID, width),
        )
        for m in range(2)
    ]
    def put(start, value):
        for i in range(value.shape[0] // 8):
            side, row = place(start // 8 + i)
            partial[side, row : row + 8, :] = value[8 * i : 8 * i + 8]

    for a in range(3):
        put(a * 192, beside([mids[m][:, a * HID : (a + 1) * HID] for m in range(2)]))
    last = over_rows(lambda r: g3s[r + 1 : r + 4].reshape(96, width), lambda r: h2s[r + 3])
    for a in range(3):
        at_row = MID_ROWS + 24 * a
        put(at_row, last[32 * a : 32 * a + 24, :])

    def core_copy(which):
        start, size = ((0, split), (split, half - split))[which]
        return pltpu.make_async_remote_copy(
            src_ref=partial.at[1 - core, pl.ds(start, size)], dst_ref=theirs.at[pl.ds(start, size)],
            send_sem=cp_send.at[which], recv_sem=cp_recv.at[which],
            device_id=at(lat, partner, mem), device_id_type=MESH,
        )

    early = 8 * (EARLY - LOW_EARLY) // chunk
    split = early * chunk
    core_copy(0).start()
    if line > 1:
        pl.semaphore_wait(entered, line - 1)

    def piece(ref, index):
        return ref.at[pl.ds(pl.multiple_of(index * chunk, chunk), chunk)]

    def reduce_rows(which):
        core_copy(which).wait()
        start, count = ((0, early), (early, owners - early))[which]
        span = slice(start * chunk, (start + count) * chunk)
        halved[span, :] = partial[core, span, :] + theirs[span, :]

        def send(lat_to, z_to):
            to = turn_of(lat_to, z_to)
            wanted = jnp.logical_and(to >= start, to < start + count)

            @pl.when(jnp.logical_and(owns(lat_to), wanted))
            def _():
                pltpu.make_async_remote_copy(
                    src_ref=piece(halved, to), dst_ref=scattered.at[rank],
                    send_sem=rs_send, recv_sem=rs_recv,
                    device_id=of_plane(lat_to, z_to), device_id_type=MESH,
                ).start()

        around(send)

    d1s = []
    for m in range(2):
        products = [
            jnp.dot(w2t[m], d2s[m, x], preferred_element_type=F32) for x in range(rc + 2)
        ]
        own = []
        for r in range(rc):
            h = s1[m, r + 4, HID : 2 * HID].astype(F32)
            own.append((taps(products, r, (2, 1, 0)) * (1.0 - h * h)).astype(BF16))
        d1s.append(own)
        if m == 0:
            reduce_rows(0)
    first = over_rows(
        lambda r: s0[r + 4 : r + 7].reshape(96, width),
        lambda r: jnp.concatenate([d1s[0][r], d1s[1][r]], axis=0),
    )
    for a in range(3):
        at_row = MID_ROWS + SMALL_ROWS + 24 * a
        put(at_row, first[32 * a : 32 * a + 24, :])
    used = 8 * (EARLY - LOW_EARLY + SMALL_ROWS // 8 - LOW_LATE)
    if half > used:
        partial[1, used:, :] = jnp.zeros((half - used, 128), F32)
    core_copy(1).start()
    reduce_rows(1)

    def passed(ref, count, sem):
        pltpu.make_async_copy(ref.at[pl.ds(0, count)], ref.at[pl.ds(0, count)], sem).wait()

    @pl.when(is_owner)
    def _():
        passed(scattered, plane - 1, rs_recv)
        start = pl.multiple_of(turn * chunk, chunk)
        total = halved[pl.ds(start, chunk), :]
        for i in range(1, plane):
            total = total + scattered[lax.rem(rank + i, plane)]
        gathered[core, pl.ds(start, chunk), :] = total

        def spread(lat_to, z_to, far=1):
            for side in range(1 - far, 2):
                pltpu.make_async_remote_copy(
                    src_ref=piece(gathered.at[core], turn), dst_ref=piece(gathered.at[core], turn),
                    send_sem=ag_send.at[side], recv_sem=ag_recv.at[side],
                    device_id=at(lat_to, 2 * z_to + (core if side == 0 else 1 - core), mem),
                    device_id_type=MESH,
                ).start()

        around(spread)
        spread(lat, place_z, far=0)

    for m in range(n_mem):
        for l in range(n_lon):
            @pl.when(elsewhere(l, m))
            def _(l=l, m=m):
                pltpu.make_async_copy(
                    pred_buf.at[:, :, pl.ds(0, cc)], force_rx.at[m, l], fr_sem.at[m, l]
                ).wait()

    force_own().wait()

    @pl.when(lat > 0)
    def _():
        pltpu.make_async_copy(row_send.at[0], row_rx.at[0], or_sem.at[0]).wait()

    @pl.when(lat < n_lat - 1)
    def _():
        pltpu.make_async_copy(row_send.at[0], row_rx.at[1], or_sem.at[1]).wait()

    pltpu.make_async_copy(col_send.at[0], col_rx.at[0], or_sem.at[2]).wait()
    pltpu.make_async_copy(col_send.at[0], col_rx.at[1], or_sem.at[3]).wait()

    summed = force_rx[0]
    for m in range(1, n_mem):
        summed = summed + force_rx[m]
    mean = (summed * (1.0 / (2 * n_mem))).reshape(LEV * 2 * rc, cc)
    for r in range(COARSE):
        tall[pl.ds(r, LEV * 2 * rc, stride=COARSE), :] = mean
    force_up[...] = jnp.dot(
        tall[...], expand, precision=lax.Precision.HIGHEST, preferred_element_type=F32
    ).reshape(force_up.shape)
    for q in range(3 * LEV):
        pad[q, 7:8, :] = row_rx[0, q : q + 1, :]
        pad[q, 8 + rows : 9 + rows, :] = row_rx[1, q : q + 1, :]

    loads[4].wait()
    lane_ids = lax.broadcasted_iota(jnp.int32, (8, cols), 1)
    for s in range(rows // 8):
        base = 8 + 8 * s
        ids = (lat * rows + 8 * s + lax.broadcasted_iota(jnp.int32, (8, cols), 0)).astype(F32)
        coriolis = jnp.sin(-math.pi / 2 + math.pi * (ids + 0.5) / (rows * n_lat))
        wet = 0.1 * land[8 * s : 8 * s + 8, :].astype(F32)
        sum_x = jnp.zeros((8, cols), F32)
        sum_y = jnp.zeros((8, cols), F32)
        for l in range(LEV):
            got = []
            for c in range(3):
                q = c * LEV + l
                centre = pad[q, base : base + 8, :]
                south = pad[q, base - 1 : base + 7, :]
                north = pad[q, base + 1 : base + 9, :]
                before = col_rx[0, 8 * s : 8 * s + 8, q : q + 1]
                after = col_rx[1, 8 * s : 8 * s + 8, q : q + 1]
                west = jnp.where(lane_ids == 0, before, shift_cols(centre, 1))
                east = jnp.where(lane_ids == cols - 1, after, shift_cols(centre, -1))
                got.append((centre, east, west, north, south))
            laps = [e + w + n + so - 4.0 * ce for ce, e, w, n, so in got]
            u, v, t = got[0][0], got[1][0], got[2][0]
            dx = got[2][1] - got[2][2]
            dy = got[2][3] - got[2][4]
            sum_x = sum_x + dx
            sum_y = sum_y + dy
            fu = force_up[l * 2, 8 * s : 8 * s + 8, :]
            fv = force_up[l * 2 + 1, 8 * s : 8 * s + 8, :]
            velo_new[0, l, 8 * s : 8 * s + 8, :] = u + wet * (
                coriolis * v + 0.25 * sum_x + 0.5 * laps[0] + fu
            )
            velo_new[1, l, 8 * s : 8 * s + 8, :] = v + wet * (
                -coriolis * u + 0.25 * sum_y + 0.5 * laps[1] + fv
            )
            temp_new[l, 8 * s : 8 * s + 8, :] = t + wet * (
                -0.5 * (u * dx + v * dy) + 0.3 * laps[2]
            )

    stores = [
        pltpu.make_async_copy(velo_new, velo_out, out_sem.at[0]),
        pltpu.make_async_copy(temp_new, temp_out, out_sem.at[1]),
    ]
    for store in stores:
        store.start()

    @pl.when(is_owner)
    def _():
        passed(halved, (owners - 1) * chunk, ag_recv.at[0])

    @pl.when(jnp.logical_not(is_owner))
    def _():
        passed(halved, owners * chunk, ag_recv.at[0])

    def keep(side, sem):
        return pltpu.make_async_copy(gathered.at[side], grads.at[side], out_sem.at[sem])

    keep(core, 2).start()
    passed(halved, owners * chunk, ag_recv.at[1])
    keep(1 - core, 3).start()

    for store in stores:
        store.wait()
    for l in range(n_lon):
        @pl.when(lat < n_lat - 1)
        def _(l=l):
            up_copy(l).wait_send()

        @pl.when(lat > 0)
        def _(l=l):
            down_copy(l).wait_send()

        @pl.when(lon != l)
        def _(l=l):
            own_copy(l).wait_send()

        for m in range(n_mem):
            @pl.when(elsewhere(l, m))
            def _(l=l, m=m):
                force_copy(l, m).wait_send()

    @pl.when(lat < n_lat - 1)
    def _():
        row_up().wait_send()

    @pl.when(lat > 0)
    def _():
        row_down().wait_send()

    col_east().wait_send()
    col_west().wait_send()

    @pl.when(is_owner)
    def _():
        passed(halved, (owners - 1) * chunk, rs_send)
        passed(scattered, plane - 1, ag_send.at[0])
        passed(scattered, plane, ag_send.at[1])

    @pl.when(jnp.logical_not(is_owner))
    def _():
        passed(halved, owners * chunk, rs_send)

    keep(core, 2).wait()
    keep(1 - core, 3).wait()


def finish(
    velo_in, temp_in, halves_in, velo_out, temp_out, first_out, middle_out, last_out,
    velo, temp, halves, first, middle, last, sems,
):
    load = pltpu.make_async_copy(halves_in, halves, sems.at[0])
    load.start()
    blocks = [(velo_in.at[c], velo.at[c], velo_out.at[c]) for c in range(2)]
    blocks.append((temp_in, temp, temp_out))
    moves = [pltpu.make_async_copy(b[0], b[1], sems.at[1 + i]) for i, b in enumerate(blocks)]
    for move in moves:
        move.start()
    load.wait()

    def rows_of(start, size, cols):
        side, row = place(start // 8)
        return halves[side, row + start % 8 : row + start % 8 + size, cols]

    stores = []
    for m in range(2):
        cols = slice(m * HID, (m + 1) * HID)
        for a in range(3):
            for b in range(3):
                k = 3 * a + b
                for i in range(HID // 8):
                    middle[m, k, 8 * i : 8 * i + 8] = rows_of(a * 192 + b * HID + 8 * i, 8, cols)
                at_row = MID_ROWS + (2 - a) * 24 + b * 8 + 4 + 2 * m
                last[m, k] = rows_of(at_row, 2, cols)
                for c in range(3):
                    at_row = MID_ROWS + SMALL_ROWS + a * 24 + b * 8 + c
                    first[k, c, m : m + 1, :] = rows_of(at_row, 1, cols)
        stores.append(pltpu.make_async_copy(middle.at[m], middle_out.at[m], sems.at[4 + m]))
        stores[-1].start()
    stores.append(pltpu.make_async_copy(first, first_out, sems.at[6]))
    stores.append(pltpu.make_async_copy(last, last_out, sems.at[7]))
    for store in stores[2:]:
        store.start()
    for i, (move, b) in enumerate(zip(moves, blocks)):
        move.wait()
        stores.append(pltpu.make_async_copy(b[1], b[2], sems.at[8 + i]))
        stores[-1].start()
    for store in stores:
        store.wait()


def per_device(n_lat, n_lon, n_mem, velo, temp, land, target, w_first, w_middle, w_last):
    rows, cols = temp.shape[1], temp.shape[2]
    rc, cc = rows // COARSE, cols // COARSE
    width = cc * n_lon
    plane = n_lat * (n_lon // 2)
    chunk, owners = chunking(n_lat, n_lon // 2)
    half = chunk * owners
    mine = w_first.shape[0]

    hbm = pl.BlockSpec(memory_space=pl.ANY)
    dma = pltpu.SemaphoreType.DMA
    fields = [jax.ShapeDtypeStruct(velo.shape, F32), jax.ShapeDtypeStruct(temp.shape, F32)]
    velo_next, temp_next, grads = pl.pallas_call(
        functools.partial(kernel, n_lat, n_lon, n_mem),
        out_shape=(*fields, jax.ShapeDtypeStruct((2, half, 128), F32)),
        in_specs=[hbm] * 7,
        out_specs=(hbm, hbm, hbm),
        scratch_shapes=[
            pltpu.VMEM(velo.shape, F32),
            pltpu.VMEM(temp.shape, F32),
            pltpu.VMEM(land.shape, jnp.int32),
            pltpu.VMEM(target.shape, BF16),
            pltpu.VMEM((9, 3, mine, HID), BF16),
            pltpu.VMEM(w_middle.shape, BF16),
            pltpu.VMEM(w_last.shape, BF16),
            pltpu.VMEM((LEV * rows, cc), F32),
            pltpu.VMEM((LEV * 2 * rows, cc), F32),
            pltpu.VMEM((LEV * rc * 8, cc), F32),
            pltpu.VMEM((LEV, rc, 8, cc), BF16),
            pltpu.VMEM((n_lon, rc + 2 * HALO, 8, cc), BF16),
            pltpu.VMEM((rc + 2 * HALO, 32, width), BF16),
            pltpu.VMEM((2, rc + 8, 3 * HID, width), BF16),
            pltpu.VMEM((rc + 6, 2 * HID, width), BF16),
            pltpu.VMEM((rc + 4, 32, width), BF16),
            pltpu.VMEM((2, rc + 2, 3 * HID, width), BF16),
            pltpu.VMEM((2, rc, width), F32),
            pltpu.VMEM((n_mem, n_lon, 2, rc, cc), F32),
            pltpu.VMEM((LEV * 2, rows, cols), F32),
            pltpu.VMEM((3 * LEV, rows + 16, cols), F32),
            pltpu.VMEM((2, 16, cols), F32),
            pltpu.VMEM((2, 16, cols), F32),
            pltpu.VMEM((2, rows, 128), F32),
            pltpu.VMEM((2, rows, 128), F32),
            pltpu.VMEM((96, 128), F32),
            pltpu.VMEM((72, 128), F32),
            pltpu.VMEM((2, half, 128), F32),
            pltpu.VMEM((half, 128), F32),
            pltpu.VMEM((half, 128), F32),
            pltpu.VMEM((plane, chunk, 128), F32),
            pltpu.VMEM((2, half, 128), F32),
            dma((8,)),
            dma((4,)),
            pltpu.SemaphoreType.REGULAR,
            dma((2,)),
            dma((2,)),
            dma((3, n_lon)),
            dma((3, n_lon)),
            dma((4,)),
            dma((4,)),
            dma((n_mem, n_lon)),
            dma((n_mem, n_lon)),
            dma,
            dma,
            dma,
            dma((2,)),
            dma((2,)),
        ],
        compiler_params=pltpu.CompilerParams(
            collective_id=0, has_side_effects=True, vmem_limit_bytes=56 * 1024 * 1024
        ),
        name="ocean_step",
    )(velo, temp, land, target, jnp.transpose(w_first, (1, 3, 0, 2)), w_middle, w_last)
    velo_next, temp_next, first, middle, last = pl.pallas_call(
        finish,
        out_shape=(
            *fields,
            jax.ShapeDtypeStruct((9, 3, mine, HID), F32),
            jax.ShapeDtypeStruct(w_middle.shape, F32),
            jax.ShapeDtypeStruct(w_last.shape, F32),
        ),
        in_specs=[hbm] * 3,
        out_specs=(hbm,) * 5,
        scratch_shapes=[
            pltpu.VMEM(velo.shape, F32),
            pltpu.VMEM(temp.shape, F32),
            pltpu.VMEM((2, half, 128), F32),
            pltpu.VMEM((9, 3, mine, HID), F32),
            pltpu.VMEM(w_middle.shape, F32),
            pltpu.VMEM(w_last.shape, F32),
            dma((11,)),
        ],
        name="finish",
    )(velo_next, temp_next, grads)
    return (velo_next, temp_next, jnp.transpose(first, (2, 0, 3, 1)), middle, last)


def solution(mesh):
    return jax.shard_map(
        functools.partial(per_device, mesh.shape["lat"], mesh.shape["lon"], mesh.shape["mem"]),
        mesh=mesh,
        in_specs=(
            P(None, None, "lat", "lon"),
            P(None, "lat", "lon"),
            P("lat", "lon"),
            P(None, None, "lat", "lon"),
            P("mem", None, None, None),
            P("mem", None, None, None),
            P("mem", None, None, None),
        ),
        out_specs=(
            P(None, None, "lat", "lon"),
            P(None, "lat", "lon"),
            P("mem", None, None, None),
            P("mem", None, None, None),
            P("mem", None, None, None),
        ),
        check_vma=False,
    )
```

```python
import functools
import math

import jax
import jax.numpy as jnp
from jax import lax
from jax.experimental import pallas as pl
from jax.experimental.pallas import tpu as pltpu
from jax.sharding import PartitionSpec as P

LEV = 4
COARSE = 4
HID = 64
HALO = 5
MESH = pl.DeviceIdType.MESH
F32 = jnp.float32
BF16 = jnp.bfloat16
MID_ROWS = 9 * HID
SMALL_ROWS = 72
GRAD_ROWS = MID_ROWS + SMALL_ROWS
FIRST_ROWS = 16
NT = (((1,), (1,)), ((), ()))


def chunking(n_lat, planes):
    tiles = -(-GRAD_ROWS // 16)
    most = (n_lat // 4 * 3 if n_lat % 4 == 0 else n_lat) * planes
    per = -(-tiles // most)
    return per * 8, -(-tiles // per)


TILES = GRAD_ROWS // 8
LOW = (TILES + 1) // 2


def place(tile):
    return (0, 8 * tile) if tile < LOW else (1, 8 * (tile - LOW))


def shift_cols(value, by):
    return pltpu.roll(value, by % value.shape[-1], axis=value.ndim - 1)


def kernel(
    n_lat, n_lon, n_mem,
    velo_in, temp_in, land_in, target_in, first_in, middle_in, last_in,
    velo_out, temp_out, grads, small_out,
    velo_new, temp_new, land, target, w_first, w_middle, w_last,
    narrow, tall, staged, send_buf, rx, s0, s1, h2s, g3s, d2s, pred_buf, force_rx, force_up, pad,
    row_send, row_rx, col_send, col_rx, w1_rows, wl_rows, partial, theirs, halved, scattered, gathered,
    small_part, small_theirs, small_all, small_sum,
    in_sem, out_sem,
    entered, cp_send, cp_recv, cs_sem, cr_sem, os_sem, or_sem, fs_sem, fr_sem, fl_sem, rs_send, rs_recv, ag_send, ag_recv, fg_send, fg_recv,
):
    lat = lax.axis_index("lat")
    lon = lax.axis_index("lon")
    mem = lax.axis_index("mem")
    rows = temp_in.shape[1]
    cols = temp_in.shape[2]
    rc = rows // COARSE
    cc = cols // COARSE
    width = cc * n_lon
    nyc = rc * n_lat
    planes = n_lon // 2
    plane = n_lat * planes
    chunk, owners = chunking(n_lat, planes)
    half = chunk * owners
    core = lax.rem(lon, 2)
    partner = lon + 1 - 2 * core
    place_z = lax.div(lon, 2)
    rank = lat * planes + place_z

    def owns(lat_of):
        return lax.rem(lat_of, 4) != 3 if n_lat % 4 == 0 else lat_of >= 0

    def turn_of(lat_of, z_of):
        return (lat_of - lax.div(lat_of, 4) if n_lat % 4 == 0 else lat_of) * planes + z_of

    turn = turn_of(lat, place_z)
    is_owner = jnp.logical_and(owns(lat), turn < owners)

    def wrapped(value, size):
        return jnp.where(value >= size, value - size, value)

    def around(which):
        for i in list(range(1, n_lat)) + [0]:
            for k in range(planes):
                z = wrapped(place_z + (k + 1 if i == 0 else k), planes)
                if i > 0 or k < planes - 1:
                    which(wrapped(lat + i, n_lat), z)

    def at(lat_to, lon_to, mem_to):
        return {"lat": lat_to, "lon": lon_to, "mem": mem_to}

    inner = pl.ds(8, rows)
    loads = [
        pltpu.make_async_copy(velo_in.at[c], pad.at[pl.ds(c * LEV, LEV), inner], in_sem.at[c])
        for c in range(2)
    ]
    loads.append(
        pltpu.make_async_copy(temp_in, pad.at[pl.ds(2 * LEV, LEV), inner], in_sem.at[2])
    )
    loads.append(pltpu.make_async_copy(target_in, target, in_sem.at[3]))
    loads.append(pltpu.make_async_copy(land_in, land, in_sem.at[4]))
    loads.append(pltpu.make_async_copy(first_in, w_first, in_sem.at[5]))
    loads.append(pltpu.make_async_copy(middle_in, w_middle, in_sem.at[6]))
    loads.append(pltpu.make_async_copy(last_in, w_last, in_sem.at[7]))
    for load in loads:
        load.start()

    def of_plane(lat_to, z_to):
        return at(lat_to, 2 * z_to + core, mem)

    barrier = pltpu.get_barrier_semaphore()

    def greet(device):
        pl.semaphore_signal(barrier, inc=1, device_id=device, device_id_type=MESH)

    line = 4 if n_lat % 4 == 0 else n_lat
    line_start = lax.div(lat, line) * line
    greeted = 0
    for i in range(line, n_lat, line):
        for z in range(planes):
            greet(of_plane(wrapped(lat + i, n_lat), z))
            greeted += 1
    for i in range(1, line):
        for z in range(planes):
            greet(of_plane(line_start + wrapped(lat - line_start + i, line), z))
            greeted += 1
    for i in range(1, n_lon):
        greet(at(lat, wrapped(lon + i, n_lon), mem))
        greeted += 1
    for i in range(1, n_mem):
        for l in range(n_lon):
            greet(at(lat, l, wrapped(mem + i, n_mem)))
            greeted += 1

    @pl.when(lat > 0)
    def _():
        for l in range(n_lon):
            greet(at(lat - 1, l, mem))

    @pl.when(lat < n_lat - 1)
    def _():
        for l in range(n_lon):
            greet(at(lat + 1, l, mem))

    greeted = greeted + jnp.where(lat > 0, n_lon, 0) + jnp.where(lat < n_lat - 1, n_lon, 0)

    q_ids = lax.broadcasted_iota(jnp.int32, (cc, cols), 0)
    i_ids = lax.broadcasted_iota(jnp.int32, (cc, cols), 1)
    expand = jnp.where(i_ids // COARSE == q_ids, 1.0, 0.0).astype(F32)

    staged[...] = jnp.zeros_like(staged)
    for c in range(3):
        loads[c].wait()
        fine = pad[c * LEV : (c + 1) * LEV, 8 : 8 + rows, :].reshape(LEV * rows, cols)
        fine = fine * (1.0 / COARSE**2)
        high = fine.astype(BF16)
        rest = fine - high.astype(F32)
        middle = rest.astype(BF16)
        low = (rest - middle.astype(F32)).astype(BF16)
        parts = lax.dot_general(
            jnp.concatenate([high, middle, low], axis=0), expand.astype(BF16), NT,
            preferred_element_type=F32,
        )
        n = LEV * rows
        narrow[...] = parts[0:n] + parts[n : 2 * n] + parts[2 * n : 3 * n]
        pooled = narrow[pl.ds(0, LEV * rc, stride=COARSE), :]
        for r in range(1, COARSE):
            pooled = pooled + narrow[pl.ds(r, LEV * rc, stride=COARSE), :]
        staged[pl.ds(c, LEV * rc, stride=8), :] = pooled
    loads[3].wait()
    for c in range(2):
        goal = target[c].astype(F32).reshape(LEV * rc, cc)
        staged[pl.ds(4 + c, LEV * rc, stride=8), :] = goal
        staged[pl.ds(6 + c, LEV * rc, stride=8), :] = goal
    send_buf[...] = staged[...].astype(BF16).reshape(send_buf.shape)

    @pl.when(lat == 0)
    def _():
        rx[:, 0:HALO] = jnp.zeros((n_lon, HALO, 8, cc), BF16)
        row_rx[0] = jnp.zeros_like(row_rx[0])

    @pl.when(lat == n_lat - 1)
    def _():
        rx[:, HALO + rc : 2 * HALO + rc] = jnp.zeros((n_lon, HALO, 8, cc), BF16)
        row_rx[1] = jnp.zeros_like(row_rx[1])

    pl.semaphore_wait(barrier, greeted)

    def own_copy(l):
        return pltpu.make_async_remote_copy(
            src_ref=send_buf.at[l], dst_ref=rx.at[lon, pl.ds(HALO, rc)],
            send_sem=cs_sem.at[0, l], recv_sem=cr_sem.at[0, lon],
            device_id=at(lat, l, mem), device_id_type=MESH,
        )

    def up_copy(l):
        return pltpu.make_async_remote_copy(
            src_ref=send_buf.at[l, pl.ds(rc - HALO, HALO)], dst_ref=rx.at[lon, pl.ds(0, HALO)],
            send_sem=cs_sem.at[1, l], recv_sem=cr_sem.at[1, lon],
            device_id=at(lat + 1, l, mem), device_id_type=MESH,
        )

    def down_copy(l):
        return pltpu.make_async_remote_copy(
            src_ref=send_buf.at[l, pl.ds(0, HALO)], dst_ref=rx.at[lon, pl.ds(HALO + rc, HALO)],
            send_sem=cs_sem.at[2, l], recv_sem=cr_sem.at[2, lon],
            device_id=at(lat - 1, l, mem), device_id_type=MESH,
        )

    def row_up():
        return pltpu.make_async_remote_copy(
            src_ref=row_send.at[1], dst_ref=row_rx.at[0], send_sem=os_sem.at[0], recv_sem=or_sem.at[0],
            device_id=at(lat + 1, lon, mem), device_id_type=MESH,
        )

    def row_down():
        return pltpu.make_async_remote_copy(
            src_ref=row_send.at[0], dst_ref=row_rx.at[1], send_sem=os_sem.at[1], recv_sem=or_sem.at[1],
            device_id=at(lat - 1, lon, mem), device_id_type=MESH,
        )

    def col_east():
        return pltpu.make_async_remote_copy(
            src_ref=col_send.at[1], dst_ref=col_rx.at[0], send_sem=os_sem.at[2], recv_sem=or_sem.at[2],
            device_id=at(lat, lax.rem(lon + 1, n_lon), mem), device_id_type=MESH,
        )

    def col_west():
        return pltpu.make_async_remote_copy(
            src_ref=col_send.at[0], dst_ref=col_rx.at[1], send_sem=os_sem.at[3], recv_sem=or_sem.at[3],
            device_id=at(lat, lax.rem(lon + n_lon - 1, n_lon), mem), device_id_type=MESH,
        )

    for l in range(n_lon):
        @pl.when(lat < n_lat - 1)
        def _(l=l):
            up_copy(l).start()

        @pl.when(lat > 0)
        def _(l=l):
            down_copy(l).start()

        @pl.when(lon != l)
        def _(l=l):
            own_copy(l).start()

    for i in range(1, line):
        pl.semaphore_signal(
            entered, inc=1,
            device_id=of_plane(line_start + wrapped(lat - line_start + i, line), place_z),
            device_id_type=MESH,
        )

    lane = lax.broadcasted_iota(jnp.int32, (rows, 128), 1)
    west_cols = jnp.zeros((rows, 128), F32)
    east_cols = jnp.zeros((rows, 128), F32)
    for q in range(3 * LEV):
        first = pad[q, 8 : 8 + rows, 0:128]
        last = pad[q, 8 : 8 + rows, cols - 128 : cols]
        west_cols = jnp.where(lane == q, jnp.broadcast_to(first[:, 0:1], (rows, 128)), west_cols)
        east_cols = jnp.where(lane == q, jnp.broadcast_to(last[:, 127:128], (rows, 128)), east_cols)
        row_send[0, q : q + 1, :] = pad[q, 8:9, :]
        row_send[1, q : q + 1, :] = pad[q, 7 + rows : 8 + rows, :]
    col_send[0] = west_cols
    col_send[1] = east_cols

    @pl.when(lat < n_lat - 1)
    def _():
        row_up().start()

    @pl.when(lat > 0)
    def _():
        row_down().start()

    col_east().start()
    col_west().start()

    rx[lon, HALO : HALO + rc] = send_buf[lon]
    def flip(matrix):
        size = matrix.shape[1]
        eye = jnp.where(
            lax.broadcasted_iota(jnp.int32, (size, size), 0)
            == lax.broadcasted_iota(jnp.int32, (size, size), 1),
            1.0, 0.0,
        ).astype(BF16)
        return lax.dot_general(eye, matrix, NT, preferred_element_type=F32).astype(BF16)

    def beside(blocks):
        return jnp.concatenate(blocks, axis=1)

    for load in loads[5:]:
        load.wait()
    w1_rows[...] = jnp.zeros_like(w1_rows)
    wl_rows[...] = jnp.zeros_like(wl_rows)
    for a in range(3):
        for b in range(3):
            k = 3 * a + b
            for c in range(3):
                pair = w_first[k, c].astype(F32)
                for m in range(2):
                    at_row = a * 32 + b * 8 + c
                    w1_rows[at_row : at_row + 1, m * HID : (m + 1) * HID] = pair[m : m + 1]
            for m in range(2):
                at_row = a * 24 + b * 8 + 4 + 2 * m
                wl_rows[at_row : at_row + 2, m * HID : (m + 1) * HID] = w_last[m, k].astype(F32)
    w1 = flip(w1_rows[...].astype(BF16))
    wl = wl_rows[...].astype(BF16)
    gap = jnp.zeros((8, 2 * HID), F32)
    w3 = jnp.concatenate([p for t in (2, 1, 0) for p in (wl_rows[24 * t : 24 * t + 24, :], gap)], axis=0)
    w3t = flip(w3.astype(BF16))
    w2 = [
        jnp.concatenate([beside([w_middle[m, 3 * a + b] for b in range(3)]) for a in range(3)], axis=0)
        for m in range(2)
    ]
    w2t = [
        flip(jnp.concatenate([beside([w_middle[m, 3 * a + b] for a in range(3)]) for b in range(3)], axis=0))
        for m in range(2)
    ]

    def arrived(kind, l, src, dst):
        pltpu.make_async_copy(src, dst, cr_sem.at[kind, l]).wait()

    for l in range(n_lon):
        @pl.when(lon != l)
        def _(l=l):
            arrived(0, l, send_buf.at[l], rx.at[l, pl.ds(HALO, rc)])

        @pl.when(lat > 0)
        def _(l=l):
            arrived(1, l, send_buf.at[l, pl.ds(0, HALO)], rx.at[l, pl.ds(0, HALO)])

        @pl.when(lat < n_lat - 1)
        def _(l=l):
            arrived(2, l, send_buf.at[l, pl.ds(0, HALO)], rx.at[l, pl.ds(HALO + rc, HALO)])

    def inside(g):
        return jnp.where(jnp.logical_and(g >= 0, g < nyc), 1.0, 0.0).astype(F32)

    def received(x):
        return jnp.concatenate([rx[l, x].astype(F32) for l in range(n_lon)], axis=-1)

    def three(v):
        return jnp.concatenate([shift_cols(v, 1), v, shift_cols(v, -1), jnp.zeros_like(v)], axis=0)

    for x in range(rc + 2 * HALO):
        s0[x] = three(received(x)).astype(BF16)

    for r in range(rc + 8):
        block = s0[r : r + 3].reshape(96, width)
        h = jnp.tanh(jnp.dot(w1, block, preferred_element_type=F32)) * inside(lat * rc - 4 + r)
        for m in range(2):
            hm = h[m * HID : (m + 1) * HID]
            s1[m, r, 0:HID] = shift_cols(hm, 1).astype(BF16)
            s1[m, r, HID : 2 * HID] = hm.astype(BF16)
            s1[m, r, 2 * HID : 3 * HID] = shift_cols(hm, -1).astype(BF16)

    def taps(products, r, order):
        return sum(
            products[r + i][j * HID : (j + 1) * HID] for i, j in enumerate(order)
        )

    for m in range(2):
        products = [
            jnp.dot(w2[m], s1[m, x], preferred_element_type=F32) for x in range(rc + 8)
        ]
        for r in range(rc + 6):
            h = jnp.tanh(taps(products, r, (0, 1, 2))) * inside(lat * rc - 3 + r)
            h2s[r, m * HID : (m + 1) * HID] = h.astype(BF16)

    scale = 2.0 / (2.0 * LEV * nyc * width)
    sub = lax.broadcasted_iota(jnp.int32, (8, width), 0)
    outs = [jnp.dot(wl, h2s[x], preferred_element_type=F32) for x in range(rc + 6)]
    for r in range(rc + 4):
        u = [sum(outs[r + a][24 * a + 8 * b : 24 * a + 8 * b + 8] for a in range(3)) for b in range(3)]
        pred = shift_cols(u[0], 1) + u[1] + shift_cols(u[2], -1)
        g3 = jnp.where(sub >= 4, (pred - received(r + 3)) * scale, 0.0) * inside(lat * rc - 2 + r)
        g3s[r] = jnp.concatenate(
            [shift_cols(g3, -1), g3, shift_cols(g3, 1), jnp.zeros_like(g3)], axis=0
        ).astype(BF16)
        if 2 <= r < 2 + rc:
            both = pred[4:6] + pred[6:8]
            for o in range(2):
                pred_buf[o, r - 2 : r - 1, :] = both[o : o + 1]

    def force_copy(l, m):
        return pltpu.make_async_remote_copy(
            src_ref=pred_buf.at[:, :, pl.ds(l * cc, cc)], dst_ref=force_rx.at[mem, lon],
            send_sem=fs_sem.at[m, l], recv_sem=fr_sem.at[mem, lon],
            device_id=at(lat, l, m), device_id_type=MESH,
        )

    def force_own():
        return pltpu.make_async_copy(
            pred_buf.at[:, :, pl.ds(pl.multiple_of(lon * cc, cc), cc)], force_rx.at[mem, lon], fl_sem
        )

    def elsewhere(l, m):
        return jnp.logical_or(lon != l, mem != m)

    for m in range(n_mem):
        for l in range(n_lon):
            @pl.when(elsewhere(l, m))
            def _(l=l, m=m):
                force_copy(l, m).start()

    force_own().start()

    for r in range(rc + 2):
        block = g3s[r : r + 3].reshape(96, width)
        h = h2s[r + 2].astype(F32)
        d = jnp.dot(w3t, block, preferred_element_type=F32) * (1.0 - h * h)
        d = d * inside(lat * rc - 1 + r)
        for m in range(2):
            dm = d[m * HID : (m + 1) * HID]
            d2s[m, r, 0:HID] = shift_cols(dm, -1).astype(BF16)
            d2s[m, r, HID : 2 * HID] = dm.astype(BF16)
            d2s[m, r, 2 * HID : 3 * HID] = shift_cols(dm, 1).astype(BF16)

    def over_rows(left, right):
        return lax.dot_general(
            beside([left(r) for r in range(rc)]), beside([right(r) for r in range(rc)]), NT,
            preferred_element_type=F32,
        )

    mids = [
        over_rows(
            lambda r: d2s[m, r + 1],
            lambda r: s1[m, r + 3 : r + 6, HID : 2 * HID].reshape(3 * HID, width),
        )
        for m in range(2)
    ]
    def put(start, value):
        for i in range(value.shape[0] // 8):
            side, row = place(start // 8 + i)
            partial[side, row : row + 8, :] = value[8 * i : 8 * i + 8]

    for a in range(3):
        put(a * 192, beside([mids[m][:, a * HID : (a + 1) * HID] for m in range(2)]))
    last = over_rows(lambda r: g3s[r + 1 : r + 4].reshape(96, width), lambda r: h2s[r + 3])
    for a in range(3):
        at_row = MID_ROWS + 24 * a
        put(at_row, last[32 * a : 32 * a + 24, :])

    def core_copy(which):
        src, dst = ((partial, theirs), (small_part, small_theirs))[which]
        return pltpu.make_async_remote_copy(
            src_ref=src.at[1 - core], dst_ref=dst,
            send_sem=cp_send.at[which], recv_sem=cp_recv.at[which],
            device_id=at(lat, partner, mem), device_id_type=MESH,
        )

    for side, used in ((0, 8 * LOW), (1, 8 * (TILES - LOW))):
        if half > used:
            partial[side, used:, :] = jnp.zeros((half - used, 128), F32)
    core_copy(0).start()
    if line > 1:
        pl.semaphore_wait(entered, line - 1)

    def piece(ref, index):
        return ref.at[pl.ds(pl.multiple_of(index * chunk, chunk), chunk)]

    def reduce_rows():
        core_copy(0).wait()
        halved[...] = partial[core] + theirs[...]

        def send(lat_to, z_to):
            to = turn_of(lat_to, z_to)

            @pl.when(jnp.logical_and(owns(lat_to), to < owners))
            def _():
                pltpu.make_async_remote_copy(
                    src_ref=piece(halved, to), dst_ref=scattered.at[rank],
                    send_sem=rs_send, recv_sem=rs_recv,
                    device_id=of_plane(lat_to, z_to), device_id_type=MESH,
                ).start()

        around(send)

    d1s = []
    for m in range(2):
        products = [
            jnp.dot(w2t[m], d2s[m, x], preferred_element_type=F32) for x in range(rc + 2)
        ]
        own = []
        for r in range(rc):
            h = s1[m, r + 4, HID : 2 * HID].astype(F32)
            own.append((taps(products, r, (2, 1, 0)) * (1.0 - h * h)).astype(BF16))
        d1s.append(own)
        if m == 0:
            reduce_rows()
    first = over_rows(
        lambda r: s0[r + 4 : r + 7].reshape(96, width),
        lambda r: jnp.concatenate([d1s[0][r], d1s[1][r]], axis=0),
    )
    small_part[...] = jnp.zeros_like(small_part)
    for k in range(9):
        for c in range(3):
            side, row = divmod(3 * k + c, FIRST_ROWS)
            at_row = 32 * (k // 3) + 8 * (k % 3) + c
            small_part[side, row : row + 1, :] = first[at_row : at_row + 1, :]
    core_copy(1).start()
    core_copy(1).wait()
    small_all[rank] = small_part[core] + small_theirs[...]

    def tell(lat_to, z_to):
        pltpu.make_async_remote_copy(
            src_ref=small_all.at[rank], dst_ref=small_all.at[rank],
            send_sem=fg_send, recv_sem=fg_recv,
            device_id=of_plane(lat_to, z_to), device_id_type=MESH,
        ).start()

    around(tell)

    def passed(ref, count, sem):
        pltpu.make_async_copy(ref.at[pl.ds(0, count)], ref.at[pl.ds(0, count)], sem).wait()

    @pl.when(is_owner)
    def _():
        passed(scattered, plane - 1, rs_recv)
        start = pl.multiple_of(turn * chunk, chunk)
        total = halved[pl.ds(start, chunk), :]
        for i in range(1, plane):
            total = total + scattered[lax.rem(rank + i, plane)]
        gathered[core, pl.ds(start, chunk), :] = total

        def spread(lat_to, z_to):
            pltpu.make_async_remote_copy(
                src_ref=piece(gathered.at[core], turn), dst_ref=piece(gathered.at[core], turn),
                send_sem=ag_send, recv_sem=ag_recv,
                device_id=of_plane(lat_to, z_to), device_id_type=MESH,
            ).start()

        around(spread)

    for m in range(n_mem):
        for l in range(n_lon):
            @pl.when(elsewhere(l, m))
            def _(l=l, m=m):
                pltpu.make_async_copy(
                    pred_buf.at[:, :, pl.ds(0, cc)], force_rx.at[m, l], fr_sem.at[m, l]
                ).wait()

    force_own().wait()

    @pl.when(lat > 0)
    def _():
        pltpu.make_async_copy(row_send.at[0], row_rx.at[0], or_sem.at[0]).wait()

    @pl.when(lat < n_lat - 1)
    def _():
        pltpu.make_async_copy(row_send.at[0], row_rx.at[1], or_sem.at[1]).wait()

    pltpu.make_async_copy(col_send.at[0], col_rx.at[0], or_sem.at[2]).wait()
    pltpu.make_async_copy(col_send.at[0], col_rx.at[1], or_sem.at[3]).wait()

    summed = force_rx[0]
    for m in range(1, n_mem):
        summed = summed + force_rx[m]
    mean = (summed * (1.0 / (2 * n_mem))).reshape(LEV * 2 * rc, cc)
    for r in range(COARSE):
        tall[pl.ds(r, LEV * 2 * rc, stride=COARSE), :] = mean
    force_up[...] = jnp.dot(
        tall[...], expand, precision=lax.Precision.HIGHEST, preferred_element_type=F32
    ).reshape(force_up.shape)
    for q in range(3 * LEV):
        pad[q, 7:8, :] = row_rx[0, q : q + 1, :]
        pad[q, 8 + rows : 9 + rows, :] = row_rx[1, q : q + 1, :]

    loads[4].wait()
    lane_ids = lax.broadcasted_iota(jnp.int32, (8, cols), 1)
    for s in range(rows // 8):
        base = 8 + 8 * s
        ids = (lat * rows + 8 * s + lax.broadcasted_iota(jnp.int32, (8, cols), 0)).astype(F32)
        coriolis = jnp.sin(-math.pi / 2 + math.pi * (ids + 0.5) / (rows * n_lat))
        wet = 0.1 * land[8 * s : 8 * s + 8, :].astype(F32)
        sum_x = jnp.zeros((8, cols), F32)
        sum_y = jnp.zeros((8, cols), F32)
        for l in range(LEV):
            got = []
            for c in range(3):
                q = c * LEV + l
                centre = pad[q, base : base + 8, :]
                south = pad[q, base - 1 : base + 7, :]
                north = pad[q, base + 1 : base + 9, :]
                before = col_rx[0, 8 * s : 8 * s + 8, q : q + 1]
                after = col_rx[1, 8 * s : 8 * s + 8, q : q + 1]
                west = jnp.where(lane_ids == 0, before, shift_cols(centre, 1))
                east = jnp.where(lane_ids == cols - 1, after, shift_cols(centre, -1))
                got.append((centre, east, west, north, south))
            laps = [e + w + n + so - 4.0 * ce for ce, e, w, n, so in got]
            u, v, t = got[0][0], got[1][0], got[2][0]
            dx = got[2][1] - got[2][2]
            dy = got[2][3] - got[2][4]
            sum_x = sum_x + dx
            sum_y = sum_y + dy
            fu = force_up[l * 2, 8 * s : 8 * s + 8, :]
            fv = force_up[l * 2 + 1, 8 * s : 8 * s + 8, :]
            velo_new[0, l, 8 * s : 8 * s + 8, :] = u + wet * (
                coriolis * v + 0.25 * sum_x + 0.5 * laps[0] + fu
            )
            velo_new[1, l, 8 * s : 8 * s + 8, :] = v + wet * (
                -coriolis * u + 0.25 * sum_y + 0.5 * laps[1] + fv
            )
            temp_new[l, 8 * s : 8 * s + 8, :] = t + wet * (
                -0.5 * (u * dx + v * dy) + 0.3 * laps[2]
            )

    stores = [
        pltpu.make_async_copy(velo_new, velo_out, out_sem.at[0]),
        pltpu.make_async_copy(temp_new, temp_out, out_sem.at[1]),
    ]
    for store in stores:
        store.start()

    def share(ref, sem):
        return pltpu.make_async_remote_copy(
            src_ref=ref.at[core], dst_ref=ref.at[core],
            send_sem=cp_send.at[sem], recv_sem=cp_recv.at[sem],
            device_id=at(lat, partner, mem), device_id_type=MESH,
        )

    def keep(ref, out, side, sem):
        return pltpu.make_async_copy(ref.at[side], out.at[side], out_sem.at[sem])

    passed(small_all, plane - 1, fg_recv)
    total = small_all[0]
    for i in range(1, plane):
        total = total + small_all[i]
    small_sum[core] = total
    share(small_sum, 3).start()
    keep(small_sum, small_out, core, 4).start()

    @pl.when(is_owner)
    def _():
        passed(halved, (owners - 1) * chunk, ag_recv)

    @pl.when(jnp.logical_not(is_owner))
    def _():
        passed(halved, owners * chunk, ag_recv)

    share(gathered, 2).start()
    keep(gathered, grads, core, 2).start()
    share(small_sum, 3).wait()
    keep(small_sum, small_out, 1 - core, 5).start()

    for store in stores:
        store.wait()
    for l in range(n_lon):
        @pl.when(lat < n_lat - 1)
        def _(l=l):
            up_copy(l).wait_send()

        @pl.when(lat > 0)
        def _(l=l):
            down_copy(l).wait_send()

        @pl.when(lon != l)
        def _(l=l):
            own_copy(l).wait_send()

        for m in range(n_mem):
            @pl.when(elsewhere(l, m))
            def _(l=l, m=m):
                force_copy(l, m).wait_send()

    @pl.when(lat < n_lat - 1)
    def _():
        row_up().wait_send()

    @pl.when(lat > 0)
    def _():
        row_down().wait_send()

    col_east().wait_send()
    col_west().wait_send()

    @pl.when(is_owner)
    def _():
        passed(halved, (owners - 1) * chunk, rs_send)
        passed(scattered, plane - 1, ag_send)

    @pl.when(jnp.logical_not(is_owner))
    def _():
        passed(halved, owners * chunk, rs_send)

    share(gathered, 2).wait()
    keep(gathered, grads, 1 - core, 3).start()
    passed(small_all, plane - 1, fg_send)
    for ref, out, sem in ((gathered, grads, 2), (small_sum, small_out, 4)):
        keep(ref, out, core, sem).wait()
        keep(ref, out, 1 - core, sem + 1).wait()


def finish(
    velo_in, temp_in, halves_in, small_in, velo_out, temp_out, first_out, middle_out, last_out,
    velo, temp, halves, small, first, middle, last, sems,
):
    load = pltpu.make_async_copy(halves_in, halves, sems.at[0])
    load.start()
    load_small = pltpu.make_async_copy(small_in, small, sems.at[11])
    load_small.start()
    blocks = [(velo_in.at[c], velo.at[c], velo_out.at[c]) for c in range(2)]
    blocks.append((temp_in, temp, temp_out))
    moves = [pltpu.make_async_copy(b[0], b[1], sems.at[1 + i]) for i, b in enumerate(blocks)]
    for move in moves:
        move.start()
    load.wait()
    load_small.wait()

    def rows_of(start, size, cols):
        side, row = place(start // 8)
        return halves[side, row + start % 8 : row + start % 8 + size, cols]

    stores = []
    for m in range(2):
        cols = slice(m * HID, (m + 1) * HID)
        for a in range(3):
            for b in range(3):
                k = 3 * a + b
                for i in range(HID // 8):
                    middle[m, k, 8 * i : 8 * i + 8] = rows_of(a * 192 + b * HID + 8 * i, 8, cols)
                at_row = MID_ROWS + (2 - a) * 24 + b * 8 + 4 + 2 * m
                last[m, k] = rows_of(at_row, 2, cols)
                for c in range(3):
                    side, row = divmod(3 * k + c, FIRST_ROWS)
                    first[k, c, m : m + 1, :] = small[side, row : row + 1, cols]
        stores.append(pltpu.make_async_copy(middle.at[m], middle_out.at[m], sems.at[4 + m]))
        stores[-1].start()
    stores.append(pltpu.make_async_copy(first, first_out, sems.at[6]))
    stores.append(pltpu.make_async_copy(last, last_out, sems.at[7]))
    for store in stores[2:]:
        store.start()
    for i, (move, b) in enumerate(zip(moves, blocks)):
        move.wait()
        stores.append(pltpu.make_async_copy(b[1], b[2], sems.at[8 + i]))
        stores[-1].start()
    for store in stores:
        store.wait()


def per_device(n_lat, n_lon, n_mem, velo, temp, land, target, w_first, w_middle, w_last):
    rows, cols = temp.shape[1], temp.shape[2]
    rc, cc = rows // COARSE, cols // COARSE
    width = cc * n_lon
    plane = n_lat * (n_lon // 2)
    chunk, owners = chunking(n_lat, n_lon // 2)
    half = chunk * owners
    mine = w_first.shape[0]

    hbm = pl.BlockSpec(memory_space=pl.ANY)
    dma = pltpu.SemaphoreType.DMA
    fields = [jax.ShapeDtypeStruct(velo.shape, F32), jax.ShapeDtypeStruct(temp.shape, F32)]
    velo_next, temp_next, grads, small = pl.pallas_call(
        functools.partial(kernel, n_lat, n_lon, n_mem),
        out_shape=(
            *fields,
            jax.ShapeDtypeStruct((2, half, 128), F32),
            jax.ShapeDtypeStruct((2, FIRST_ROWS, 128), F32),
        ),
        in_specs=[hbm] * 7,
        out_specs=(hbm,) * 4,
        scratch_shapes=[
            pltpu.VMEM(velo.shape, F32),
            pltpu.VMEM(temp.shape, F32),
            pltpu.VMEM(land.shape, jnp.int32),
            pltpu.VMEM(target.shape, BF16),
            pltpu.VMEM((9, 3, mine, HID), BF16),
            pltpu.VMEM(w_middle.shape, BF16),
            pltpu.VMEM(w_last.shape, BF16),
            pltpu.VMEM((LEV * rows, cc), F32),
            pltpu.VMEM((LEV * 2 * rows, cc), F32),
            pltpu.VMEM((LEV * rc * 8, cc), F32),
            pltpu.VMEM((LEV, rc, 8, cc), BF16),
            pltpu.VMEM((n_lon, rc + 2 * HALO, 8, cc), BF16),
            pltpu.VMEM((rc + 2 * HALO, 32, width), BF16),
            pltpu.VMEM((2, rc + 8, 3 * HID, width), BF16),
            pltpu.VMEM((rc + 6, 2 * HID, width), BF16),
            pltpu.VMEM((rc + 4, 32, width), BF16),
            pltpu.VMEM((2, rc + 2, 3 * HID, width), BF16),
            pltpu.VMEM((2, rc, width), F32),
            pltpu.VMEM((n_mem, n_lon, 2, rc, cc), F32),
            pltpu.VMEM((LEV * 2, rows, cols), F32),
            pltpu.VMEM((3 * LEV, rows + 16, cols), F32),
            pltpu.VMEM((2, 16, cols), F32),
            pltpu.VMEM((2, 16, cols), F32),
            pltpu.VMEM((2, rows, 128), F32),
            pltpu.VMEM((2, rows, 128), F32),
            pltpu.VMEM((96, 128), F32),
            pltpu.VMEM((72, 128), F32),
            pltpu.VMEM((2, half, 128), F32),
            pltpu.VMEM((half, 128), F32),
            pltpu.VMEM((half, 128), F32),
            pltpu.VMEM((plane, chunk, 128), F32),
            pltpu.VMEM((2, half, 128), F32),
            pltpu.VMEM((2, FIRST_ROWS, 128), F32),
            pltpu.VMEM((FIRST_ROWS, 128), F32),
            pltpu.VMEM((plane, FIRST_ROWS, 128), F32),
            pltpu.VMEM((2, FIRST_ROWS, 128), F32),
            dma((8,)),
            dma((6,)),
            pltpu.SemaphoreType.REGULAR,
            dma((4,)),
            dma((4,)),
            dma((3, n_lon)),
            dma((3, n_lon)),
            dma((4,)),
            dma((4,)),
            dma((n_mem, n_lon)),
            dma((n_mem, n_lon)),
            dma,
            dma,
            dma,
            dma,
            dma,
            dma,
            dma,
        ],
        compiler_params=pltpu.CompilerParams(
            collective_id=0, has_side_effects=True, vmem_limit_bytes=56 * 1024 * 1024
        ),
        name="ocean_step",
    )(velo, temp, land, target, jnp.transpose(w_first, (1, 3, 0, 2)), w_middle, w_last)
    velo_next, temp_next, first, middle, last = pl.pallas_call(
        finish,
        out_shape=(
            *fields,
            jax.ShapeDtypeStruct((9, 3, mine, HID), F32),
            jax.ShapeDtypeStruct(w_middle.shape, F32),
            jax.ShapeDtypeStruct(w_last.shape, F32),
        ),
        in_specs=[hbm] * 4,
        out_specs=(hbm,) * 5,
        scratch_shapes=[
            pltpu.VMEM(velo.shape, F32),
            pltpu.VMEM(temp.shape, F32),
            pltpu.VMEM((2, half, 128), F32),
            pltpu.VMEM((2, FIRST_ROWS, 128), F32),
            pltpu.VMEM((9, 3, mine, HID), F32),
            pltpu.VMEM(w_middle.shape, F32),
            pltpu.VMEM(w_last.shape, F32),
            dma((12,)),
        ],
        name="finish",
    )(velo_next, temp_next, grads, small)
    return (velo_next, temp_next, jnp.transpose(first, (2, 0, 3, 1)), middle, last)


def solution(mesh):
    return jax.shard_map(
        functools.partial(per_device, mesh.shape["lat"], mesh.shape["lon"], mesh.shape["mem"]),
        mesh=mesh,
        in_specs=(
            P(None, None, "lat", "lon"),
            P(None, "lat", "lon"),
            P("lat", "lon"),
            P(None, None, "lat", "lon"),
            P("mem", None, None, None),
            P("mem", None, None, None),
            P("mem", None, None, None),
        ),
        out_specs=(
            P(None, None, "lat", "lon"),
            P(None, "lat", "lon"),
            P("mem", None, None, None),
            P("mem", None, None, None),
            P("mem", None, None, None),
        ),
        check_vma=False,
    )
```

```python
import functools
import math

import jax
import jax.numpy as jnp
from jax import lax
from jax.experimental import pallas as pl
from jax.experimental.pallas import tpu as pltpu
from jax.sharding import PartitionSpec as P

LEV = 4
COARSE = 4
HID = 64
HALO = 5
MESH = pl.DeviceIdType.MESH
F32 = jnp.float32
BF16 = jnp.bfloat16
MID_ROWS = 9 * HID
SMALL_ROWS = 72
GRAD_ROWS = MID_ROWS + 2 * SMALL_ROWS
NT = (((1,), (1,)), ((), ()))


def chunking(n_lat, planes):
    tiles = -(-GRAD_ROWS // 16)
    owners = (n_lat // 4 * 3 if n_lat % 4 == 0 else n_lat) * planes
    return -(-tiles // owners) * 8, owners


EARLY = (MID_ROWS + SMALL_ROWS) // 8
LOW_EARLY, LOW_LATE = (EARLY + 1) // 2, (SMALL_ROWS // 8 + 1) // 2


def place(tile):
    if tile < EARLY:
        return divmod_half(tile, LOW_EARLY, 0, 0)
    return divmod_half(tile - EARLY, LOW_LATE, LOW_EARLY, EARLY - LOW_EARLY)


def divmod_half(tile, low, base_low, base_high):
    return (0, 8 * (base_low + tile)) if tile < low else (1, 8 * (base_high + tile - low))


def shift_cols(value, by):
    return pltpu.roll(value, by % value.shape[-1], axis=value.ndim - 1)


def kernel(
    n_lat, n_lon, n_mem,
    velo_in, temp_in, land_in, target_in, first_in, middle_in, last_in,
    velo_out, temp_out, grads,
    velo_new, temp_new, land, target, w_first, w_middle, w_last,
    narrow, tall, staged, send_buf, rx, s0, s1, h2s, g3s, d2s, pred_buf, force_rx, force_up, pad,
    row_send, row_rx, col_send, col_rx, w1_rows, wl_rows, partial, theirs, halved, scattered, gathered,
    in_sem, out_sem,
    entered, cp_send, cp_recv, cs_sem, cr_sem, os_sem, or_sem, fs_sem, fr_sem, fl_sem, rs_send, rs_recv, ag_send, ag_recv,
):
    lat = lax.axis_index("lat")
    lon = lax.axis_index("lon")
    mem = lax.axis_index("mem")
    rows = temp_in.shape[1]
    cols = temp_in.shape[2]
    rc = rows // COARSE
    cc = cols // COARSE
    width = cc * n_lon
    nyc = rc * n_lat
    planes = n_lon // 2
    plane = n_lat * planes
    chunk, owners = chunking(n_lat, planes)
    half = chunk * owners
    core = lax.rem(lon, 2)
    partner = lon + 1 - 2 * core
    place_z = lax.div(lon, 2)
    rank = lat * planes + place_z

    def owns(lat_of):
        return lax.rem(lat_of, 4) != 3 if n_lat % 4 == 0 else lat_of >= 0

    def turn_of(lat_of, z_of):
        return (lat_of - lax.div(lat_of, 4) if n_lat % 4 == 0 else lat_of) * planes + z_of

    turn = turn_of(lat, place_z)
    is_owner = owns(lat)

    def wrapped(value, size):
        return jnp.where(value >= size, value - size, value)

    def around(which):
        for i in list(range(1, n_lat)) + [0]:
            for k in range(planes):
                z = wrapped(place_z + (k + 1 if i == 0 else k), planes)
                if i > 0 or k < planes - 1:
                    which(wrapped(lat + i, n_lat), z)

    def at(lat_to, lon_to, mem_to):
        return {"lat": lat_to, "lon": lon_to, "mem": mem_to}

    inner = pl.ds(8, rows)
    loads = [
        pltpu.make_async_copy(velo_in.at[c], pad.at[pl.ds(c * LEV, LEV), inner], in_sem.at[c])
        for c in range(2)
    ]
    loads.append(
        pltpu.make_async_copy(temp_in, pad.at[pl.ds(2 * LEV, LEV), inner], in_sem.at[2])
    )
    loads.append(pltpu.make_async_copy(target_in, target, in_sem.at[3]))
    loads.append(pltpu.make_async_copy(land_in, land, in_sem.at[4]))
    loads.append(pltpu.make_async_copy(first_in, w_first, in_sem.at[5]))
    loads.append(pltpu.make_async_copy(middle_in, w_middle, in_sem.at[6]))
    loads.append(pltpu.make_async_copy(last_in, w_last, in_sem.at[7]))
    for load in loads:
        load.start()

    def of_plane(lat_to, z_to):
        return at(lat_to, 2 * z_to + core, mem)

    barrier = pltpu.get_barrier_semaphore()

    def greet(device):
        pl.semaphore_signal(barrier, inc=1, device_id=device, device_id_type=MESH)

    line = 4 if n_lat % 4 == 0 else n_lat
    line_start = lax.div(lat, line) * line
    greeted = 0
    for i in range(line, n_lat, line):
        for z in range(planes):
            greet(of_plane(wrapped(lat + i, n_lat), z))
            greeted += 1
    for i in range(1, line):
        for z in range(planes):
            greet(of_plane(line_start + wrapped(lat - line_start + i, line), z))
            greeted += 1
    for i in range(1, n_lon):
        greet(at(lat, wrapped(lon + i, n_lon), mem))
        greeted += 1
    for i in range(1, n_mem):
        for l in range(n_lon):
            greet(at(lat, l, wrapped(mem + i, n_mem)))
            greeted += 1

    @pl.when(lat > 0)
    def _():
        for l in range(n_lon):
            greet(at(lat - 1, l, mem))

    @pl.when(lat < n_lat - 1)
    def _():
        for l in range(n_lon):
            greet(at(lat + 1, l, mem))

    greeted = greeted + jnp.where(lat > 0, n_lon, 0) + jnp.where(lat < n_lat - 1, n_lon, 0)

    q_ids = lax.broadcasted_iota(jnp.int32, (cc, cols), 0)
    i_ids = lax.broadcasted_iota(jnp.int32, (cc, cols), 1)
    expand = jnp.where(i_ids // COARSE == q_ids, 1.0, 0.0).astype(F32)

    staged[...] = jnp.zeros_like(staged)
    for c in range(3):
        loads[c].wait()
        fine = pad[c * LEV : (c + 1) * LEV, 8 : 8 + rows, :].reshape(LEV * rows, cols)
        fine = fine * (1.0 / COARSE**2)
        high = fine.astype(BF16)
        rest = fine - high.astype(F32)
        middle = rest.astype(BF16)
        low = (rest - middle.astype(F32)).astype(BF16)
        parts = lax.dot_general(
            jnp.concatenate([high, middle, low], axis=0), expand.astype(BF16), NT,
            preferred_element_type=F32,
        )
        n = LEV * rows
        narrow[...] = parts[0:n] + parts[n : 2 * n] + parts[2 * n : 3 * n]
        pooled = narrow[pl.ds(0, LEV * rc, stride=COARSE), :]
        for r in range(1, COARSE):
            pooled = pooled + narrow[pl.ds(r, LEV * rc, stride=COARSE), :]
        staged[pl.ds(c, LEV * rc, stride=8), :] = pooled
    loads[3].wait()
    for c in range(2):
        goal = target[c].astype(F32).reshape(LEV * rc, cc)
        staged[pl.ds(4 + c, LEV * rc, stride=8), :] = goal
        staged[pl.ds(6 + c, LEV * rc, stride=8), :] = goal
    send_buf[...] = staged[...].astype(BF16).reshape(send_buf.shape)

    @pl.when(lat == 0)
    def _():
        rx[:, 0:HALO] = jnp.zeros((n_lon, HALO, 8, cc), BF16)
        row_rx[0] = jnp.zeros_like(row_rx[0])

    @pl.when(lat == n_lat - 1)
    def _():
        rx[:, HALO + rc : 2 * HALO + rc] = jnp.zeros((n_lon, HALO, 8, cc), BF16)
        row_rx[1] = jnp.zeros_like(row_rx[1])

    pl.semaphore_wait(barrier, greeted)

    def own_copy(l):
        return pltpu.make_async_remote_copy(
            src_ref=send_buf.at[l], dst_ref=rx.at[lon, pl.ds(HALO, rc)],
            send_sem=cs_sem.at[0, l], recv_sem=cr_sem.at[0, lon],
            device_id=at(lat, l, mem), device_id_type=MESH,
        )

    def up_copy(l):
        return pltpu.make_async_remote_copy(
            src_ref=send_buf.at[l, pl.ds(rc - HALO, HALO)], dst_ref=rx.at[lon, pl.ds(0, HALO)],
            send_sem=cs_sem.at[1, l], recv_sem=cr_sem.at[1, lon],
            device_id=at(lat + 1, l, mem), device_id_type=MESH,
        )

    def down_copy(l):
        return pltpu.make_async_remote_copy(
            src_ref=send_buf.at[l, pl.ds(0, HALO)], dst_ref=rx.at[lon, pl.ds(HALO + rc, HALO)],
            send_sem=cs_sem.at[2, l], recv_sem=cr_sem.at[2, lon],
            device_id=at(lat - 1, l, mem), device_id_type=MESH,
        )

    def row_up():
        return pltpu.make_async_remote_copy(
            src_ref=row_send.at[1], dst_ref=row_rx.at[0], send_sem=os_sem.at[0], recv_sem=or_sem.at[0],
            device_id=at(lat + 1, lon, mem), device_id_type=MESH,
        )

    def row_down():
        return pltpu.make_async_remote_copy(
            src_ref=row_send.at[0], dst_ref=row_rx.at[1], send_sem=os_sem.at[1], recv_sem=or_sem.at[1],
            device_id=at(lat - 1, lon, mem), device_id_type=MESH,
        )

    def col_east():
        return pltpu.make_async_remote_copy(
            src_ref=col_send.at[1], dst_ref=col_rx.at[0], send_sem=os_sem.at[2], recv_sem=or_sem.at[2],
            device_id=at(lat, lax.rem(lon + 1, n_lon), mem), device_id_type=MESH,
        )

    def col_west():
        return pltpu.make_async_remote_copy(
            src_ref=col_send.at[0], dst_ref=col_rx.at[1], send_sem=os_sem.at[3], recv_sem=or_sem.at[3],
            device_id=at(lat, lax.rem(lon + n_lon - 1, n_lon), mem), device_id_type=MESH,
        )

    for l in range(n_lon):
        @pl.when(lat < n_lat - 1)
        def _(l=l):
            up_copy(l).start()

        @pl.when(lat > 0)
        def _(l=l):
            down_copy(l).start()

        @pl.when(lon != l)
        def _(l=l):
            own_copy(l).start()

    for i in range(1, line):
        pl.semaphore_signal(
            entered, inc=1,
            device_id=of_plane(line_start + wrapped(lat - line_start + i, line), place_z),
            device_id_type=MESH,
        )

    lane = lax.broadcasted_iota(jnp.int32, (rows, 128), 1)
    west_cols = jnp.zeros((rows, 128), F32)
    east_cols = jnp.zeros((rows, 128), F32)
    for q in range(3 * LEV):
        first = pad[q, 8 : 8 + rows, 0:128]
        last = pad[q, 8 : 8 + rows, cols - 128 : cols]
        west_cols = jnp.where(lane == q, jnp.broadcast_to(first[:, 0:1], (rows, 128)), west_cols)
        east_cols = jnp.where(lane == q, jnp.broadcast_to(last[:, 127:128], (rows, 128)), east_cols)
        row_send[0, q : q + 1, :] = pad[q, 8:9, :]
        row_send[1, q : q + 1, :] = pad[q, 7 + rows : 8 + rows, :]
    col_send[0] = west_cols
    col_send[1] = east_cols

    @pl.when(lat < n_lat - 1)
    def _():
        row_up().start()

    @pl.when(lat > 0)
    def _():
        row_down().start()

    col_east().start()
    col_west().start()

    rx[lon, HALO : HALO + rc] = send_buf[lon]
    def flip(matrix):
        size = matrix.shape[1]
        eye = jnp.where(
            lax.broadcasted_iota(jnp.int32, (size, size), 0)
            == lax.broadcasted_iota(jnp.int32, (size, size), 1),
            1.0, 0.0,
        ).astype(BF16)
        return lax.dot_general(eye, matrix, NT, preferred_element_type=F32).astype(BF16)

    def beside(blocks):
        return jnp.concatenate(blocks, axis=1)

    for load in loads[5:]:
        load.wait()
    w1_rows[...] = jnp.zeros_like(w1_rows)
    wl_rows[...] = jnp.zeros_like(wl_rows)
    for a in range(3):
        for b in range(3):
            k = 3 * a + b
            for c in range(3):
                pair = w_first[k, c].astype(F32)
                for m in range(2):
                    at_row = a * 32 + b * 8 + c
                    w1_rows[at_row : at_row + 1, m * HID : (m + 1) * HID] = pair[m : m + 1]
            for m in range(2):
                at_row = a * 24 + b * 8 + 4 + 2 * m
                wl_rows[at_row : at_row + 2, m * HID : (m + 1) * HID] = w_last[m, k].astype(F32)
    w1 = flip(w1_rows[...].astype(BF16))
    wl = wl_rows[...].astype(BF16)
    gap = jnp.zeros((8, 2 * HID), F32)
    w3 = jnp.concatenate([p for t in (2, 1, 0) for p in (wl_rows[24 * t : 24 * t + 24, :], gap)], axis=0)
    w3t = flip(w3.astype(BF16))
    w2 = [
        jnp.concatenate([beside([w_middle[m, 3 * a + b] for b in range(3)]) for a in range(3)], axis=0)
        for m in range(2)
    ]
    w2t = [
        flip(jnp.concatenate([beside([w_middle[m, 3 * a + b] for a in range(3)]) for b in range(3)], axis=0))
        for m in range(2)
    ]

    def arrived(kind, l, src, dst):
        pltpu.make_async_copy(src, dst, cr_sem.at[kind, l]).wait()

    for l in range(n_lon):
        @pl.when(lon != l)
        def _(l=l):
            arrived(0, l, send_buf.at[l], rx.at[l, pl.ds(HALO, rc)])

        @pl.when(lat > 0)
        def _(l=l):
            arrived(1, l, send_buf.at[l, pl.ds(0, HALO)], rx.at[l, pl.ds(0, HALO)])

        @pl.when(lat < n_lat - 1)
        def _(l=l):
            arrived(2, l, send_buf.at[l, pl.ds(0, HALO)], rx.at[l, pl.ds(HALO + rc, HALO)])

    def inside(g):
        return jnp.where(jnp.logical_and(g >= 0, g < nyc), 1.0, 0.0).astype(F32)

    def received(x):
        return jnp.concatenate([rx[l, x].astype(F32) for l in range(n_lon)], axis=-1)

    def three(v):
        return jnp.concatenate([shift_cols(v, 1), v, shift_cols(v, -1), jnp.zeros_like(v)], axis=0)

    for x in range(rc + 2 * HALO):
        s0[x] = three(received(x)).astype(BF16)

    for r in range(rc + 8):
        block = s0[r : r + 3].reshape(96, width)
        h = jnp.tanh(jnp.dot(w1, block, preferred_element_type=F32)) * inside(lat * rc - 4 + r)
        for m in range(2):
            hm = h[m * HID : (m + 1) * HID].astype(BF16)
            s1[m, r, 0:HID] = shift_cols(hm, 1)
            s1[m, r, HID : 2 * HID] = hm
            s1[m, r, 2 * HID : 3 * HID] = shift_cols(hm, -1)

    def taps(products, r, order):
        return sum(
            products[r + i][j * HID : (j + 1) * HID] for i, j in enumerate(order)
        )

    for m in range(2):
        products = [
            jnp.dot(w2[m], s1[m, x], preferred_element_type=F32) for x in range(rc + 8)
        ]
        for r in range(rc + 6):
            h = jnp.tanh(taps(products, r, (0, 1, 2))) * inside(lat * rc - 3 + r)
            h2s[r, m * HID : (m + 1) * HID] = h.astype(BF16)

    scale = 2.0 / (2.0 * LEV * nyc * width)
    sub = lax.broadcasted_iota(jnp.int32, (8, width), 0)
    outs = [jnp.dot(wl, h2s[x], preferred_element_type=F32) for x in range(rc + 6)]
    for r in range(rc + 4):
        u = [sum(outs[r + a][24 * a + 8 * b : 24 * a + 8 * b + 8] for a in range(3)) for b in range(3)]
        pred = shift_cols(u[0], 1) + u[1] + shift_cols(u[2], -1)
        g3 = jnp.where(sub >= 4, (pred - received(r + 3)) * scale, 0.0) * inside(lat * rc - 2 + r)
        g3s[r] = jnp.concatenate(
            [shift_cols(g3, -1), g3, shift_cols(g3, 1), jnp.zeros_like(g3)], axis=0
        ).astype(BF16)
        if 2 <= r < 2 + rc:
            both = pred[4:6] + pred[6:8]
            for o in range(2):
                pred_buf[o, r - 2 : r - 1, :] = both[o : o + 1]

    def force_copy(l, m):
        return pltpu.make_async_remote_copy(
            src_ref=pred_buf.at[:, :, pl.ds(l * cc, cc)], dst_ref=force_rx.at[mem, lon],
            send_sem=fs_sem.at[m, l], recv_sem=fr_sem.at[mem, lon],
            device_id=at(lat, l, m), device_id_type=MESH,
        )

    def force_own():
        return pltpu.make_async_copy(
            pred_buf.at[:, :, pl.ds(pl.multiple_of(lon * cc, cc), cc)], force_rx.at[mem, lon], fl_sem
        )

    def elsewhere(l, m):
        return jnp.logical_or(lon != l, mem != m)

    for m in range(n_mem):
        for l in range(n_lon):
            @pl.when(elsewhere(l, m))
            def _(l=l, m=m):
                force_copy(l, m).start()

    force_own().start()

    for r in range(rc + 2):
        block = g3s[r : r + 3].reshape(96, width)
        h = h2s[r + 2].astype(F32)
        d = jnp.dot(w3t, block, preferred_element_type=F32) * (1.0 - h * h)
        d = d * inside(lat * rc - 1 + r)
        for m in range(2):
            dm = d[m * HID : (m + 1) * HID].astype(BF16)
            d2s[m, r, 0:HID] = shift_cols(dm, -1)
            d2s[m, r, HID : 2 * HID] = dm
            d2s[m, r, 2 * HID : 3 * HID] = shift_cols(dm, 1)

    def over_rows(left, right):
        return lax.dot_general(
            beside([left(r) for r in range(rc)]), beside([right(r) for r in range(rc)]), NT,
            preferred_element_type=F32,
        )

    mids = [
        over_rows(
            lambda r: d2s[m, r + 1],
            lambda r: s1[m, r + 3 : r + 6, HID : 2 * HID].reshape(3 * HID, width),
        )
        for m in range(2)
    ]
    def put(start, value):
        for i in range(value.shape[0] // 8):
            side, row = place(start // 8 + i)
            partial[side, row : row + 8, :] = value[8 * i : 8 * i + 8]

    for a in range(3):
        put(a * 192, beside([mids[m][:, a * HID : (a + 1) * HID] for m in range(2)]))
    last = over_rows(lambda r: g3s[r + 1 : r + 4].reshape(96, width), lambda r: h2s[r + 3])
    for a in range(3):
        at_row = MID_ROWS + 24 * a
        put(at_row, last[32 * a : 32 * a + 24, :])

    def core_copy(which):
        start, size = ((0, split), (split, half - split))[which]
        return pltpu.make_async_remote_copy(
            src_ref=partial.at[1 - core, pl.ds(start, size)], dst_ref=theirs.at[pl.ds(start, size)],
            send_sem=cp_send.at[which], recv_sem=cp_recv.at[which],
            device_id=at(lat, partner, mem), device_id_type=MESH,
        )

    early = 8 * (EARLY - LOW_EARLY) // chunk
    split = early * chunk
    core_copy(0).start()
    if line > 1:
        pl.semaphore_wait(entered, line - 1)

    def piece(ref, index):
        return ref.at[pl.ds(pl.multiple_of(index * chunk, chunk), chunk)]

    def reduce_rows(which):
        core_copy(which).wait()
        start, count = ((0, early), (early, owners - early))[which]
        span = slice(start * chunk, (start + count) * chunk)
        halved[span, :] = partial[core, span, :] + theirs[span, :]

        def send(lat_to, z_to):
            to = turn_of(lat_to, z_to)
            wanted = jnp.logical_and(to >= start, to < start + count)

            @pl.when(jnp.logical_and(owns(lat_to), wanted))
            def _():
                pltpu.make_async_remote_copy(
                    src_ref=piece(halved, to), dst_ref=scattered.at[rank],
                    send_sem=rs_send, recv_sem=rs_recv,
                    device_id=of_plane(lat_to, z_to), device_id_type=MESH,
                ).start()

        around(send)

    d1s = []
    for m in range(2):
        products = [
            jnp.dot(w2t[m], d2s[m, x], preferred_element_type=F32) for x in range(rc + 2)
        ]
        own = []
        for r in range(rc):
            h = s1[m, r + 4, HID : 2 * HID].astype(F32)
            own.append((taps(products, r, (2, 1, 0)) * (1.0 - h * h)).astype(BF16))
        d1s.append(own)
        if m == 0:
            reduce_rows(0)
    first = over_rows(
        lambda r: s0[r + 4 : r + 7].reshape(96, width),
        lambda r: jnp.concatenate([d1s[0][r], d1s[1][r]], axis=0),
    )
    for a in range(3):
        at_row = MID_ROWS + SMALL_ROWS + 24 * a
        put(at_row, first[32 * a : 32 * a + 24, :])
    used = 8 * (EARLY - LOW_EARLY + SMALL_ROWS // 8 - LOW_LATE)
    if half > used:
        partial[1, used:, :] = jnp.zeros((half - used, 128), F32)
    core_copy(1).start()
    reduce_rows(1)

    def passed(ref, count, sem):
        pltpu.make_async_copy(ref.at[pl.ds(0, count)], ref.at[pl.ds(0, count)], sem).wait()

    @pl.when(is_owner)
    def _():
        passed(scattered, plane - 1, rs_recv)
        start = pl.multiple_of(turn * chunk, chunk)
        total = halved[pl.ds(start, chunk), :]
        for i in range(1, plane):
            total = total + scattered[lax.rem(rank + i, plane)]
        gathered[core, pl.ds(start, chunk), :] = total

        def spread(lat_to, z_to, sem):
            pltpu.make_async_remote_copy(
                src_ref=piece(gathered.at[core], turn), dst_ref=piece(gathered.at[core], turn),
                send_sem=ag_send, recv_sem=ag_recv.at[sem],
                device_id=of_plane(lat_to, z_to), device_id_type=MESH,
            ).start()

        @pl.when(turn < early)
        def _():
            around(functools.partial(spread, sem=0))

        @pl.when(turn >= early)
        def _():
            around(functools.partial(spread, sem=1))

    for m in range(n_mem):
        for l in range(n_lon):
            @pl.when(elsewhere(l, m))
            def _(l=l, m=m):
                pltpu.make_async_copy(
                    pred_buf.at[:, :, pl.ds(0, cc)], force_rx.at[m, l], fr_sem.at[m, l]
                ).wait()

    force_own().wait()

    @pl.when(lat > 0)
    def _():
        pltpu.make_async_copy(row_send.at[0], row_rx.at[0], or_sem.at[0]).wait()

    @pl.when(lat < n_lat - 1)
    def _():
        pltpu.make_async_copy(row_send.at[0], row_rx.at[1], or_sem.at[1]).wait()

    pltpu.make_async_copy(col_send.at[0], col_rx.at[0], or_sem.at[2]).wait()
    pltpu.make_async_copy(col_send.at[0], col_rx.at[1], or_sem.at[3]).wait()

    summed = force_rx[0]
    for m in range(1, n_mem):
        summed = summed + force_rx[m]
    mean = (summed * (1.0 / (2 * n_mem))).reshape(LEV * 2 * rc, cc)
    for r in range(COARSE):
        tall[pl.ds(r, LEV * 2 * rc, stride=COARSE), :] = mean
    force_up[...] = jnp.dot(
        tall[...], expand, precision=lax.Precision.HIGHEST, preferred_element_type=F32
    ).reshape(force_up.shape)
    for q in range(3 * LEV):
        pad[q, 7:8, :] = row_rx[0, q : q + 1, :]
        pad[q, 8 + rows : 9 + rows, :] = row_rx[1, q : q + 1, :]

    loads[4].wait()
    lane_ids = lax.broadcasted_iota(jnp.int32, (8, cols), 1)
    for s in range(rows // 8):
        base = 8 + 8 * s
        ids = (lat * rows + 8 * s + lax.broadcasted_iota(jnp.int32, (8, cols), 0)).astype(F32)
        coriolis = jnp.sin(-math.pi / 2 + math.pi * (ids + 0.5) / (rows * n_lat))
        wet = 0.1 * land[8 * s : 8 * s + 8, :].astype(F32)
        sum_x = jnp.zeros((8, cols), F32)
        sum_y = jnp.zeros((8, cols), F32)
        for l in range(LEV):
            got = []
            for c in range(3):
                q = c * LEV + l
                centre = pad[q, base : base + 8, :]
                south = pad[q, base - 1 : base + 7, :]
                north = pad[q, base + 1 : base + 9, :]
                before = col_rx[0, 8 * s : 8 * s + 8, q : q + 1]
                after = col_rx[1, 8 * s : 8 * s + 8, q : q + 1]
                west = jnp.where(lane_ids == 0, before, shift_cols(centre, 1))
                east = jnp.where(lane_ids == cols - 1, after, shift_cols(centre, -1))
                got.append((centre, east, west, north, south))
            laps = [e + w + n + so - 4.0 * ce for ce, e, w, n, so in got]
            u, v, t = got[0][0], got[1][0], got[2][0]
            dx = got[2][1] - got[2][2]
            dy = got[2][3] - got[2][4]
            sum_x = sum_x + dx
            sum_y = sum_y + dy
            fu = force_up[l * 2, 8 * s : 8 * s + 8, :]
            fv = force_up[l * 2 + 1, 8 * s : 8 * s + 8, :]
            velo_new[0, l, 8 * s : 8 * s + 8, :] = u + wet * (
                coriolis * v + 0.25 * sum_x + 0.5 * laps[0] + fu
            )
            velo_new[1, l, 8 * s : 8 * s + 8, :] = v + wet * (
                -coriolis * u + 0.25 * sum_y + 0.5 * laps[1] + fv
            )
            temp_new[l, 8 * s : 8 * s + 8, :] = t + wet * (
                -0.5 * (u * dx + v * dy) + 0.3 * laps[2]
            )

    stores = [
        pltpu.make_async_copy(velo_new, velo_out, out_sem.at[0]),
        pltpu.make_async_copy(temp_new, temp_out, out_sem.at[1]),
    ]
    for store in stores:
        store.start()

    def share(which):
        start, count = ((0, early), (early, owners - early))[which]
        span = pl.ds(start * chunk, count * chunk)
        inside_it = jnp.logical_and(is_owner, jnp.logical_and(turn >= start, turn < start + count))
        if count > 1:
            @pl.when(inside_it)
            def _():
                passed(halved, (count - 1) * chunk, ag_recv.at[which])

        @pl.when(jnp.logical_not(inside_it))
        def _():
            passed(halved, count * chunk, ag_recv.at[which])

        copy = pltpu.make_async_remote_copy(
            src_ref=gathered.at[core, span], dst_ref=gathered.at[core, span],
            send_sem=cp_send.at[2 + which], recv_sem=cp_recv.at[2 + which],
            device_id=at(lat, partner, mem), device_id_type=MESH,
        )
        copy.start()
        return copy, span

    shares = [share(0), share(1)]
    keep = pltpu.make_async_copy(gathered.at[core], grads.at[core], out_sem.at[2])
    keep.start()

    for store in stores:
        store.wait()
    for l in range(n_lon):
        @pl.when(lat < n_lat - 1)
        def _(l=l):
            up_copy(l).wait_send()

        @pl.when(lat > 0)
        def _(l=l):
            down_copy(l).wait_send()

        @pl.when(lon != l)
        def _(l=l):
            own_copy(l).wait_send()

        for m in range(n_mem):
            @pl.when(elsewhere(l, m))
            def _(l=l, m=m):
                force_copy(l, m).wait_send()

    @pl.when(lat < n_lat - 1)
    def _():
        row_up().wait_send()

    @pl.when(lat > 0)
    def _():
        row_down().wait_send()

    col_east().wait_send()
    col_west().wait_send()

    @pl.when(is_owner)
    def _():
        passed(halved, (owners - 1) * chunk, rs_send)
        passed(scattered, plane - 1, ag_send)

    @pl.when(jnp.logical_not(is_owner))
    def _():
        passed(halved, owners * chunk, rs_send)

    fetched = []
    for which, (copy, span) in enumerate(shares):
        copy.wait()
        fetched.append(
            pltpu.make_async_copy(
                gathered.at[1 - core, span], grads.at[1 - core, span], out_sem.at[3 + which]
            )
        )
        fetched[-1].start()
    keep.wait()
    for fetch in fetched:
        fetch.wait()


def finish(
    velo_in, temp_in, halves_in, velo_out, temp_out, first_out, middle_out, last_out,
    velo, temp, halves, first, middle, last, sems,
):
    load = pltpu.make_async_copy(halves_in, halves, sems.at[0])
    load.start()
    blocks = [(velo_in.at[c], velo.at[c], velo_out.at[c]) for c in range(2)]
    blocks.append((temp_in, temp, temp_out))
    moves = [pltpu.make_async_copy(b[0], b[1], sems.at[1 + i]) for i, b in enumerate(blocks)]
    for move in moves:
        move.start()
    load.wait()

    def rows_of(start, size, cols):
        side, row = place(start // 8)
        return halves[side, row + start % 8 : row + start % 8 + size, cols]

    stores = []
    for m in range(2):
        cols = slice(m * HID, (m + 1) * HID)
        for a in range(3):
            for b in range(3):
                k = 3 * a + b
                for i in range(HID // 8):
                    middle[m, k, 8 * i : 8 * i + 8] = rows_of(a * 192 + b * HID + 8 * i, 8, cols)
                at_row = MID_ROWS + (2 - a) * 24 + b * 8 + 4 + 2 * m
                last[m, k] = rows_of(at_row, 2, cols)
                for c in range(3):
                    at_row = MID_ROWS + SMALL_ROWS + a * 24 + b * 8 + c
                    first[k, c, m : m + 1, :] = rows_of(at_row, 1, cols)
        stores.append(pltpu.make_async_copy(middle.at[m], middle_out.at[m], sems.at[4 + m]))
        stores[-1].start()
    stores.append(pltpu.make_async_copy(first, first_out, sems.at[6]))
    stores.append(pltpu.make_async_copy(last, last_out, sems.at[7]))
    for store in stores[2:]:
        store.start()
    for i, (move, b) in enumerate(zip(moves, blocks)):
        move.wait()
        stores.append(pltpu.make_async_copy(b[1], b[2], sems.at[8 + i]))
        stores[-1].start()
    for store in stores:
        store.wait()


def per_device(n_lat, n_lon, n_mem, velo, temp, land, target, w_first, w_middle, w_last):
    rows, cols = temp.shape[1], temp.shape[2]
    rc, cc = rows // COARSE, cols // COARSE
    width = cc * n_lon
    plane = n_lat * (n_lon // 2)
    chunk, owners = chunking(n_lat, n_lon // 2)
    half = chunk * owners
    mine = w_first.shape[0]

    hbm = pl.BlockSpec(memory_space=pl.ANY)
    dma = pltpu.SemaphoreType.DMA
    fields = [jax.ShapeDtypeStruct(velo.shape, F32), jax.ShapeDtypeStruct(temp.shape, F32)]
    velo_next, temp_next, grads = pl.pallas_call(
        functools.partial(kernel, n_lat, n_lon, n_mem),
        out_shape=(*fields, jax.ShapeDtypeStruct((2, half, 128), F32)),
        in_specs=[hbm] * 7,
        out_specs=(hbm, hbm, hbm),
        scratch_shapes=[
            pltpu.VMEM(velo.shape, F32),
            pltpu.VMEM(temp.shape, F32),
            pltpu.VMEM(land.shape, jnp.int32),
            pltpu.VMEM(target.shape, BF16),
            pltpu.VMEM((9, 3, mine, HID), BF16),
            pltpu.VMEM(w_middle.shape, BF16),
            pltpu.VMEM(w_last.shape, BF16),
            pltpu.VMEM((LEV * rows, cc), F32),
            pltpu.VMEM((LEV * 2 * rows, cc), F32),
            pltpu.VMEM((LEV * rc * 8, cc), F32),
            pltpu.VMEM((LEV, rc, 8, cc), BF16),
            pltpu.VMEM((n_lon, rc + 2 * HALO, 8, cc), BF16),
            pltpu.VMEM((rc + 2 * HALO, 32, width), BF16),
            pltpu.VMEM((2, rc + 8, 3 * HID, width), BF16),
            pltpu.VMEM((rc + 6, 2 * HID, width), BF16),
            pltpu.VMEM((rc + 4, 32, width), BF16),
            pltpu.VMEM((2, rc + 2, 3 * HID, width), BF16),
            pltpu.VMEM((2, rc, width), F32),
            pltpu.VMEM((n_mem, n_lon, 2, rc, cc), F32),
            pltpu.VMEM((LEV * 2, rows, cols), F32),
            pltpu.VMEM((3 * LEV, rows + 16, cols), F32),
            pltpu.VMEM((2, 16, cols), F32),
            pltpu.VMEM((2, 16, cols), F32),
            pltpu.VMEM((2, rows, 128), F32),
            pltpu.VMEM((2, rows, 128), F32),
            pltpu.VMEM((96, 128), F32),
            pltpu.VMEM((72, 128), F32),
            pltpu.VMEM((2, half, 128), F32),
            pltpu.VMEM((half, 128), F32),
            pltpu.VMEM((half, 128), F32),
            pltpu.VMEM((plane, chunk, 128), F32),
            pltpu.VMEM((2, half, 128), F32),
            dma((8,)),
            dma((5,)),
            pltpu.SemaphoreType.REGULAR,
            dma((4,)),
            dma((4,)),
            dma((3, n_lon)),
            dma((3, n_lon)),
            dma((4,)),
            dma((4,)),
            dma((n_mem, n_lon)),
            dma((n_mem, n_lon)),
            dma,
            dma,
            dma,
            dma,
            dma((2,)),
        ],
        compiler_params=pltpu.CompilerParams(
            collective_id=0, has_side_effects=True, vmem_limit_bytes=56 * 1024 * 1024
        ),
        name="ocean_step",
    )(velo, temp, land, target, jnp.transpose(w_first, (1, 3, 0, 2)), w_middle, w_last)
    velo_next, temp_next, first, middle, last = pl.pallas_call(
        finish,
        out_shape=(
            *fields,
            jax.ShapeDtypeStruct((9, 3, mine, HID), F32),
            jax.ShapeDtypeStruct(w_middle.shape, F32),
            jax.ShapeDtypeStruct(w_last.shape, F32),
        ),
        in_specs=[hbm] * 3,
        out_specs=(hbm,) * 5,
        scratch_shapes=[
            pltpu.VMEM(velo.shape, F32),
            pltpu.VMEM(temp.shape, F32),
            pltpu.VMEM((2, half, 128), F32),
            pltpu.VMEM((9, 3, mine, HID), F32),
            pltpu.VMEM(w_middle.shape, F32),
            pltpu.VMEM(w_last.shape, F32),
            dma((11,)),
        ],
        name="finish",
    )(velo_next, temp_next, grads)
    return (velo_next, temp_next, jnp.transpose(first, (2, 0, 3, 1)), middle, last)


def solution(mesh):
    return jax.shard_map(
        functools.partial(per_device, mesh.shape["lat"], mesh.shape["lon"], mesh.shape["mem"]),
        mesh=mesh,
        in_specs=(
            P(None, None, "lat", "lon"),
            P(None, "lat", "lon"),
            P("lat", "lon"),
            P(None, None, "lat", "lon"),
            P("mem", None, None, None),
            P("mem", None, None, None),
            P("mem", None, None, None),
        ),
        out_specs=(
            P(None, None, "lat", "lon"),
            P(None, "lat", "lon"),
            P("mem", None, None, None),
            P("mem", None, None, None),
            P("mem", None, None, None),
        ),
        check_vma=False,
    )
```

```python
import functools
import math

import jax
import jax.numpy as jnp
from jax import lax
from jax.experimental import pallas as pl
from jax.experimental.pallas import tpu as pltpu
from jax.sharding import PartitionSpec as P

LEV = 4
COARSE = 4
HID = 64
HALO = 5
MESH = pl.DeviceIdType.MESH
F32 = jnp.float32
BF16 = jnp.bfloat16
MID_ROWS = 9 * HID
SMALL_ROWS = 72
GRAD_ROWS = MID_ROWS + 2 * SMALL_ROWS
NT = (((1,), (1,)), ((), ()))


def chunking(n_lat, planes):
    tiles = -(-GRAD_ROWS // 16)
    owners = (n_lat // 4 * 3 if n_lat % 4 == 0 else n_lat) * planes
    return -(-tiles // owners) * 8, owners


EARLY = (MID_ROWS + SMALL_ROWS) // 8
LOW_EARLY, LOW_LATE = (EARLY + 1) // 2, (SMALL_ROWS // 8 + 1) // 2


def place(tile):
    if tile < EARLY:
        return divmod_half(tile, LOW_EARLY, 0, 0)
    return divmod_half(tile - EARLY, LOW_LATE, LOW_EARLY, EARLY - LOW_EARLY)


def divmod_half(tile, low, base_low, base_high):
    return (0, 8 * (base_low + tile)) if tile < low else (1, 8 * (base_high + tile - low))


def shift_cols(value, by):
    return pltpu.roll(value, by % value.shape[-1], axis=value.ndim - 1)


def kernel(
    n_lat, n_lon, n_mem,
    velo_in, temp_in, land_in, target_in, first_in, middle_in, last_in,
    velo_out, temp_out, grads,
    velo_new, temp_new, land, target, w_first, w_middle, w_last,
    narrow, tall, staged, send_buf, rx, s0, s1, h2s, g3s, d2s, pred_buf, force_rx, force_up, pad,
    row_send, row_rx, col_send, col_rx, w1_rows, wl_rows, partial, theirs, halved, scattered, gathered,
    in_sem, out_sem,
    entered, cp_send, cp_recv, cs_sem, cr_sem, os_sem, or_sem, fs_sem, fr_sem, fl_sem, rs_send, rs_recv, ag_send, ag_recv,
):
    lat = lax.axis_index("lat")
    lon = lax.axis_index("lon")
    mem = lax.axis_index("mem")
    rows = temp_in.shape[1]
    cols = temp_in.shape[2]
    rc = rows // COARSE
    cc = cols // COARSE
    width = cc * n_lon
    nyc = rc * n_lat
    planes = n_lon // 2
    plane = n_lat * planes
    chunk, owners = chunking(n_lat, planes)
    half = chunk * owners
    core = lax.rem(lon, 2)
    partner = lon + 1 - 2 * core
    place_z = lax.div(lon, 2)
    rank = lat * planes + place_z

    def owns(lat_of):
        return lax.rem(lat_of, 4) != 3 if n_lat % 4 == 0 else lat_of >= 0

    def turn_of(lat_of, z_of):
        return (lat_of - lax.div(lat_of, 4) if n_lat % 4 == 0 else lat_of) * planes + z_of

    turn = turn_of(lat, place_z)
    is_owner = owns(lat)

    def wrapped(value, size):
        return jnp.where(value >= size, value - size, value)

    def around(which):
        for i in list(range(1, n_lat)) + [0]:
            for k in range(planes):
                z = wrapped(place_z + (k + 1 if i == 0 else k), planes)
                if i > 0 or k < planes - 1:
                    which(wrapped(lat + i, n_lat), z)

    def at(lat_to, lon_to, mem_to):
        return {"lat": lat_to, "lon": lon_to, "mem": mem_to}

    inner = pl.ds(8, rows)
    loads = [
        pltpu.make_async_copy(velo_in.at[c], pad.at[pl.ds(c * LEV, LEV), inner], in_sem.at[c])
        for c in range(2)
    ]
    loads.append(
        pltpu.make_async_copy(temp_in, pad.at[pl.ds(2 * LEV, LEV), inner], in_sem.at[2])
    )
    loads.append(pltpu.make_async_copy(target_in, target, in_sem.at[3]))
    loads.append(pltpu.make_async_copy(land_in, land, in_sem.at[4]))
    loads.append(pltpu.make_async_copy(first_in, w_first, in_sem.at[5]))
    loads.append(pltpu.make_async_copy(middle_in, w_middle, in_sem.at[6]))
    loads.append(pltpu.make_async_copy(last_in, w_last, in_sem.at[7]))
    for load in loads:
        load.start()

    def of_plane(lat_to, z_to):
        return at(lat_to, 2 * z_to + core, mem)

    barrier = pltpu.get_barrier_semaphore()

    def greet(device):
        pl.semaphore_signal(barrier, inc=1, device_id=device, device_id_type=MESH)

    line = 4 if n_lat % 4 == 0 else n_lat
    line_start = lax.div(lat, line) * line
    greeted = 0
    for i in range(line, n_lat, line):
        for z in range(planes):
            greet(of_plane(wrapped(lat + i, n_lat), z))
            greeted += 1
    for i in range(1, line):
        for z in range(planes):
            greet(of_plane(line_start + wrapped(lat - line_start + i, line), z))
            greeted += 1
    for i in range(1, n_lon):
        greet(at(lat, wrapped(lon + i, n_lon), mem))
        greeted += 1
    for i in range(1, n_mem):
        for l in range(n_lon):
            greet(at(lat, l, wrapped(mem + i, n_mem)))
            greeted += 1

    @pl.when(lat > 0)
    def _():
        for l in range(n_lon):
            greet(at(lat - 1, l, mem))

    @pl.when(lat < n_lat - 1)
    def _():
        for l in range(n_lon):
            greet(at(lat + 1, l, mem))

    greeted = greeted + jnp.where(lat > 0, n_lon, 0) + jnp.where(lat < n_lat - 1, n_lon, 0)

    q_ids = lax.broadcasted_iota(jnp.int32, (cc, cols), 0)
    i_ids = lax.broadcasted_iota(jnp.int32, (cc, cols), 1)
    expand = jnp.where(i_ids // COARSE == q_ids, 1.0, 0.0).astype(F32)

    staged[...] = jnp.zeros_like(staged)
    for c in range(3):
        loads[c].wait()
        fine = pad[c * LEV : (c + 1) * LEV, 8 : 8 + rows, :].reshape(LEV * rows, cols)
        fine = fine * (1.0 / COARSE**2)
        high = fine.astype(BF16)
        rest = fine - high.astype(F32)
        middle = rest.astype(BF16)
        low = (rest - middle.astype(F32)).astype(BF16)
        parts = lax.dot_general(
            jnp.concatenate([high, middle, low], axis=0), expand.astype(BF16), NT,
            preferred_element_type=F32,
        )
        n = LEV * rows
        narrow[...] = parts[0:n] + parts[n : 2 * n] + parts[2 * n : 3 * n]
        pooled = narrow[pl.ds(0, LEV * rc, stride=COARSE), :]
        for r in range(1, COARSE):
            pooled = pooled + narrow[pl.ds(r, LEV * rc, stride=COARSE), :]
        staged[pl.ds(c, LEV * rc, stride=8), :] = pooled
    loads[3].wait()
    for c in range(2):
        goal = target[c].astype(F32).reshape(LEV * rc, cc)
        staged[pl.ds(4 + c, LEV * rc, stride=8), :] = goal
        staged[pl.ds(6 + c, LEV * rc, stride=8), :] = goal
    send_buf[...] = staged[...].astype(BF16).reshape(send_buf.shape)

    @pl.when(lat == 0)
    def _():
        rx[:, 0:HALO] = jnp.zeros((n_lon, HALO, 8, cc), BF16)
        row_rx[0] = jnp.zeros_like(row_rx[0])

    @pl.when(lat == n_lat - 1)
    def _():
        rx[:, HALO + rc : 2 * HALO + rc] = jnp.zeros((n_lon, HALO, 8, cc), BF16)
        row_rx[1] = jnp.zeros_like(row_rx[1])

    pl.semaphore_wait(barrier, greeted)

    def own_copy(l):
        return pltpu.make_async_remote_copy(
            src_ref=send_buf.at[l], dst_ref=rx.at[lon, pl.ds(HALO, rc)],
            send_sem=cs_sem.at[0, l], recv_sem=cr_sem.at[0, lon],
            device_id=at(lat, l, mem), device_id_type=MESH,
        )

    def up_copy(l):
        return pltpu.make_async_remote_copy(
            src_ref=send_buf.at[l, pl.ds(rc - HALO, HALO)], dst_ref=rx.at[lon, pl.ds(0, HALO)],
            send_sem=cs_sem.at[1, l], recv_sem=cr_sem.at[1, lon],
            device_id=at(lat + 1, l, mem), device_id_type=MESH,
        )

    def down_copy(l):
        return pltpu.make_async_remote_copy(
            src_ref=send_buf.at[l, pl.ds(0, HALO)], dst_ref=rx.at[lon, pl.ds(HALO + rc, HALO)],
            send_sem=cs_sem.at[2, l], recv_sem=cr_sem.at[2, lon],
            device_id=at(lat - 1, l, mem), device_id_type=MESH,
        )

    def row_up():
        return pltpu.make_async_remote_copy(
            src_ref=row_send.at[1], dst_ref=row_rx.at[0], send_sem=os_sem.at[0], recv_sem=or_sem.at[0],
            device_id=at(lat + 1, lon, mem), device_id_type=MESH,
        )

    def row_down():
        return pltpu.make_async_remote_copy(
            src_ref=row_send.at[0], dst_ref=row_rx.at[1], send_sem=os_sem.at[1], recv_sem=or_sem.at[1],
            device_id=at(lat - 1, lon, mem), device_id_type=MESH,
        )

    def col_east():
        return pltpu.make_async_remote_copy(
            src_ref=col_send.at[1], dst_ref=col_rx.at[0], send_sem=os_sem.at[2], recv_sem=or_sem.at[2],
            device_id=at(lat, lax.rem(lon + 1, n_lon), mem), device_id_type=MESH,
        )

    def col_west():
        return pltpu.make_async_remote_copy(
            src_ref=col_send.at[0], dst_ref=col_rx.at[1], send_sem=os_sem.at[3], recv_sem=or_sem.at[3],
            device_id=at(lat, lax.rem(lon + n_lon - 1, n_lon), mem), device_id_type=MESH,
        )

    for l in range(n_lon):
        @pl.when(lat < n_lat - 1)
        def _(l=l):
            up_copy(l).start()

        @pl.when(lat > 0)
        def _(l=l):
            down_copy(l).start()

        @pl.when(lon != l)
        def _(l=l):
            own_copy(l).start()

    for i in range(1, line):
        pl.semaphore_signal(
            entered, inc=1,
            device_id=of_plane(line_start + wrapped(lat - line_start + i, line), place_z),
            device_id_type=MESH,
        )

    lane = lax.broadcasted_iota(jnp.int32, (rows, 128), 1)
    west_cols = jnp.zeros((rows, 128), F32)
    east_cols = jnp.zeros((rows, 128), F32)
    for q in range(3 * LEV):
        first = pad[q, 8 : 8 + rows, 0:128]
        last = pad[q, 8 : 8 + rows, cols - 128 : cols]
        west_cols = jnp.where(lane == q, jnp.broadcast_to(first[:, 0:1], (rows, 128)), west_cols)
        east_cols = jnp.where(lane == q, jnp.broadcast_to(last[:, 127:128], (rows, 128)), east_cols)
        row_send[0, q : q + 1, :] = pad[q, 8:9, :]
        row_send[1, q : q + 1, :] = pad[q, 7 + rows : 8 + rows, :]
    col_send[0] = west_cols
    col_send[1] = east_cols

    @pl.when(lat < n_lat - 1)
    def _():
        row_up().start()

    @pl.when(lat > 0)
    def _():
        row_down().start()

    col_east().start()
    col_west().start()

    rx[lon, HALO : HALO + rc] = send_buf[lon]
    def flip(matrix):
        size = matrix.shape[1]
        eye = jnp.where(
            lax.broadcasted_iota(jnp.int32, (size, size), 0)
            == lax.broadcasted_iota(jnp.int32, (size, size), 1),
            1.0, 0.0,
        ).astype(BF16)
        return lax.dot_general(eye, matrix, NT, preferred_element_type=F32).astype(BF16)

    def beside(blocks):
        return jnp.concatenate(blocks, axis=1)

    for load in loads[5:]:
        load.wait()
    w1_rows[...] = jnp.zeros_like(w1_rows)
    wl_rows[...] = jnp.zeros_like(wl_rows)
    for a in range(3):
        for b in range(3):
            k = 3 * a + b
            for c in range(3):
                pair = w_first[k, c].astype(F32)
                for m in range(2):
                    at_row = a * 32 + b * 8 + c
                    w1_rows[at_row : at_row + 1, m * HID : (m + 1) * HID] = pair[m : m + 1]
            for m in range(2):
                at_row = a * 24 + b * 8 + 4 + 2 * m
                wl_rows[at_row : at_row + 2, m * HID : (m + 1) * HID] = w_last[m, k].astype(F32)
    w1 = flip(w1_rows[...].astype(BF16))
    wl = wl_rows[...].astype(BF16)
    gap = jnp.zeros((8, 2 * HID), F32)
    w3 = jnp.concatenate([p for t in (2, 1, 0) for p in (wl_rows[24 * t : 24 * t + 24, :], gap)], axis=0)
    w3t = flip(w3.astype(BF16))
    w2 = [
        jnp.concatenate([beside([w_middle[m, 3 * a + b] for b in range(3)]) for a in range(3)], axis=0)
        for m in range(2)
    ]
    w2t = [
        flip(jnp.concatenate([beside([w_middle[m, 3 * a + b] for a in range(3)]) for b in range(3)], axis=0))
        for m in range(2)
    ]

    def arrived(kind, l, src, dst):
        pltpu.make_async_copy(src, dst, cr_sem.at[kind, l]).wait()

    for l in range(n_lon):
        @pl.when(lon != l)
        def _(l=l):
            arrived(0, l, send_buf.at[l], rx.at[l, pl.ds(HALO, rc)])

        @pl.when(lat > 0)
        def _(l=l):
            arrived(1, l, send_buf.at[l, pl.ds(0, HALO)], rx.at[l, pl.ds(0, HALO)])

        @pl.when(lat < n_lat - 1)
        def _(l=l):
            arrived(2, l, send_buf.at[l, pl.ds(0, HALO)], rx.at[l, pl.ds(HALO + rc, HALO)])

    def inside(g):
        return jnp.where(jnp.logical_and(g >= 0, g < nyc), 1.0, 0.0).astype(F32)

    def only_inside(value, r, above):
        return value if above <= r < above + rc else value * inside(lat * rc - above + r)

    def received(x):
        return jnp.concatenate([rx[l, x].astype(F32) for l in range(n_lon)], axis=-1)

    def three(v):
        return jnp.concatenate([shift_cols(v, 1), v, shift_cols(v, -1), jnp.zeros_like(v)], axis=0)

    for x in range(rc + 2 * HALO):
        s0[x] = three(received(x)).astype(BF16)

    for r in range(rc + 8):
        block = s0[r : r + 3].reshape(96, width)
        h = only_inside(jnp.tanh(jnp.dot(w1, block, preferred_element_type=F32)), r, 4)
        for m in range(2):
            hm = h[m * HID : (m + 1) * HID].astype(BF16)
            s1[m, r, 0:HID] = shift_cols(hm, 1)
            s1[m, r, HID : 2 * HID] = hm
            s1[m, r, 2 * HID : 3 * HID] = shift_cols(hm, -1)

    def taps(products, r, order):
        return sum(
            products[r + i][j * HID : (j + 1) * HID] for i, j in enumerate(order)
        )

    for m in range(2):
        products = [
            jnp.dot(w2[m], s1[m, x], preferred_element_type=F32) for x in range(rc + 8)
        ]
        for r in range(rc + 6):
            h = only_inside(jnp.tanh(taps(products, r, (0, 1, 2))), r, 3)
            h2s[r, m * HID : (m + 1) * HID] = h.astype(BF16)

    scale = 2.0 / (2.0 * LEV * nyc * width)
    sub = lax.broadcasted_iota(jnp.int32, (8, width), 0)
    outs = [jnp.dot(wl, h2s[x], preferred_element_type=F32) for x in range(rc + 6)]
    for r in range(rc + 4):
        u = [sum(outs[r + a][24 * a + 8 * b : 24 * a + 8 * b + 8] for a in range(3)) for b in range(3)]
        pred = shift_cols(u[0], 1) + u[1] + shift_cols(u[2], -1)
        g3 = only_inside(jnp.where(sub >= 4, (pred - received(r + 3)) * scale, 0.0), r, 2)
        g3s[r] = jnp.concatenate(
            [shift_cols(g3, -1), g3, shift_cols(g3, 1), jnp.zeros_like(g3)], axis=0
        ).astype(BF16)
        if 2 <= r < 2 + rc:
            both = pred[4:6] + pred[6:8]
            for o in range(2):
                pred_buf[o, r - 2 : r - 1, :] = both[o : o + 1]

    def force_copy(l, m):
        return pltpu.make_async_remote_copy(
            src_ref=pred_buf.at[:, :, pl.ds(l * cc, cc)], dst_ref=force_rx.at[mem, lon],
            send_sem=fs_sem.at[m, l], recv_sem=fr_sem.at[mem, lon],
            device_id=at(lat, l, m), device_id_type=MESH,
        )

    def force_own():
        return pltpu.make_async_copy(
            pred_buf.at[:, :, pl.ds(pl.multiple_of(lon * cc, cc), cc)], force_rx.at[mem, lon], fl_sem
        )

    def elsewhere(l, m):
        return jnp.logical_or(lon != l, mem != m)

    for m in range(n_mem):
        for l in range(n_lon):
            @pl.when(elsewhere(l, m))
            def _(l=l, m=m):
                force_copy(l, m).start()

    force_own().start()

    for r in range(rc + 2):
        block = g3s[r : r + 3].reshape(96, width)
        h = h2s[r + 2].astype(F32)
        d = jnp.dot(w3t, block, preferred_element_type=F32) * (1.0 - h * h)
        d = only_inside(d, r, 1)
        for m in range(2):
            dm = d[m * HID : (m + 1) * HID].astype(BF16)
            d2s[m, r, 0:HID] = shift_cols(dm, -1)
            d2s[m, r, HID : 2 * HID] = dm
            d2s[m, r, 2 * HID : 3 * HID] = shift_cols(dm, 1)

    def over_rows(left, right):
        return lax.dot_general(
            beside([left(r) for r in range(rc)]), beside([right(r) for r in range(rc)]), NT,
            preferred_element_type=F32,
        )

    mids = [
        over_rows(
            lambda r: d2s[m, r + 1],
            lambda r: s1[m, r + 3 : r + 6, HID : 2 * HID].reshape(3 * HID, width),
        )
        for m in range(2)
    ]
    def put(start, value):
        for i in range(value.shape[0] // 8):
            side, row = place(start // 8 + i)
            partial[side, row : row + 8, :] = value[8 * i : 8 * i + 8]

    for a in range(3):
        put(a * 192, beside([mids[m][:, a * HID : (a + 1) * HID] for m in range(2)]))
    last = over_rows(lambda r: g3s[r + 1 : r + 4].reshape(96, width), lambda r: h2s[r + 3])
    for a in range(3):
        at_row = MID_ROWS + 24 * a
        put(at_row, last[32 * a : 32 * a + 24, :])

    def core_copy(which):
        start, size = ((0, split), (split, half - split))[which]
        return pltpu.make_async_remote_copy(
            src_ref=partial.at[1 - core, pl.ds(start, size)], dst_ref=theirs.at[pl.ds(start, size)],
            send_sem=cp_send.at[which], recv_sem=cp_recv.at[which],
            device_id=at(lat, partner, mem), device_id_type=MESH,
        )

    early = 8 * (EARLY - LOW_EARLY) // chunk
    split = early * chunk
    core_copy(0).start()
    if line > 1:
        pl.semaphore_wait(entered, line - 1)

    def piece(ref, index):
        return ref.at[pl.ds(pl.multiple_of(index * chunk, chunk), chunk)]

    def reduce_rows(which):
        core_copy(which).wait()
        start, count = ((0, early), (early, owners - early))[which]
        span = slice(start * chunk, (start + count) * chunk)
        halved[span, :] = partial[core, span, :] + theirs[span, :]

        def send(lat_to, z_to):
            to = turn_of(lat_to, z_to)
            wanted = jnp.logical_and(to >= start, to < start + count)

            @pl.when(jnp.logical_and(owns(lat_to), wanted))
            def _():
                pltpu.make_async_remote_copy(
                    src_ref=piece(halved, to), dst_ref=scattered.at[rank],
                    send_sem=rs_send, recv_sem=rs_recv,
                    device_id=of_plane(lat_to, z_to), device_id_type=MESH,
                ).start()

        around(send)

    d1s = []
    for m in range(2):
        products = [
            jnp.dot(w2t[m], d2s[m, x], preferred_element_type=F32) for x in range(rc + 2)
        ]
        own = []
        for r in range(rc):
            h = s1[m, r + 4, HID : 2 * HID].astype(F32)
            own.append((taps(products, r, (2, 1, 0)) * (1.0 - h * h)).astype(BF16))
        d1s.append(own)
        if m == 0:
            reduce_rows(0)
    first = over_rows(
        lambda r: s0[r + 4 : r + 7].reshape(96, width),
        lambda r: jnp.concatenate([d1s[0][r], d1s[1][r]], axis=0),
    )
    for a in range(3):
        at_row = MID_ROWS + SMALL_ROWS + 24 * a
        put(at_row, first[32 * a : 32 * a + 24, :])
    used = 8 * (EARLY - LOW_EARLY + SMALL_ROWS // 8 - LOW_LATE)
    if half > used:
        partial[1, used:, :] = jnp.zeros((half - used, 128), F32)
    core_copy(1).start()
    reduce_rows(1)

    def passed(ref, count, sem):
        pltpu.make_async_copy(ref.at[pl.ds(0, count)], ref.at[pl.ds(0, count)], sem).wait()

    @pl.when(is_owner)
    def _():
        passed(scattered, plane - 1, rs_recv)
        start = pl.multiple_of(turn * chunk, chunk)
        total = halved[pl.ds(start, chunk), :]
        for i in range(1, plane):
            total = total + scattered[lax.rem(rank + i, plane)]
        gathered[core, pl.ds(start, chunk), :] = total

        def spread(lat_to, z_to, sem):
            pltpu.make_async_remote_copy(
                src_ref=piece(gathered.at[core], turn), dst_ref=piece(gathered.at[core], turn),
                send_sem=ag_send, recv_sem=ag_recv.at[sem],
                device_id=of_plane(lat_to, z_to), device_id_type=MESH,
            ).start()

        @pl.when(turn < early)
        def _():
            around(functools.partial(spread, sem=0))

        @pl.when(turn >= early)
        def _():
            around(functools.partial(spread, sem=1))

    for m in range(n_mem):
        for l in range(n_lon):
            @pl.when(elsewhere(l, m))
            def _(l=l, m=m):
                pltpu.make_async_copy(
                    pred_buf.at[:, :, pl.ds(0, cc)], force_rx.at[m, l], fr_sem.at[m, l]
                ).wait()

    force_own().wait()

    @pl.when(lat > 0)
    def _():
        pltpu.make_async_copy(row_send.at[0], row_rx.at[0], or_sem.at[0]).wait()

    @pl.when(lat < n_lat - 1)
    def _():
        pltpu.make_async_copy(row_send.at[0], row_rx.at[1], or_sem.at[1]).wait()

    pltpu.make_async_copy(col_send.at[0], col_rx.at[0], or_sem.at[2]).wait()
    pltpu.make_async_copy(col_send.at[0], col_rx.at[1], or_sem.at[3]).wait()

    summed = force_rx[0]
    for m in range(1, n_mem):
        summed = summed + force_rx[m]
    mean = (summed * (1.0 / (2 * n_mem))).reshape(LEV * 2 * rc, cc)
    for r in range(COARSE):
        tall[pl.ds(r, LEV * 2 * rc, stride=COARSE), :] = mean
    force_up[...] = jnp.dot(
        tall[...], expand, precision=lax.Precision.HIGHEST, preferred_element_type=F32
    ).reshape(force_up.shape)
    for q in range(3 * LEV):
        pad[q, 7:8, :] = row_rx[0, q : q + 1, :]
        pad[q, 8 + rows : 9 + rows, :] = row_rx[1, q : q + 1, :]

    loads[4].wait()
    lane_ids = lax.broadcasted_iota(jnp.int32, (8, cols), 1)
    for s in range(rows // 8):
        base = 8 + 8 * s
        ids = (lat * rows + 8 * s + lax.broadcasted_iota(jnp.int32, (8, cols), 0)).astype(F32)
        coriolis = jnp.sin(-math.pi / 2 + math.pi * (ids + 0.5) / (rows * n_lat))
        wet = 0.1 * land[8 * s : 8 * s + 8, :].astype(F32)
        sum_x = jnp.zeros((8, cols), F32)
        sum_y = jnp.zeros((8, cols), F32)
        for l in range(LEV):
            got = []
            for c in range(3):
                q = c * LEV + l
                centre = pad[q, base : base + 8, :]
                south = pad[q, base - 1 : base + 7, :]
                north = pad[q, base + 1 : base + 9, :]
                before = col_rx[0, 8 * s : 8 * s + 8, q : q + 1]
                after = col_rx[1, 8 * s : 8 * s + 8, q : q + 1]
                west = jnp.where(lane_ids == 0, before, shift_cols(centre, 1))
                east = jnp.where(lane_ids == cols - 1, after, shift_cols(centre, -1))
                got.append((centre, east, west, north, south))
            laps = [e + w + n + so - 4.0 * ce for ce, e, w, n, so in got]
            u, v, t = got[0][0], got[1][0], got[2][0]
            dx = got[2][1] - got[2][2]
            dy = got[2][3] - got[2][4]
            sum_x = sum_x + dx
            sum_y = sum_y + dy
            fu = force_up[l * 2, 8 * s : 8 * s + 8, :]
            fv = force_up[l * 2 + 1, 8 * s : 8 * s + 8, :]
            velo_new[0, l, 8 * s : 8 * s + 8, :] = u + wet * (
                coriolis * v + 0.25 * sum_x + 0.5 * laps[0] + fu
            )
            velo_new[1, l, 8 * s : 8 * s + 8, :] = v + wet * (
                -coriolis * u + 0.25 * sum_y + 0.5 * laps[1] + fv
            )
            temp_new[l, 8 * s : 8 * s + 8, :] = t + wet * (
                -0.5 * (u * dx + v * dy) + 0.3 * laps[2]
            )

    stores = [
        pltpu.make_async_copy(velo_new, velo_out, out_sem.at[0]),
        pltpu.make_async_copy(temp_new, temp_out, out_sem.at[1]),
    ]
    for store in stores:
        store.start()

    def share(which):
        start, count = ((0, early), (early, owners - early))[which]
        span = pl.ds(start * chunk, count * chunk)
        inside_it = jnp.logical_and(is_owner, jnp.logical_and(turn >= start, turn < start + count))
        if count > 1:
            @pl.when(inside_it)
            def _():
                passed(halved, (count - 1) * chunk, ag_recv.at[which])

        @pl.when(jnp.logical_not(inside_it))
        def _():
            passed(halved, count * chunk, ag_recv.at[which])

        copy = pltpu.make_async_remote_copy(
            src_ref=gathered.at[core, span], dst_ref=gathered.at[core, span],
            send_sem=cp_send.at[2 + which], recv_sem=cp_recv.at[2 + which],
            device_id=at(lat, partner, mem), device_id_type=MESH,
        )
        copy.start()
        return copy, span

    shares = [share(0), share(1)]
    keep = pltpu.make_async_copy(gathered.at[core], grads.at[core], out_sem.at[2])
    keep.start()

    for store in stores:
        store.wait()
    for l in range(n_lon):
        @pl.when(lat < n_lat - 1)
        def _(l=l):
            up_copy(l).wait_send()

        @pl.when(lat > 0)
        def _(l=l):
            down_copy(l).wait_send()

        @pl.when(lon != l)
        def _(l=l):
            own_copy(l).wait_send()

        for m in range(n_mem):
            @pl.when(elsewhere(l, m))
            def _(l=l, m=m):
                force_copy(l, m).wait_send()

    @pl.when(lat < n_lat - 1)
    def _():
        row_up().wait_send()

    @pl.when(lat > 0)
    def _():
        row_down().wait_send()

    col_east().wait_send()
    col_west().wait_send()

    @pl.when(is_owner)
    def _():
        passed(halved, (owners - 1) * chunk, rs_send)
        passed(scattered, plane - 1, ag_send)

    @pl.when(jnp.logical_not(is_owner))
    def _():
        passed(halved, owners * chunk, rs_send)

    fetched = []
    for which, (copy, span) in enumerate(shares):
        copy.wait()
        fetched.append(
            pltpu.make_async_copy(
                gathered.at[1 - core, span], grads.at[1 - core, span], out_sem.at[3 + which]
            )
        )
        fetched[-1].start()
    keep.wait()
    for fetch in fetched:
        fetch.wait()


def finish(
    velo_in, temp_in, halves_in, velo_out, temp_out, first_out, middle_out, last_out,
    velo, temp, halves, first, middle, last, sems,
):
    load = pltpu.make_async_copy(halves_in, halves, sems.at[0])
    load.start()
    blocks = [(velo_in.at[c], velo.at[c], velo_out.at[c]) for c in range(2)]
    blocks.append((temp_in, temp, temp_out))
    moves = [pltpu.make_async_copy(b[0], b[1], sems.at[1 + i]) for i, b in enumerate(blocks)]
    for move in moves:
        move.start()
    load.wait()

    def rows_of(start, size, cols):
        side, row = place(start // 8)
        return halves[side, row + start % 8 : row + start % 8 + size, cols]

    stores = []
    for m in range(2):
        cols = slice(m * HID, (m + 1) * HID)
        for a in range(3):
            for b in range(3):
                k = 3 * a + b
                for i in range(HID // 8):
                    middle[m, k, 8 * i : 8 * i + 8] = rows_of(a * 192 + b * HID + 8 * i, 8, cols)
                at_row = MID_ROWS + (2 - a) * 24 + b * 8 + 4 + 2 * m
                last[m, k] = rows_of(at_row, 2, cols)
                for c in range(3):
                    at_row = MID_ROWS + SMALL_ROWS + a * 24 + b * 8 + c
                    first[k, c, m : m + 1, :] = rows_of(at_row, 1, cols)
        stores.append(pltpu.make_async_copy(middle.at[m], middle_out.at[m], sems.at[4 + m]))
        stores[-1].start()
    stores.append(pltpu.make_async_copy(first, first_out, sems.at[6]))
    stores.append(pltpu.make_async_copy(last, last_out, sems.at[7]))
    for store in stores[2:]:
        store.start()
    for i, (move, b) in enumerate(zip(moves, blocks)):
        move.wait()
        stores.append(pltpu.make_async_copy(b[1], b[2], sems.at[8 + i]))
        stores[-1].start()
    for store in stores:
        store.wait()


def per_device(n_lat, n_lon, n_mem, velo, temp, land, target, w_first, w_middle, w_last):
    rows, cols = temp.shape[1], temp.shape[2]
    rc, cc = rows // COARSE, cols // COARSE
    width = cc * n_lon
    plane = n_lat * (n_lon // 2)
    chunk, owners = chunking(n_lat, n_lon // 2)
    half = chunk * owners
    mine = w_first.shape[0]

    hbm = pl.BlockSpec(memory_space=pl.ANY)
    dma = pltpu.SemaphoreType.DMA
    fields = [jax.ShapeDtypeStruct(velo.shape, F32), jax.ShapeDtypeStruct(temp.shape, F32)]
    velo_next, temp_next, grads = pl.pallas_call(
        functools.partial(kernel, n_lat, n_lon, n_mem),
        out_shape=(*fields, jax.ShapeDtypeStruct((2, half, 128), F32)),
        in_specs=[hbm] * 7,
        out_specs=(hbm, hbm, hbm),
        scratch_shapes=[
            pltpu.VMEM(velo.shape, F32),
            pltpu.VMEM(temp.shape, F32),
            pltpu.VMEM(land.shape, jnp.int32),
            pltpu.VMEM(target.shape, BF16),
            pltpu.VMEM((9, 3, mine, HID), BF16),
            pltpu.VMEM(w_middle.shape, BF16),
            pltpu.VMEM(w_last.shape, BF16),
            pltpu.VMEM((LEV * rows, cc), F32),
            pltpu.VMEM((LEV * 2 * rows, cc), F32),
            pltpu.VMEM((LEV * rc * 8, cc), F32),
            pltpu.VMEM((LEV, rc, 8, cc), BF16),
            pltpu.VMEM((n_lon, rc + 2 * HALO, 8, cc), BF16),
            pltpu.VMEM((rc + 2 * HALO, 32, width), BF16),
            pltpu.VMEM((2, rc + 8, 3 * HID, width), BF16),
            pltpu.VMEM((rc + 6, 2 * HID, width), BF16),
            pltpu.VMEM((rc + 4, 32, width), BF16),
            pltpu.VMEM((2, rc + 2, 3 * HID, width), BF16),
            pltpu.VMEM((2, rc, width), F32),
            pltpu.VMEM((n_mem, n_lon, 2, rc, cc), F32),
            pltpu.VMEM((LEV * 2, rows, cols), F32),
            pltpu.VMEM((3 * LEV, rows + 16, cols), F32),
            pltpu.VMEM((2, 16, cols), F32),
            pltpu.VMEM((2, 16, cols), F32),
            pltpu.VMEM((2, rows, 128), F32),
            pltpu.VMEM((2, rows, 128), F32),
            pltpu.VMEM((96, 128), F32),
            pltpu.VMEM((72, 128), F32),
            pltpu.VMEM((2, half, 128), F32),
            pltpu.VMEM((half, 128), F32),
            pltpu.VMEM((half, 128), F32),
            pltpu.VMEM((plane, chunk, 128), F32),
            pltpu.VMEM((2, half, 128), F32),
            dma((8,)),
            dma((5,)),
            pltpu.SemaphoreType.REGULAR,
            dma((4,)),
            dma((4,)),
            dma((3, n_lon)),
            dma((3, n_lon)),
            dma((4,)),
            dma((4,)),
            dma((n_mem, n_lon)),
            dma((n_mem, n_lon)),
            dma,
            dma,
            dma,
            dma,
            dma((2,)),
        ],
        compiler_params=pltpu.CompilerParams(
            collective_id=0, has_side_effects=True, vmem_limit_bytes=56 * 1024 * 1024
        ),
        name="ocean_step",
    )(velo, temp, land, target, jnp.transpose(w_first, (1, 3, 0, 2)), w_middle, w_last)
    velo_next, temp_next, first, middle, last = pl.pallas_call(
        finish,
        out_shape=(
            *fields,
            jax.ShapeDtypeStruct((9, 3, mine, HID), F32),
            jax.ShapeDtypeStruct(w_middle.shape, F32),
            jax.ShapeDtypeStruct(w_last.shape, F32),
        ),
        in_specs=[hbm] * 3,
        out_specs=(hbm,) * 5,
        scratch_shapes=[
            pltpu.VMEM(velo.shape, F32),
            pltpu.VMEM(temp.shape, F32),
            pltpu.VMEM((2, half, 128), F32),
            pltpu.VMEM((9, 3, mine, HID), F32),
            pltpu.VMEM(w_middle.shape, F32),
            pltpu.VMEM(w_last.shape, F32),
            dma((11,)),
        ],
        name="finish",
    )(velo_next, temp_next, grads)
    return (velo_next, temp_next, jnp.transpose(first, (2, 0, 3, 1)), middle, last)


def solution(mesh):
    return jax.shard_map(
        functools.partial(per_device, mesh.shape["lat"], mesh.shape["lon"], mesh.shape["mem"]),
        mesh=mesh,
        in_specs=(
            P(None, None, "lat", "lon"),
            P(None, "lat", "lon"),
            P("lat", "lon"),
            P(None, None, "lat", "lon"),
            P("mem", None, None, None),
            P("mem", None, None, None),
            P("mem", None, None, None),
        ),
        out_specs=(
            P(None, None, "lat", "lon"),
            P(None, "lat", "lon"),
            P("mem", None, None, None),
            P("mem", None, None, None),
            P("mem", None, None, None),
        ),
        check_vma=False,
    )
```
